32 devices in a mesh: exp: 8 (over y, x, core), tp: 4 (over z).
Axes of the slice: x: 2, y: 2, z: 4, core: 2. Of those that a mesh axis runs over, the one named last changes fastest.
Arguments:
- tokens: bfloat16 [65536, 384], P(('exp', 'tp')), may hold values from -24 to 24
- cotangent: bfloat16 [65536, 384], P(('exp', 'tp')), may hold values from -1 to 1
- routes: int32 [65536, 2], P(('exp', 'tp')), may hold values from 0 to 7, all different within a row; in each aligned block of 2048 rows (0 to 2047, 2048 to 4095, ...) at most 1024 rows name the same one
- segments: int32 [64, 1024], P(('exp', 'tp')), may hold values from 0 to 7, never falling along the last dimension, each value on 1 to 256 neighbouring positions
- variates: int32 [64, 1024], P(('exp', 'tp')), may hold values from 0 to 3
- positions: int32 [64, 1024], P(('exp', 'tp')), may hold values from 0 to 1023
- step_count: int32 [1], replicated, may hold values from 1 to 20
- dense_state: float32 [4, 592896], P(None, ('exp', 'tp')), as said below
- gate_up_state: float32 [4, 8, 2, 384, 512], P(None, 'exp', None, None, 'tp'), as said below
- down_state: float32 [4, 8, 512, 384], P(None, 'exp', 'tp'), as said below
- small_state: float32 [4, 780], replicated, as said below
Outputs:
- block_out: bfloat16 [65536, 384], P(('exp', 'tp'))
- grad_in: bfloat16 [65536, 384], P(('exp', 'tp'))
- dense_new: float32 [4, 592896], P(None, ('exp', 'tp'))
- dense_copy: bfloat16 [592896], P(('exp', 'tp'))
- gate_up_new: float32 [4, 8, 2, 384, 512], P(None, 'exp', None, None, 'tp')
- gate_up_copy: bfloat16 [8, 2, 384, 512], P('exp', None, None, 'tp')
- down_new: float32 [4, 8, 512, 384], P(None, 'exp', 'tp')
- down_copy: bfloat16 [8, 512, 384], P('exp', 'tp')
- small_new: float32 [4, 780], replicated
The draws below stay inside these ranges and needn't reach their ends.
Inputs may be any that keep to these rules, and one draw needn't show every extreme that they name: `routes`: in each aligned block of 2048 rows (the tokens of one device) no expert is named by more than 1024 rows, a bound that some block reaches; the 2 ids of a row differ. `segments`: within a row the ids never fall; a segment has at most a quarter of 1024 tokens. `dense_state`: index 2 is positive. `gate_up_state`: index 2 is positive. `down_state`: index 2 is positive. `small_state`: index 2 is positive.
All inputs are finite; a program needn't handle non-finite values.
Results may differ from the reference program's by a relative error of at most 0.015.
Values may be sent and summed in bfloat16 or wider, within the bound.
No kernel may reach another device: no remote copies, remote signals or barrier semaphores. Data moves between devices by JAX's collectives and lax.ppermute only.
A program may use at most 384 MiB of HBM per device.

```python
import math
from functools import partial
import jax
import jax.numpy as jnp
import numpy as np
from jax import lax

D = 384
HEADS = 6
HD = 64
FF = 512
TOP = 2
SEQ = 1024
SEGS = 8
VARS = 4
EXPERTS = 8
TOK_DEV = 2048
SEQS = 64
TOKENS = 65536
CAP = 1024
N_EXP = 8
N_TP = 4


grad_unit = 1.2


def bounded_normal(key, shape):
    return jnp.clip(jax.random.normal(key, shape, jnp.float32), -4.0, 4.0)


def spread_draw(key, shape):
    return bounded_normal(key, shape)


def draw_tokens(key, part):
    key_list = jax.random.split(jax.random.fold_in(key, 11), 3)
    base_draw = spread_draw(key_list[0], (TOKENS, D))
    row_scale = jnp.exp(jax.random.uniform(key_list[1], (TOKENS, 1), jnp.float32, math.log(0.3), math.log(3.0)))
    col_scale = jnp.exp(jax.random.uniform(key_list[2], (1, D), jnp.float32, math.log(0.5), math.log(2.0)))
    return (base_draw * row_scale * col_scale).astype(jnp.bfloat16)


def draw_cotangent(key, part):
    cot_key = jax.random.fold_in(key, 17)
    return (grad_unit / math.sqrt(TOKENS) * spread_draw(cot_key, (TOKENS, D))).astype(jnp.bfloat16)


def optimizer_state(key, master, grad_size, weight_size):
    key_list = jax.random.split(jax.random.fold_in(key, 23), 3)
    moment_one = grad_size * spread_draw(key_list[0], master.shape)
    moment_two = grad_size * grad_size * jnp.exp(jax.random.uniform(key_list[1], master.shape, jnp.float32, 0.0, math.log(4.0)))
    average = master + 0.2 * weight_size * bounded_normal(key_list[2], master.shape)
    return jnp.stack([master, moment_one, moment_two, average])


def draw_dense_state(key, part):
    key_list = jax.random.split(jax.random.fold_in(key, 5), 4)
    in_scale = D ** (-0.5)
    out_scale = 4.0 * D ** (-0.5)
    in_master = in_scale * bounded_normal(key_list[0], (D, 3 * D))
    out_master = out_scale * bounded_normal(key_list[1], (D, D))
    router_master = in_scale * bounded_normal(key_list[2], (D, EXPERTS))
    column_grad = jnp.concatenate([jnp.full((2 * D,), 0.4 * grad_unit, jnp.float32), jnp.full((D,), 0.6 * grad_unit, jnp.float32)])
    in_grad = jnp.broadcast_to(column_grad[None, :], (D, 3 * D))
    master = jnp.concatenate([in_master.reshape(-1), out_master.reshape(-1), router_master.reshape(-1)])
    grad_size = jnp.concatenate([in_grad.reshape(-1), jnp.full((D * D,), 0.15 * grad_unit, jnp.float32), jnp.full((D * EXPERTS,), 3.0 * grad_unit * math.sqrt(2.0 / EXPERTS), jnp.float32)])
    weight_size = jnp.concatenate([jnp.full((3 * D * D,), in_scale, jnp.float32), jnp.full((D * D,), out_scale, jnp.float32), jnp.full((D * EXPERTS,), in_scale, jnp.float32)])
    return optimizer_state(key_list[3], master, grad_size, weight_size)


def draw_gate_up_state(key, part):
    key_list = jax.random.split(jax.random.fold_in(key, 7), 2)
    weight_size = D ** (-0.5)
    master = weight_size * bounded_normal(key_list[0], (EXPERTS, 2, D, FF))
    grad_size = 0.2 * grad_unit * math.sqrt(TOP / EXPERTS)
    return optimizer_state(key_list[1], master, grad_size, weight_size)


def draw_down_state(key, part):
    key_list = jax.random.split(jax.random.fold_in(key, 9), 2)
    weight_size = FF ** (-0.5)
    master = weight_size * bounded_normal(key_list[0], (EXPERTS, FF, D))
    grad_size = 0.25 * grad_unit * math.sqrt(TOP / EXPERTS)
    return optimizer_state(key_list[1], master, grad_size, weight_size)


def draw_small_state(key, part):
    key_list = jax.random.split(jax.random.fold_in(key, 13), 3)
    gains = jax.random.uniform(key_list[0], (2 * D,), jnp.float32, 0.7, 1.3)
    biases = jax.random.uniform(key_list[1], (2 * HEADS,), jnp.float32, -1.0, 1.0)
    master = jnp.concatenate([gains, biases])
    grad_size = jnp.concatenate([jnp.full((2 * D,), 0.8 * grad_unit, jnp.float32), jnp.full((2 * HEADS,), 0.5 * grad_unit, jnp.float32)])
    weight_size = jnp.concatenate([jnp.full((2 * D,), 0.2, jnp.float32), jnp.full((2 * HEADS,), 0.5, jnp.float32)])
    return optimizer_state(key_list[2], master, grad_size, weight_size)


def set_ends(drawn, stream_key, smallest, high):
    longest = drawn.shape.index(max(drawn.shape))
    spots = []
    for shift in (0, 1):
        where = [jax.random.randint(jax.random.fold_in(stream_key, axis), (), 0, length) for axis, length in enumerate(drawn.shape)]
        where[longest] = (where[longest] + shift) % drawn.shape[longest]
        spots.append(tuple(where))
    return drawn.at[spots[0]].set(smallest).at[spots[1]].set(high)


def split_up(amount, total, most, lean):
    portions = [(1 << 20) // math.isqrt(grade ** lean) + 1 for grade in range(2, amount + 1)]
    spare, holding = total - most - (amount - 1), [1] * (amount - 1)
    while spare > 0:
        movable = [i for i in range(amount - 1) if holding[i] < most]
        whole, budget = sum([portions[i] for i in movable]), spare
        for i in movable:
            extra = min(most - holding[i], max(1, budget * portions[i] // whole), spare)
            holding[i] = holding[i] + extra
            spare = spare - extra
    return np.array([most] + holding)


def ragged(key, number_of, total, reach, skew):
    if number_of == 2:
        one = jax.random.randint(key, (), max(1, total - reach), min(reach, total - 1) + 1)
        return jnp.stack([one, total - one])
    lengths = jnp.asarray(split_up(number_of, total, reach, skew), jnp.int32)
    twos = (number_of - 1) // 2
    donor, sink = lengths[1:1 + 2 * twos:2], lengths[2:2 + 2 * twos:2]
    margin = jnp.minimum(donor - 1, reach - sink)
    shifted = jax.random.randint(jax.random.fold_in(key, 1), (twos,), 0, 1 << 20) % (margin + 1)
    lengths = lengths.at[1:1 + 2 * twos:2].set(donor - shifted).at[2:2 + 2 * twos:2].set(sink + shifted)
    return lengths[jax.random.permutation(jax.random.fold_in(key, 2), number_of)]


def assign_block(key, own, number, rows, count, top, limit, lean):
    ranking = jax.random.permutation(key, count)
    crowded, common = shares(count, rows * top, limit, lean, True), shares(count, rows * top, limit, lean, False)
    places = jnp.arange(count)

    def named(sizes, offset_by):
        used = int((sizes > 0).sum())
        fixed = max(1, used // 4)
        passed = fixed + (places - fixed + offset_by * (used - fixed)) % max(1, count - fixed)
        return jnp.zeros((count,), jnp.int32).at[ranking[jnp.where(places < fixed, places, passed)]].set(jnp.asarray(sizes, jnp.int32))

    sizes = jnp.where(number % 4 == 0, named(crowded, number // 4), named(common, number - number // 4 - 1))
    mixed = jax.random.permutation(jax.random.fold_in(own, 3), count)
    source_of, receiver = mixed[0:count // 2 * 2:2], mixed[1:count // 2 * 2:2]
    margin = jnp.minimum(sizes[source_of] - 1, limit - sizes[receiver]) // 2
    margin = jnp.where((source_of == ranking[0]) | (receiver == ranking[0]) | (sizes[receiver] == 0), 0, jnp.maximum(margin, 0))
    passed = jax.random.randint(jax.random.fold_in(own, 4), (count // 2,), 0, 1 << 20) % (margin + 1)
    sizes = sizes.at[source_of].add(-passed).at[receiver].add(passed)
    labels = jnp.searchsorted(jnp.cumsum(sizes), jnp.arange(rows * top), side="right").astype(jnp.int32)
    table = labels.reshape(top, rows).T
    table = table[jax.random.permutation(jax.random.fold_in(own, 1), rows)]
    offset_by = jax.random.randint(jax.random.fold_in(own, 2), (rows, 1), 0, top)
    return jnp.take_along_axis(table, (jnp.arange(top)[None, :] + offset_by) % top, axis=1)


def shares(amount, total, most, skew, full):
    loads = [(1 << 20) // math.isqrt(standing ** skew) + 1 for standing in range(1, amount + 1)]
    largest = most if full else min(most, max(-(-total // amount), total * loads[0] // sum(loads)))
    least = 1 if total - largest >= amount - 1 else 0
    holding, spare = [largest] + [least] * (amount - 1), total - largest - least * (amount - 1)
    while spare > 0:
        candidates = [i for i in range(1, amount) if holding[i] < largest] or [i for i in range(1, amount) if holding[i] < most]
        pool, left = sum([loads[i] for i in candidates]), spare
        for i in candidates:
            more = min(most - holding[i], max(1, left * loads[i] // pool), spare)
            holding[i] = holding[i] + more
            spare = spare - more
    return np.array(holding)


def setup_inputs(seed: int = 0) -> dict:
    seeds = jax.random.split(jax.random.key(seed), 12)
    tokens = draw_tokens(jax.random.fold_in(seeds[11], 71), 0)
    cotangent = draw_cotangent(jax.random.fold_in(seeds[11], 71), 0)
    routes_keys = jax.random.split(jax.random.fold_in(seeds[2], 1), TOKENS // TOK_DEV)
    routes_turns = jax.random.permutation(jax.random.fold_in(seeds[2], 3), TOKENS // TOK_DEV)
    routes = jax.vmap(lambda own, number: assign_block(jax.random.fold_in(seeds[2], 2), own, number, TOK_DEV, EXPERTS, TOP, CAP, 2))(routes_keys, routes_turns).reshape((TOKENS, TOP))
    segments = jax.vmap(lambda own: jnp.searchsorted(jnp.cumsum(ragged(own, SEGS, SEQ, SEQ // 4, 1)), jnp.arange(SEQ), side="right"))(jax.random.split(seeds[3], SEQS)).reshape((SEQS, SEQ)).astype(jnp.int32)
    variates = set_ends(jax.random.randint(seeds[4], (SEQS, SEQ), 0, VARS), jax.random.fold_in(seeds[4], 1), 0, VARS - 1).astype(jnp.int32)
    positions = set_ends(jax.random.randint(seeds[5], (SEQS, SEQ), 0, SEQ), jax.random.fold_in(seeds[5], 1), 0, SEQ - 1).astype(jnp.int32)
    step_count = jax.random.randint(seeds[6], (1,), 1, 21).astype(jnp.int32)
    dense_state = draw_dense_state(jax.random.fold_in(seeds[11], 71), 0)
    gate_up_state = draw_gate_up_state(jax.random.fold_in(seeds[11], 71), 0)
    down_state = draw_down_state(jax.random.fold_in(seeds[11], 71), 0)
    small_state = draw_small_state(jax.random.fold_in(seeds[11], 71), 0)
    return dict(tokens=tokens, cotangent=cotangent, routes=routes, segments=segments, variates=variates, positions=positions, step_count=step_count, dense_state=dense_state, gate_up_state=gate_up_state, down_state=down_state, small_state=small_state)


@jax.custom_vjp
def low(v):
    return lax.optimization_barrier(v.astype(jnp.bfloat16)).astype(jnp.float32)

@jax.custom_vjp
def low_back(v):
    return v

def low_keep(v):
    return (low(v), None)

def low_pass(kept, grad):
    return (grad,)

def back_keep(v):
    return (v, None)

def back_low(kept, grad):
    return (low(grad),)
low.defvjp(low_keep, low_pass)
low_back.defvjp(back_keep, back_low)
norm_epsilon = 1e-06
masked_score = -1e+30
moment_rate = 0.5
average_rate = 0.9
adam_epsilon = 1e-08
weight_decay = 0.1
rate_dense = 0.05
rate_expert = 0.04
rate_small = 0.2

def product(left, right):
    return jnp.dot(left, right, precision=lax.Precision.HIGHEST, preferred_element_type=jnp.float32)

def normalize(values, gain):
    return values * lax.rsqrt(lax.optimization_barrier(jnp.mean(values * values, axis=-1, keepdims=True)) + norm_epsilon) * gain

def rotation(position_row):
    frequency = jnp.exp(jnp.arange(HD // 2, dtype=jnp.float32) * (-2.0 * math.log(10000.0) / HD))
    angles = position_row.astype(jnp.float32)[:, None] * frequency[None, :]
    return (jnp.cos(angles)[:, None, :], jnp.sin(angles)[:, None, :])

def rotate(values, cosine, sine_part):
    half_dim = HD // 2
    front_half = values[..., :half_dim]
    back_half = values[..., half_dim:]
    return jnp.concatenate([front_half * cosine - back_half * sine_part, front_half * sine_part + back_half * cosine], axis=-1)

def attend(score_bias, packed):
    qkv_rows, segment_row, variate_row, position_row = packed
    cosine, sine_part = rotation(position_row)
    queries = low(rotate(qkv_rows[:, :D].reshape(SEQ, HEADS, HD), cosine, sine_part))
    key_rows = low(rotate(qkv_rows[:, D:2 * D].reshape(SEQ, HEADS, HD), cosine, sine_part))
    values = low(qkv_rows[:, 2 * D:].reshape(SEQ, HEADS, HD))
    scores = jnp.einsum('qhd,khd->hqk', queries, key_rows, precision=lax.Precision.HIGHEST) * HD ** (-0.5)
    same_var = (variate_row[:, None] == variate_row[None, :])[None]
    scores = low_back(scores + jnp.where(same_var, score_bias[0][:, None, None], score_bias[1][:, None, None]))
    allowed = (segment_row[:, None] == segment_row[None, :])[None]
    probs_full = jax.nn.softmax(jnp.where(allowed, scores, masked_score), axis=-1)
    mixed_out = jnp.einsum('hqk,khd->qhd', low(probs_full), values, precision=lax.Precision.HIGHEST)
    return low(low_back(mixed_out.reshape(SEQ, D)))

def expert(packed):
    in_rows, gate_up_weight, down_weight = packed
    gate_pre = low_back(product(in_rows, low(gate_up_weight[0])))
    up_pre = low_back(product(in_rows, low(gate_up_weight[1])))
    hidden = low(jax.nn.silu(gate_pre) * up_pre)
    return low(low_back(product(hidden, low(down_weight))))

def tables(routes):
    device_count = N_EXP * N_TP
    pair_routes = routes.reshape(device_count, TOK_DEV * TOP)
    matches = (pair_routes[:, :, None] == jnp.arange(EXPERTS, dtype=jnp.int32)[None, None, :]).astype(jnp.int32)
    slot_rank = lax.optimization_barrier(jnp.sum((jnp.cumsum(matches, axis=1) - matches) * matches, axis=-1))
    owner_index = jnp.arange(device_count, dtype=jnp.int32)[:, None]
    slot_index = ((pair_routes * device_count + owner_index) * CAP + slot_rank).reshape(-1).astype(jnp.int32)
    slot_total = EXPERTS * device_count * CAP
    source = jnp.zeros((slot_total,), jnp.int32).at[slot_index].set(jnp.arange(TOKENS * TOP, dtype=jnp.int32))
    filled = jnp.zeros((slot_total,), jnp.float32).at[slot_index].set(1.0)
    return (source, filled, slot_index)

def forward(inputs, dense, gate_up, down, small_params, routes, segments, variates, positions, source, filled, slot_index):
    in_proj = low(dense[:3 * D * D].reshape(D, 3 * D))
    out_proj = low(dense[3 * D * D:4 * D * D].reshape(D, D))
    router_weight = low(dense[4 * D * D:].reshape(D, EXPERTS))
    gain_one = small_params[:D]
    gain_two = small_params[D:2 * D]
    score_bias = small_params[2 * D:].reshape(2, HEADS)
    normed_one = low(normalize(inputs, gain_one))
    projected = low_back(product(normed_one, in_proj))
    mixed_out = lax.map(jax.checkpoint(partial(attend, score_bias)), (projected.reshape(SEQS, SEQ, 3 * D), segments, variates, positions))
    middle = inputs + low_back(product(mixed_out.reshape(TOKENS, D), out_proj))
    normed_two = low(normalize(middle, gain_two))
    logits = low_back(product(normed_two, router_weight))
    select = routes[:, :, None] == jnp.arange(EXPERTS, dtype=jnp.int32)[None, None, :]
    chosen = lax.optimization_barrier(jnp.sum(jnp.where(select, logits[:, None, :], 0.0), axis=-1))
    gate_probs = jax.nn.softmax(chosen, axis=-1)
    in_rows = low_back(normed_two[source // TOP]) * filled[:, None]
    outputs = lax.map(jax.checkpoint(expert), (in_rows.reshape(EXPERTS, -1, D), gate_up, down))
    paired = outputs.reshape(-1, D)[slot_index].reshape(TOKENS, TOP, D)
    return middle + lax.optimization_barrier(jnp.sum(gate_probs[:, :, None] * paired, axis=1))

def adamw_update(old_state, grad_value, rate, decay, step_value):
    moment_one = moment_rate * old_state[1] + (1.0 - moment_rate) * grad_value
    moment_two = moment_rate * old_state[2] + (1.0 - moment_rate) * grad_value * grad_value
    correction = 1.0 - jnp.power(moment_rate, step_value)
    master = old_state[0] - rate * (moment_one / correction / (jnp.sqrt(moment_two / correction) + adam_epsilon) + decay * old_state[0])
    average = average_rate * old_state[3] + (1.0 - average_rate) * master
    return jnp.stack([master, moment_one, moment_two, average])

def reference(tokens, cotangent, routes, segments, variates, positions, step_count, dense_state, gate_up_state, down_state, small_state):
    source, filled, slot_index = tables(routes)

    def closed(inputs, dense, gate_up, down, small_params):
        return forward(inputs, dense, gate_up, down, small_params, routes, segments, variates, positions, source, filled, slot_index)
    primal, pullback = jax.vjp(closed, tokens.astype(jnp.float32), dense_state[0], gate_up_state[0], down_state[0], small_state[0])
    grad_inputs, grad_dense, grad_gate_up, grad_down, grad_small = pullback(cotangent.astype(jnp.float32))
    step_value = step_count[0].astype(jnp.float32)
    dense_new = adamw_update(dense_state, grad_dense, rate_dense, weight_decay, step_value)
    gate_up_new = adamw_update(gate_up_state, grad_gate_up, rate_expert, weight_decay, step_value)
    down_new = adamw_update(down_state, grad_down, rate_expert, weight_decay, step_value)
    small_new = adamw_update(small_state, grad_small, rate_small, 0.0, step_value)
    return (primal.astype(jnp.bfloat16), grad_inputs.astype(jnp.bfloat16), dense_new, dense_new[0].astype(jnp.bfloat16), gate_up_new, gate_up_new[0].astype(jnp.bfloat16), down_new, down_new[0].astype(jnp.bfloat16), small_new)
```

```python
from functools import partial
import math

import jax
import jax.numpy as jnp
from jax import lax
from jax.experimental import pallas as pl
from jax.experimental.pallas import tpu as pltpu
from jax.sharding import PartitionSpec as P

D = 384
HEADS = 6
HD = 64
PAIRS = HEADS // 2
TOP = 2
SEQ = 1024
LANES = 128
QB = 128
CH = 256
NBLK = SEQ // QB
WIN = 128
SLOT = 256
XW = 2 * D + LANES
SEG_IDS = 8
VAR_IDS = 4
LSE_LANE = SEG_IDS + 6 * VAR_IDS
FAR = 2.0**100
VMEM_BYTES = 60 * 1024 * 1024

norm_epsilon = 1e-06
moment_rate = 0.5
average_rate = 0.9
adam_epsilon = 1e-08
weight_decay = 0.1
rate_dense = 0.05
rate_expert = 0.04
rate_small = 0.2

bf16 = jnp.bfloat16
f32 = jnp.float32


def mm(left, right):
    return lax.dot_general(left, right, (((1,), (0,)), ((), ())), preferred_element_type=f32)


def mm_nt(left, right):
    return lax.dot_general(left, right, (((1,), (1,)), ((), ())), preferred_element_type=f32)


def mm_tn(left, right):
    return lax.dot_general(left, right, (((0,), (0,)), ((), ())), preferred_element_type=f32)


def lane_ids(shape):
    return lax.broadcasted_iota(jnp.int32, shape, len(shape) - 1)


def row_ids(shape):
    return lax.broadcasted_iota(jnp.int32, shape, 0)


def three_pieces(value):
    high = value.astype(bf16)
    rest = value - high.astype(f32)
    middle = rest.astype(bf16)
    low = (rest - middle.astype(f32)).astype(bf16)
    return high.astype(f32), middle.astype(f32), low.astype(f32)


def swap_halves(values):
    lane = lane_ids(values.shape)
    return jnp.where(
        lane % HD < HD // 2,
        pltpu.roll(values, LANES - HD // 2, 1),
        pltpu.roll(values, HD // 2, 1),
    )


def call(kernel, **kwargs):
    return pl.pallas_call(
        kernel,
        compiler_params=pltpu.CompilerParams(
            vmem_limit_bytes=VMEM_BYTES, dimension_semantics=("arbitrary",)
        ),
        **kwargs,
    )


def whole(shape):
    return pl.BlockSpec(shape, lambda *_: (0,) * len(shape))


def cost(flops, moved):
    return pl.CostEstimate(flops=int(flops), transcendentals=0, bytes_accessed=int(moved))


def unpack_kernel(place, shards, in_out, out_out, router_out, flat, spread, *, shard, experts, n_tp):
    rows = shards.shape[1]
    n_dev = shards.shape[0]
    flat[...] = jnp.zeros(flat.shape, f32)
    lane = lane_ids((rows, LANES))
    for s in range(n_dev):
        rel = (lax.bitwise_xor(s // n_tp, place[0])) * n_tp + lax.bitwise_xor(s % n_tp, place[1])
        start, off = divmod(shard * s, LANES)
        piece = shards[rel].astype(f32)
        if off:
            piece = pltpu.roll(piece, off, 1)
            flat[start : start + rows] += jnp.where(lane >= off, piece, 0.0)
            flat[start + 1 : start + 1 + rows] += jnp.where(lane < off, piece, 0.0)
        else:
            flat[start : start + rows] += piece
    for j in range(9):
        in_out[:, j * LANES : (j + 1) * LANES] = flat[pl.ds(j, D, stride=9), :].astype(bf16)
    for j in range(3):
        out_out[:, j * LANES : (j + 1) * LANES] = flat[pl.ds(9 * D + j, D, stride=3), :].astype(bf16)
    share = LANES // experts
    count = D // share
    for i in range(share):
        spread[pl.ds(i, count, stride=share), :] = flat[12 * D : 12 * D + count, :]
    lanes = lane_ids((D, LANES))
    kept = jnp.where(lanes // experts == row_ids((D, LANES)) % share, spread[...], 0.0).astype(bf16)
    fold_lane = lane_ids((LANES, LANES))
    fold = (row_ids((LANES, LANES)) % experts == lax.bitwise_xor(fold_lane, place[0])) & (
        fold_lane < experts
    )
    router_out[...] = mm(kept, jnp.where(fold, 1.0, 0.0).astype(bf16)).astype(bf16)


def unpack_dense(place, shards, shard, experts, n_tp):
    total = shard * shards.shape[0] // LANES
    flat_rows = total + shards.shape[1] + 8
    return call(
        partial(unpack_kernel, shard=shard, experts=experts, n_tp=n_tp),
        grid_spec=pltpu.PrefetchScalarGridSpec(
            num_scalar_prefetch=1,
            grid=(1,),
            in_specs=[whole(shards.shape)],
            out_specs=[whole((D, 3 * D)), whole((D, D)), whole((D, LANES))],
            scratch_shapes=[pltpu.VMEM((flat_rows, LANES), f32), pltpu.VMEM((D, LANES), f32)],
        ),
        out_shape=[
            jax.ShapeDtypeStruct((D, 3 * D), bf16),
            jax.ShapeDtypeStruct((D, D), bf16),
            jax.ShapeDtypeStruct((D, LANES), bf16),
        ],
        cost_estimate=cost(1e8, 4e6),
        name="unpack_dense",
    )(place, shards)


def key_features(marks):
    lane = lane_ids(marks.shape)
    flip = (lane < SEG_IDS) | ((lane >= SEG_IDS + 3 * VAR_IDS) & (lane < LSE_LANE))
    return jnp.where(flip, 1.0 - marks, marks)


def window(win, row, block):
    at = (row * NBLK + block) * 2
    return win[at], win[at + 1]


def in_windows(start, count, step):
    @pl.when(count <= 3)
    def _():
        step(pl.multiple_of(jnp.minimum(start, NBLK - 3) * QB, QB), 3 * QB)

    @pl.when((count > 3) & (count <= 5))
    def _():
        step(pl.multiple_of(jnp.minimum(start, NBLK - 5) * QB, QB), 5 * QB)

    @pl.when(count > 5)
    def _():
        step(0, SEQ)


def forward_kernel(
    win, tokens, cot, cos_ref, sin_ref, marks_ref, routes_ref, gain_one, gain_two, biases,
    in_proj, out_proj, router,
    q_out, k_out, v_out, feat_out, mixed_out, middle_out, rows_out, probs_out,
    keys_aug, values_aug, *, experts,
):
    row = pl.program_id(0)
    for p in range(PAIRS):
        values_aug[p, :, LANES:] = jnp.ones((SEQ, LANES), bf16)

    def project(c, carry):
        at = pl.ds(pl.multiple_of(c * CH, CH), CH)
        x = tokens[at, :].astype(f32)
        factor = lax.rsqrt(jnp.mean(x * x, axis=-1, keepdims=True) + norm_epsilon)
        normed = (x * factor * gain_one[...]).astype(bf16)
        projected = mm(normed, in_proj[...])
        cosine, sine = cos_ref[at, :], sin_ref[at, :]
        features = key_features(marks_ref[at, :].astype(f32)).astype(bf16)
        for j in range(2 * PAIRS):
            part = projected[:, j * LANES : (j + 1) * LANES]
            turned = part * cosine + swap_halves(part) * sine
            if j < PAIRS:
                q_out[at, j * LANES : (j + 1) * LANES] = (
                    turned.astype(bf16) * jnp.asarray(HD**-0.5, bf16)
                )
            else:
                p = j - PAIRS
                turned = turned.astype(bf16)
                k_out[at, p * LANES : (p + 1) * LANES] = turned
                keys_aug[p, at, :LANES] = turned
                keys_aug[p, at, LANES:] = features
        for p in range(PAIRS):
            part = projected[:, 2 * D + p * LANES : 2 * D + (p + 1) * LANES].astype(bf16)
            v_out[at, p * LANES : (p + 1) * LANES] = part
            values_aug[p, at, :LANES] = part
        return carry

    lax.fori_loop(0, SEQ // CH, project, 0)

    lane = lane_ids((QB, LANES))
    first = jnp.where(lane_ids((1, LANES)) < HD, 1.0, 0.0).astype(bf16)
    second = jnp.where(lane_ids((1, LANES)) >= HD, 1.0, 0.0).astype(bf16)

    def attend(block, carry):
        at = pl.ds(pl.multiple_of(block * QB, QB), QB)
        start, count = window(win, row, block)
        marks = marks_ref[at, :].astype(f32)

        def step(key_start, keys):
            key_at = pl.ds(key_start, keys)
            for p in range(PAIRS):
                queries = q_out[at, p * LANES : (p + 1) * LANES]
                feat = [marks * biases[2 * p + i : 2 * p + i + 1, :] for i in range(2)]
                stacked = jnp.concatenate(
                    [
                        jnp.concatenate([queries * first, feat[0].astype(bf16)], axis=1),
                        jnp.concatenate([queries * second, feat[1].astype(bf16)], axis=1),
                    ],
                    axis=0,
                )
                scores = mm_nt(stacked, keys_aug[p, key_at, :])
                top = jnp.max(scores, axis=1, keepdims=True)
                weights = jnp.exp(scores - top).astype(bf16)
                sums = mm(weights, values_aug[p, key_at, :])
                total = sums[:, LANES:]
                mixed = sums[:, :LANES] / total
                mixed_out[at, p * LANES : (p + 1) * LANES] = jnp.where(
                    lane < HD, mixed[:QB], mixed[QB:]
                ).astype(bf16)
                summary = -(top + jnp.log(total))
                high, middle, low = three_pieces(summary)
                for i in range(2):
                    part = slice(i * QB, (i + 1) * QB)
                    feat_out[2 * p + i, at, :] = jnp.where(
                        lane == LSE_LANE,
                        high[part],
                        jnp.where(
                            lane == LSE_LANE + 1,
                            middle[part],
                            jnp.where(lane == LSE_LANE + 2, low[part], feat[i]),
                        ),
                    ).astype(bf16)

        in_windows(start, count, step)
        return carry

    lax.fori_loop(0, NBLK, attend, 0)

    def finish(c, carry):
        at = pl.ds(pl.multiple_of(c * CH, CH), CH)
        middle = tokens[at, :].astype(f32) + mm(mixed_out[at, :], out_proj[...])
        middle_out[at, :] = middle
        factor = lax.rsqrt(jnp.mean(middle * middle, axis=-1, keepdims=True) + norm_epsilon)
        normed = (middle * factor * gain_two[...]).astype(bf16)
        rows_out[at, :D] = normed
        rows_out[at, D : 2 * D] = cot[at, :]
        logits = mm(normed, router[...])
        lanes = lane_ids((CH, LANES))
        named = (lanes == routes_ref[at, 0:1]) | (lanes == routes_ref[at, 1:2])
        top = jnp.max(jnp.where(named, logits, -3.0e38), axis=1, keepdims=True)
        weights = jnp.where(named, jnp.exp(jnp.where(named, logits - top, 0.0)), 0.0)
        probs = weights / jnp.sum(weights, axis=1, keepdims=True)
        probs_out[at, :] = probs
        high, mid, low = three_pieces(probs)
        rows_out[at, 2 * D :] = (
            high + pltpu.roll(mid, experts, 1) + pltpu.roll(low, 2 * experts, 1)
        ).astype(bf16)
        return carry

    lax.fori_loop(0, SEQ // CH, finish, 0)


def forward(win, tokens, cot, cosine, sine, marks, routes, gain_one, gain_two, biases, weights, experts):
    tok = tokens.shape[0]
    seqs = tok // SEQ

    def rows(width):
        return pl.BlockSpec((SEQ, width), lambda i, *_: (i, 0))

    in_proj, out_proj, router = weights
    return call(
        partial(forward_kernel, experts=experts),
        grid_spec=pltpu.PrefetchScalarGridSpec(
            num_scalar_prefetch=1,
            grid=(seqs,),
            in_specs=[
                rows(D), rows(D), rows(LANES), rows(LANES), rows(LANES), rows(TOP),
                whole((1, D)), whole((1, D)), whole((8, LANES)),
                whole((D, 3 * D)), whole((D, D)), whole((D, LANES)),
            ],
            out_specs=[
                rows(D), rows(D), rows(D),
                pl.BlockSpec((HEADS, SEQ, LANES), lambda i, *_: (0, i, 0)),
                rows(D), rows(D), rows(XW), rows(LANES),
            ],
            scratch_shapes=[
                pltpu.VMEM((PAIRS, SEQ, 2 * LANES), bf16),
                pltpu.VMEM((PAIRS, SEQ, 2 * LANES), bf16),
            ],
        ),
        out_shape=[
            jax.ShapeDtypeStruct((tok, D), bf16),
            jax.ShapeDtypeStruct((tok, D), bf16),
            jax.ShapeDtypeStruct((tok, D), bf16),
            jax.ShapeDtypeStruct((HEADS, tok, LANES), bf16),
            jax.ShapeDtypeStruct((tok, D), bf16),
            jax.ShapeDtypeStruct((tok, D), f32),
            jax.ShapeDtypeStruct((tok, XW), bf16),
            jax.ShapeDtypeStruct((tok, LANES), f32),
        ],
        cost_estimate=cost(2e10, 2e7),
        name="attention_forward",
    )(win, tokens, cot, cosine, sine, marks, routes, gain_one, gain_two, biases, *weights)


def experts_kernel(table, *refs, group, experts, blocks):
    weights = refs[: len(group)]
    rows, place_lanes, place_rows = refs[len(group) : len(group) + 3]
    part_out = refs[len(group) + 3]
    grads = refs[len(group) + 4 : 2 * len(group) + 4]
    slots, grad_in, grad_down, total = refs[2 * len(group) + 4 :]
    ff = grad_down.shape[0]

    def first_slot(block, r):
        return pl.multiple_of(table[block * experts + r], 16)

    def windows(block):
        return table[blocks * experts + block]

    tail = blocks - 1
    for g in range(len(group)):
        slots[g, 0:16, :] = jnp.zeros((16, XW), bf16)

    def gather(block, carry):
        at = pl.ds(pl.multiple_of(block * CH, CH), CH)
        source = rows[at, :]

        def picked(w):
            slot = row_ids((WIN, CH)).astype(f32) + (w * WIN).astype(f32)
            return mm(
                jnp.concatenate(
                    [
                        jnp.where(place_lanes[r : r + 1, at] == slot, 1.0, 0.0).astype(bf16)
                        for r in group
                    ],
                    axis=0,
                ),
                source,
            ).astype(bf16)

        moved = picked(jnp.int32(0))
        for g, r in enumerate(group):
            start = first_slot(block, r)
            slots[g, pl.ds(start, 16), :] += moved[g * WIN : g * WIN + 16]
            slots[g, pl.ds(start + 16, WIN - 16), :] = moved[g * WIN + 16 : (g + 1) * WIN]

        def more(w, inner):
            moved = picked(w)
            for g, r in enumerate(group):
                slots[g, pl.ds(first_slot(block, r) + w * WIN, WIN), :] = moved[
                    g * WIN : (g + 1) * WIN
                ]
            return inner

        return lax.fori_loop(1, windows(block), more, carry)

    lax.fori_loop(0, blocks, gather, 0)

    for g, r in enumerate(group):
        end = first_slot(tail, r) + windows(tail) * WIN
        slots[g, pl.ds(end, SLOT), :] = jnp.zeros((SLOT, XW), bf16)
        gate_w = jnp.concatenate([weights[g][z, :D, :] for z in range(ff // LANES)], axis=1)
        up_w = jnp.concatenate([weights[g][z, D : 2 * D, :] for z in range(ff // LANES)], axis=1)
        down_w = jnp.concatenate(
            [
                jnp.concatenate(
                    [weights[g][z, (6 + j) * LANES : (7 + j) * LANES, :] for j in range(3)], axis=1
                )
                for z in range(ff // LANES)
            ],
            axis=0,
        )
        grad_in[...] = jnp.zeros(grad_in.shape, f32)
        grad_down[...] = jnp.zeros(grad_down.shape, f32)

        def step(i, carry, g=g, r=r, gate_w=gate_w, up_w=up_w, down_w=down_w):
            at = pl.ds(pl.multiple_of(i * SLOT, SLOT), SLOT)
            x = slots[g, at, :D]
            cot = slots[g, at, D : 2 * D].astype(f32)
            parts = slots[g, at, 2 * D :].astype(f32)
            prob = (
                parts[:, r : r + 1]
                + parts[:, experts + r : experts + r + 1]
                + parts[:, 2 * experts + r : 2 * experts + r + 1]
            )
            gate_pre = mm(x, gate_w)
            up_pre = mm(x, up_w)
            sigmoid = 1.0 / (1.0 + jnp.exp(-gate_pre))
            silu = gate_pre * sigmoid
            hidden = (silu * up_pre).astype(bf16)
            result = mm(hidden, down_w).astype(bf16).astype(f32)
            grad_result = (prob * cot).astype(bf16)
            grad_hidden = mm_nt(grad_result, down_w)
            grad_gate = (
                grad_hidden * up_pre * sigmoid * (1.0 + gate_pre * (1.0 - sigmoid))
            ).astype(bf16)
            grad_up = (grad_hidden * silu).astype(bf16)
            grad_rows = mm_nt(grad_gate, gate_w) + mm_nt(grad_up, up_w)
            grad_in[:, :ff] += mm_tn(x, grad_gate)
            grad_in[:, ff:] += mm_tn(x, grad_up)
            grad_down[...] += mm_tn(hidden, grad_result)
            score = jnp.sum(cot * result, axis=1, keepdims=True)
            high, mid, _ = three_pieces(jnp.broadcast_to(score, (SLOT, LANES)))
            lane = lane_ids((SLOT, LANES))
            slots[g, at, :D] = (prob * result).astype(bf16)
            slots[g, at, D : 2 * D] = grad_rows.astype(bf16)
            slots[g, at, 2 * D :] = jnp.where(
                lane == r, high, jnp.where(lane == experts + r, mid, 0.0)
            ).astype(bf16)
            return carry

        lax.fori_loop(0, table[blocks * experts + blocks + r], step, 0)
        for z in range(ff // LANES):
            cols = slice(z * LANES, (z + 1) * LANES)
            grads[g][z, :D, :] = grad_in[:, cols].astype(bf16)
            grads[g][z, D : 2 * D, :] = grad_in[:, ff + z * LANES : ff + (z + 1) * LANES].astype(bf16)
            for j in range(3):
                grads[g][z, (6 + j) * LANES : (7 + j) * LANES, :] = grad_down[
                    cols, j * LANES : (j + 1) * LANES
                ].astype(bf16)

    def scatter(block, carry):
        at = pl.ds(pl.multiple_of(block * CH, CH), CH)
        places = place_rows[at, :]

        def sent(w):
            slot = lane_ids((CH, WIN)).astype(f32) + (w * WIN).astype(f32)
            pick = jnp.concatenate(
                [jnp.where(places[:, r : r + 1] == slot, 1.0, 0.0).astype(bf16) for r in group],
                axis=1,
            )
            source = jnp.concatenate(
                [slots[g, pl.ds(first_slot(block, r) + w * WIN, WIN), :] for g, r in enumerate(group)],
                axis=0,
            )
            return mm(pick, source)

        total[...] = sent(jnp.int32(0))

        def more(w, inner):
            total[...] += sent(w)
            return inner

        lax.fori_loop(1, windows(block), more, 0)
        part_out[at, :] = total[...].astype(bf16)
        return carry

    lax.fori_loop(0, blocks, scatter, 0)


def run_experts(table, weights, rows, place_lanes, place_rows, group, experts, cap):
    tok = rows.shape[0]
    ff = weights[0].shape[0] * LANES
    blocks = tok // CH
    shape = weights[0].shape
    out = call(
        partial(experts_kernel, group=group, experts=experts, blocks=blocks),
        grid_spec=pltpu.PrefetchScalarGridSpec(
            num_scalar_prefetch=1,
            grid=(1,),
            in_specs=[whole(shape)] * len(group)
            + [whole((tok, XW)), whole(place_lanes.shape), whole((tok, LANES))],
            out_specs=[whole((tok, XW))] + [whole(shape)] * len(group),
            scratch_shapes=[
                pltpu.VMEM((len(group), cap + 4 * WIN + SLOT, XW), bf16),
                pltpu.VMEM((D, 2 * ff), f32),
                pltpu.VMEM((ff, D), f32),
                pltpu.VMEM((CH, XW), f32),
            ],
        ),
        out_shape=[jax.ShapeDtypeStruct((tok, XW), bf16)]
        + [jax.ShapeDtypeStruct(shape, bf16)] * len(group),
        cost_estimate=cost(4e9 * len(group), 3e6 * len(group) + 8e6),
        name="experts",
    )(table, *weights, rows, place_lanes, place_rows)
    return out[0], out[1:]


def backward_kernel(
    win, place, *refs, experts, n_tp, parts, shard,
):
    part_refs = refs[:parts]
    (
        tokens, rows_ref, probs_ref, middle_ref, mixed_ref, q_ref, k_ref, v_ref, feat_ref, marks_ref,
        cos_ref, sin_ref, gain_one, gain_two, in_proj, out_proj, router,
        block_out, grad_in_out, dense_out, gain_out, bias_out,
        grad_middle, grad_mixed, keys_aug, values_aug, grad_q, grad_k, grad_v,
        grad_in_proj, grad_out_proj, grad_router, flat,
    ) = refs[parts:]
    row = pl.program_id(0)

    @pl.when(row == 0)
    def _():
        grad_in_proj[...] = jnp.zeros(grad_in_proj.shape, f32)
        grad_out_proj[...] = jnp.zeros(grad_out_proj.shape, f32)
        grad_router[...] = jnp.zeros(grad_router.shape, f32)
        gain_out[...] = jnp.zeros(gain_out.shape, f32)
        bias_out[...] = jnp.zeros(bias_out.shape, f32)

    fold_row, fold_lane = row_ids((LANES, LANES)), lane_ids((LANES, LANES))
    tile = jnp.where(
        (lax.bitwise_xor(fold_row, place[0]) == fold_lane % experts) & (fold_row < experts), 1.0, 0.0
    ).astype(bf16)

    def head(c, carry):
        at = pl.ds(pl.multiple_of(c * CH, CH), CH)
        back = part_refs[0][at, :].astype(f32)
        for ref in part_refs[1:]:
            back = back + ref[at, :].astype(f32)
        middle = middle_ref[at, :]
        block_out[at, :] = (middle + back[:, :D]).astype(bf16)
        scores = back[:, 2 * D :]
        scores = scores + pltpu.roll(scores, LANES - experts, 1)
        probs = probs_ref[at, :]
        inner = jnp.sum(probs * scores, axis=1, keepdims=True)
        grad_logits = (probs * (scores - inner)).astype(bf16)
        grad_normed = mm_nt(grad_logits, router[...]) + back[:, D : 2 * D]
        grad_router[...] += mm_tn(rows_ref[at, :D], mm(grad_logits, tile).astype(bf16))
        factor = lax.rsqrt(jnp.mean(middle * middle, axis=-1, keepdims=True) + norm_epsilon)
        weighted = grad_normed * gain_two[...]
        gain_out[1:2, :] += jnp.sum(grad_normed * middle * factor, axis=0, keepdims=True)
        cot = rows_ref[at, D : 2 * D].astype(f32)
        grad = (
            cot
            + factor * weighted
            - middle
            * (factor * factor * factor)
            * jnp.mean(weighted * middle, axis=-1, keepdims=True)
        )
        grad_middle[at, :] = grad
        branch = grad.astype(bf16)
        grad_out_proj[...] += mm_tn(mixed_ref[at, :], branch)
        grad_mixed[at, :] = mm_nt(branch, out_proj[...]).astype(bf16)
        features = key_features(marks_ref[at, :].astype(f32)).astype(bf16)
        for p in range(PAIRS):
            cols = slice(p * LANES, (p + 1) * LANES)
            keys_aug[p, at, :LANES] = k_ref[at, cols]
            keys_aug[p, at, LANES:] = features
            values_aug[p, at, :LANES] = v_ref[at, cols]
            values_aug[p, at, LANES:] = features
        return carry

    lax.fori_loop(0, SEQ // CH, head, 0)
    grad_k[...] = jnp.zeros(grad_k.shape, f32)
    grad_v[...] = jnp.zeros(grad_v.shape, f32)

    lane = lane_ids((QB, LANES))
    first = jnp.where(lane_ids((1, LANES)) < HD, 1.0, 0.0).astype(bf16)
    second = jnp.where(lane_ids((1, LANES)) >= HD, 1.0, 0.0).astype(bf16)

    def attend(block, carry):
        at = pl.ds(pl.multiple_of(block * QB, QB), QB)
        start, count = window(win, row, block)
        marks = marks_ref[at, :].astype(f32)

        def step(key_start, keys):
            key_at = pl.ds(key_start, keys)
            for p in range(PAIRS):
                cols = slice(p * LANES, (p + 1) * LANES)
                queries = q_ref[at, cols]
                out_grad = grad_mixed[at, cols]
                product = out_grad.astype(f32) * mixed_ref[at, cols].astype(f32)
                q_rows, g_rows = [], []
                for i, mask in enumerate((first, second)):
                    inside = (lane < HD) if i == 0 else (lane >= HD)
                    inner = -jnp.sum(jnp.where(inside, product, 0.0), axis=1, keepdims=True)
                    high, middle, low = three_pieces(jnp.broadcast_to(inner, (QB, LANES)))
                    extra = jnp.where(
                        lane == LSE_LANE,
                        high,
                        jnp.where(
                            lane == LSE_LANE + 1,
                            middle,
                            jnp.where(lane == LSE_LANE + 2, low, 0.0),
                        ),
                    ).astype(bf16)
                    q_rows.append(
                        jnp.concatenate([queries * mask, feat_ref[2 * p + i, at, :]], axis=1)
                    )
                    g_rows.append(jnp.concatenate([out_grad * mask, extra], axis=1))
                stacked = jnp.concatenate(q_rows, axis=0)
                grads = jnp.concatenate(g_rows, axis=0)
                keys_here = keys_aug[p, key_at, :]
                probs = jnp.exp(mm_nt(keys_here, stacked))
                shifted = mm_nt(values_aug[p, key_at, :], grads)
                grad_scores = (probs * shifted).astype(bf16)
                grad_v[key_at, cols] += mm(probs.astype(bf16), grads[:, :LANES])
                grad_k[key_at, cols] += mm(grad_scores, stacked[:, :LANES])
                back = mm_tn(grad_scores, keys_here)
                grad_q[at, cols] = (
                    jnp.where(lane < HD, back[:QB, :LANES], back[QB:, :LANES]) * HD**-0.5
                )
                for i in range(2):
                    bias_out[2 * p + i : 2 * p + i + 1, :] += jnp.sum(
                        marks * back[i * QB : (i + 1) * QB, LANES:], axis=0, keepdims=True
                    )

        in_windows(start, count, step)
        return carry

    lax.fori_loop(0, NBLK, attend, 0)

    def tail(c, carry):
        at = pl.ds(pl.multiple_of(c * CH, CH), CH)
        cosine, sine = cos_ref[at, :], sin_ref[at, :]
        pieces = []
        for ref in (grad_q, grad_k):
            for p in range(PAIRS):
                part = ref[at, p * LANES : (p + 1) * LANES]
                pieces.append((part * cosine - swap_halves(part) * sine).astype(bf16))
        pieces.append(grad_v[at, :].astype(bf16))
        grad_projected = jnp.concatenate(pieces, axis=1)
        x = tokens[at, :].astype(f32)
        factor = lax.rsqrt(jnp.mean(x * x, axis=-1, keepdims=True) + norm_epsilon)
        normed = (x * factor * gain_one[...]).astype(bf16)
        grad_in_proj[...] += mm_tn(normed, grad_projected)
        grad_normed = mm_nt(grad_projected, in_proj[...])
        weighted = grad_normed * gain_one[...]
        gain_out[0:1, :] += jnp.sum(grad_normed * x * factor, axis=0, keepdims=True)
        grad_in_out[at, :] = (
            grad_middle[at, :]
            + factor * weighted
            - x * (factor * factor * factor) * jnp.mean(weighted * x, axis=-1, keepdims=True)
        ).astype(bf16)
        return carry

    lax.fori_loop(0, SEQ // CH, tail, 0)

    @pl.when(row == pl.num_programs(0) - 1)
    def _():
        for j in range(9):
            flat[pl.ds(j, D, stride=9), :] = grad_in_proj[:, j * LANES : (j + 1) * LANES]
        for j in range(3):
            flat[pl.ds(9 * D + j, D, stride=3), :] = grad_out_proj[:, j * LANES : (j + 1) * LANES]
        share = LANES // experts
        count = D // share
        lanes = lane_ids((D, LANES))
        grad_router[...] = jnp.where(
            lanes // experts == row_ids((D, LANES)) % share, grad_router[...], 0.0
        )
        merged = grad_router[pl.ds(0, count, stride=share), :]
        for i in range(1, share):
            merged = merged + grad_router[pl.ds(i, count, stride=share), :]
        flat[12 * D : 12 * D + count, :] = merged
        spare = flat.shape[0] - (12 * D + count)
        flat[12 * D + count :, :] = jnp.zeros((spare, LANES), f32)
        n_dev = dense_out.shape[0]
        rows = dense_out.shape[1]
        half = n_dev // 2
        piece_lane = lane_ids((rows, LANES))
        for s in range(n_dev):
            exp_rel = lax.bitwise_xor(s // n_tp, place[0])
            rel = (
                (exp_rel % 2) * half + (exp_rel // 2) * n_tp + lax.bitwise_xor(s % n_tp, place[1])
            )
            start, off = divmod(shard * s, LANES)
            piece = flat[start : start + rows, :]
            if off:
                piece = jnp.where(
                    piece_lane < LANES - off,
                    pltpu.roll(piece, LANES - off, 1),
                    pltpu.roll(flat[start + 1 : start + 1 + rows, :], LANES - off, 1),
                )
            dense_out[rel] = piece.astype(bf16)


def backward(win, place, parts, tokens, saved, marks, cosine, sine, gains, weights, sizes):
    experts, n_exp, n_tp, shard, shard_rows = sizes
    q, k, v, feat, mixed, middle, rows_arr, probs = saved
    tok = tokens.shape[0]

    def rows(width):
        return pl.BlockSpec((SEQ, width), lambda i, *_: (i, 0))

    flat_rows = shard * n_exp * n_tp // LANES + shard_rows + 8
    return call(
        partial(backward_kernel, experts=experts, n_tp=n_tp, parts=len(parts), shard=shard),
        grid_spec=pltpu.PrefetchScalarGridSpec(
            num_scalar_prefetch=2,
            grid=(tok // SEQ,),
            in_specs=[rows(XW)] * len(parts)
            + [
                rows(D), rows(XW), rows(LANES), rows(D), rows(D), rows(D), rows(D), rows(D),
                pl.BlockSpec((HEADS, SEQ, LANES), lambda i, *_: (0, i, 0)),
                rows(LANES), rows(LANES), rows(LANES), whole((1, D)), whole((1, D)),
                whole((D, 3 * D)), whole((D, D)), whole((D, LANES)),
            ],
            out_specs=[
                rows(D), rows(D), whole((n_exp * n_tp, shard_rows, LANES)), whole((8, D)), whole((8, LANES)),
            ],
            scratch_shapes=[
                pltpu.VMEM((SEQ, D), f32),
                pltpu.VMEM((SEQ, D), bf16),
                pltpu.VMEM((PAIRS, SEQ, 2 * LANES), bf16),
                pltpu.VMEM((PAIRS, SEQ, 2 * LANES), bf16),
                pltpu.VMEM((SEQ, D), f32),
                pltpu.VMEM((SEQ, D), f32),
                pltpu.VMEM((SEQ, D), f32),
                pltpu.VMEM((D, 3 * D), f32),
                pltpu.VMEM((D, D), f32),
                pltpu.VMEM((D, LANES), f32),
                pltpu.VMEM((flat_rows, LANES), f32),
            ],
        ),
        out_shape=[
            jax.ShapeDtypeStruct((tok, D), bf16),
            jax.ShapeDtypeStruct((tok, D), bf16),
            jax.ShapeDtypeStruct((n_exp * n_tp, shard_rows, LANES), bf16),
            jax.ShapeDtypeStruct((8, D), f32),
            jax.ShapeDtypeStruct((8, LANES), f32),
        ],
        cost_estimate=cost(4e10, 3e7),
        name="attention_backward",
    )(
        win, place, *parts, tokens, rows_arr, probs, middle, mixed, q, k, v, feat, marks,
        cosine, sine, *gains, *weights,
    )


def swap(values, axis, mask):
    size = lax.axis_size(axis)
    return lax.ppermute(values, axis, [(i, i ^ mask) for i in range(size)])


def add_up(parts):
    total = parts[0].astype(f32)
    for part in parts[1:]:
        total = total + part.astype(f32)
    return total


def even_sum(parts):
    while len(parts) > 1:
        parts = [parts[i] + parts[i + 1] for i in range(0, len(parts), 2)]
    return parts[0]


def adamw_update(old_state, grad_value, rate, decay, step_value):
    moment_one = moment_rate * old_state[1] + (1.0 - moment_rate) * grad_value
    moment_two = moment_rate * old_state[2] + (1.0 - moment_rate) * grad_value * grad_value
    correction = 1.0 - jnp.power(moment_rate, step_value)
    master = old_state[0] - rate * (
        moment_one / correction / (jnp.sqrt(moment_two / correction) + adam_epsilon)
        + decay * old_state[0]
    )
    average = average_rate * old_state[3] + (1.0 - average_rate) * master
    return jnp.stack([master, moment_one, moment_two, average])


def local(
    tokens, cotangent, routes, segments, variates, positions, step_count,
    dense_state, gate_up_state, down_state, small_state,
):
    tok = tokens.shape[0]
    n_exp, n_tp = lax.axis_size("exp"), lax.axis_size("tp")
    experts = n_exp * gate_up_state.shape[1]
    cap = 2 * tok * TOP // experts
    my_exp, my_tp = lax.axis_index("exp"), lax.axis_index("tp")
    place = jnp.stack([my_exp, my_tp]).astype(jnp.int32)
    shard = dense_state.shape[1]
    shard_rows = -(-shard // (16 * LANES)) * 16

    own = jnp.pad(dense_state[0].astype(bf16), (0, shard_rows * LANES - shard))
    own = own.reshape(1, shard_rows, LANES)
    line = jnp.concatenate([own] + [swap(own, "tp", j) for j in range(1, n_tp)], axis=0)
    plane = [line] + [swap(line, "exp", m) for m in range(2, n_exp, 2)]
    pairs = jnp.stack(plane)
    both = jnp.stack([pairs, swap(pairs, "exp", 1)], axis=1)
    weights = unpack_dense(
        place, both.reshape(n_exp * n_tp, shard_rows, LANES), shard, experts, n_tp
    )

    gate_up = gate_up_state[0, 0].astype(bf16)
    down = down_state[0, 0].astype(bf16)
    gate_up = jnp.concatenate(
        [gate_up] + [swap(gate_up, "tp", j) for j in range(1, n_tp)], axis=2
    )
    down = jnp.concatenate([down] + [swap(down, "tp", j) for j in range(1, n_tp)], axis=0)
    ff = gate_up.shape[2]
    cuts = ff // LANES
    packed = jnp.concatenate(
        [
            gate_up.reshape(2 * D, cuts, LANES).transpose(1, 0, 2),
            down.reshape(cuts, LANES, 3, LANES).transpose(0, 2, 1, 3).reshape(cuts, D, LANES),
        ],
        axis=1,
    )
    expert_weights = {0: packed}
    for m in range(2, n_exp, 2):
        expert_weights[m] = swap(packed, "exp", m)
    for m in range(0, n_exp, 2):
        expert_weights[m + 1] = swap(expert_weights[m], "exp", 1)

    near = lax.bitwise_xor(routes, my_exp.astype(jnp.int32))
    blocks = tok // CH
    ids = jnp.arange(experts, dtype=jnp.int32)
    named = (near[:, 0:1] == ids) | (near[:, 1:2] == ids)
    named_blocks = named.reshape(blocks, CH, experts)
    steps = jnp.arange(CH, dtype=jnp.int32)
    before = (steps[:, None] > steps[None, :]).astype(bf16)
    rank = jnp.einsum(
        "st,bte->bse", before, named_blocks.astype(bf16), preferred_element_type=f32
    )
    counts = jnp.sum(named_blocks.astype(jnp.int32), axis=1)
    block_ids = jnp.arange(blocks, dtype=jnp.int32)
    base = jnp.sum(
        jnp.where((block_ids[:, None] > block_ids[None, :])[:, :, None], counts[None], 0), axis=1
    )
    odd = base % 16
    spot = jnp.where(named_blocks, rank + odd[:, None, :].astype(f32), -1.0).reshape(tok, experts)
    place_lanes = spot.T
    place_rows = jnp.pad(spot, ((0, 0), (0, LANES - experts)), constant_values=-1.0)
    window_counts = jnp.max((odd + counts) // WIN + 1, axis=1)
    slot_steps = (jnp.sum(counts, axis=0) + SLOT - 1) // SLOT
    table = jnp.concatenate([(base - odd).reshape(-1), window_counts, slot_steps])

    seg, var = segments.reshape(tok, 1), variates.reshape(tok, 1)
    lanes = jnp.arange(LANES, dtype=jnp.int32)[None, :]
    marks = jnp.where(
        lanes < SEG_IDS,
        seg == lanes,
        jnp.where(lanes < LSE_LANE, var == lanes % VAR_IDS, lanes < LSE_LANE + 3),
    ).astype(bf16)
    small_params = small_state[0]
    gains = (small_params[:D].reshape(1, D), small_params[D : 2 * D].reshape(1, D))
    score_bias = small_params[2 * D :].reshape(2, HEADS)
    high = lax.reduce_precision(score_bias, 8, 7)
    mid = lax.reduce_precision(score_bias - high, 8, 7)
    low = lax.reduce_precision(score_bias - high - mid, 8, 7)
    pieces = jnp.stack([high, mid, low], axis=1).transpose(2, 0, 1)
    biases = jnp.concatenate(
        [
            jnp.full((HEADS, SEG_IDS), -FAR, f32),
            jnp.repeat(pieces.reshape(HEADS, 6), VAR_IDS, axis=1),
            jnp.zeros((HEADS, LANES - LSE_LANE), f32),
        ],
        axis=1,
    )
    biases = jnp.pad(biases, ((0, 2), (0, 0)))
    head_ids = segments[:, ::QB]
    tail_ids = segments[:, QB - 1 :: QB]
    lowest = jnp.sum((segments[:, None, :] < head_ids[:, :, None]).astype(jnp.int32), axis=2)
    highest = jnp.sum((segments[:, None, :] <= tail_ids[:, :, None]).astype(jnp.int32), axis=2)
    win_start = lowest // QB
    win_count = (highest + QB - 1) // QB - win_start
    win = jnp.stack([win_start, win_count], axis=2).reshape(-1)
    frequency = jnp.exp(jnp.arange(HD // 2, dtype=f32) * (-2.0 * math.log(10000.0) / HD))
    angles = positions.reshape(tok, 1).astype(f32) * jnp.tile(frequency, 4)[None, :]
    cosine = jnp.cos(angles)
    sine = jnp.sin(angles) * jnp.where(lanes % HD < HD // 2, -1.0, 1.0)

    saved = forward(
        win, tokens, cotangent, cosine, sine, marks, near, *gains, biases, weights, experts
    )
    routed = saved[6]
    groups = [(0, 1), (2, 3, 4, 5), (6, 7)] if n_exp == 8 else [
        tuple(range(i, i + 4)) for i in range(0, n_exp, 4)
    ]
    parts, expert_grads = [], {}
    for group in groups:
        part, grads = run_experts(
            table, [expert_weights[r] for r in group], routed, place_lanes, place_rows, group, experts, cap
        )
        parts.append(part)
        expert_grads.update(zip(group, grads))

    if len(parts) > 3:
        parts = [add_up(parts).astype(bf16)]

    block_out, grad_in, dense_grad, gain_grad, bias_grad = backward(
        win, place, parts, tokens, saved, marks, cosine, sine, gains, weights,
        (experts, n_exp, n_tp, shard, shard_rows),
    )

    halves = []
    for m in range(0, n_exp, 2):
        half = add_up([expert_grads[m], swap(expert_grads[m + 1], "exp", 1)])
        halves.append(half.astype(bf16))
    mine = add_up([halves[0]] + [swap(halves[m // 2], "exp", m) for m in range(2, n_exp, 2)])
    mine = mine.astype(bf16)
    mine_in = mine[:, : 2 * D].transpose(1, 0, 2).reshape(2, D, n_tp, ff // n_tp)
    mine_down = (
        mine[:, 2 * D :].reshape(cuts, 3, LANES, LANES).transpose(0, 2, 1, 3)
        .reshape(n_tp, ff // n_tp, D)
    )
    grad_gate_up = add_up(
        [mine_in[:, :, 0]] + [swap(mine_in[:, :, j], "tp", j) for j in range(1, n_tp)]
    )[None]
    grad_down = add_up(
        [mine_down[0]] + [swap(mine_down[j], "tp", j) for j in range(1, n_tp)]
    )[None]

    dense_grad = dense_grad.reshape(2, n_exp // 2, n_tp, shard_rows, LANES)
    dense_half = add_up([dense_grad[0], swap(dense_grad[1], "exp", 1)]).astype(bf16)
    dense_line = add_up(
        [dense_half[0]] + [swap(dense_half[m // 2], "exp", m) for m in range(2, n_exp, 2)]
    ).astype(bf16)
    dense_mine = add_up(
        [dense_line[0]] + [swap(dense_line[j], "tp", j) for j in range(1, n_tp)]
    )
    dense_mine = dense_mine.reshape(-1)[:shard]

    same = jnp.sum(bias_grad[:HEADS, SEG_IDS : SEG_IDS + VAR_IDS], axis=1)
    other_lane = SEG_IDS + 3 * VAR_IDS
    other = jnp.sum(bias_grad[:HEADS, other_lane : other_lane + VAR_IDS], axis=1)
    small_grad = jnp.concatenate([gain_grad[0], gain_grad[1], same, other])
    small_grad = jnp.pad(small_grad, (0, 1024 - small_grad.shape[0])).reshape(8, LANES)
    small_grad = small_grad + swap(small_grad, "exp", 1)
    small_grad = even_sum([small_grad] + [swap(small_grad, "exp", m) for m in range(2, n_exp, 2)])
    small_grad = even_sum([small_grad] + [swap(small_grad, "tp", j) for j in range(1, n_tp)])
    small_grad = small_grad.reshape(-1)[: small_state.shape[1]]

    step_value = step_count[0].astype(f32)
    dense_new = adamw_update(dense_state, dense_mine, rate_dense, weight_decay, step_value)
    gate_up_new = adamw_update(gate_up_state, grad_gate_up, rate_expert, weight_decay, step_value)
    down_new = adamw_update(down_state, grad_down, rate_expert, weight_decay, step_value)
    small_new = adamw_update(small_state, small_grad, rate_small, 0.0, step_value)
    return (
        block_out,
        grad_in,
        dense_new,
        dense_new[0].astype(bf16),
        gate_up_new,
        gate_up_new[0].astype(bf16),
        down_new,
        down_new[0].astype(bf16),
        small_new,
    )


def solution(mesh):
    in_specs = (
        P(("exp", "tp"), None),
        P(("exp", "tp"), None),
        P(("exp", "tp"), None),
        P(("exp", "tp"), None),
        P(("exp", "tp"), None),
        P(("exp", "tp"), None),
        P(),
        P(None, ("exp", "tp")),
        P(None, "exp", None, None, "tp"),
        P(None, "exp", "tp", None),
        P(),
    )
    out_specs = (
        P(("exp", "tp"), None),
        P(("exp", "tp"), None),
        P(None, ("exp", "tp")),
        P(("exp", "tp")),
        P(None, "exp", None, None, "tp"),
        P("exp", None, None, "tp"),
        P(None, "exp", "tp", None),
        P("exp", "tp", None),
        P(),
    )
    return jax.shard_map(local, mesh=mesh, in_specs=in_specs, out_specs=out_specs, check_vma=False)
```

```python
from functools import partial
import math

import jax
import jax.numpy as jnp
from jax import lax
from jax.experimental import pallas as pl
from jax.experimental.pallas import tpu as pltpu
from jax.sharding import PartitionSpec as P

D = 384
HEADS = 6
HD = 64
PAIRS = HEADS // 2
TOP = 2
SEQ = 1024
LANES = 128
QB = 128
CH = 256
NBLK = SEQ // QB
WIN = 128
SLOT = 256
XW = 2 * D + LANES
SEG_IDS = 8
VAR_IDS = 4
LSE_LANE = SEG_IDS + 6 * VAR_IDS
END_LANE = LSE_LANE + 3 * HEADS
WIN_LANE = 64
FAR = 2.0**100
VMEM_BYTES = 32 * 1024 * 1024

norm_epsilon = 1e-06
moment_rate = 0.5
average_rate = 0.9
adam_epsilon = 1e-08
weight_decay = 0.1
rate_dense = 0.05
rate_expert = 0.04
rate_small = 0.2

bf16 = jnp.bfloat16
f32 = jnp.float32


def mm(left, right):
    return lax.dot_general(left, right, (((1,), (0,)), ((), ())), preferred_element_type=f32)


def mm_nt(left, right):
    return lax.dot_general(left, right, (((1,), (1,)), ((), ())), preferred_element_type=f32)


def mm_tn(left, right):
    return lax.dot_general(left, right, (((0,), (0,)), ((), ())), preferred_element_type=f32)


def lane_ids(shape):
    return lax.broadcasted_iota(jnp.int32, shape, len(shape) - 1)


def row_ids(shape):
    return lax.broadcasted_iota(jnp.int32, shape, 0)


def three_pieces(value):
    high = value.astype(bf16)
    rest = value - high.astype(f32)
    middle = rest.astype(bf16)
    low = (rest - middle.astype(f32)).astype(bf16)
    return high.astype(f32), middle.astype(f32), low.astype(f32)


def swap_halves(values):
    lane = lane_ids(values.shape)
    return jnp.where(
        lane % HD < HD // 2,
        pltpu.roll(values, LANES - HD // 2, 1),
        pltpu.roll(values, HD // 2, 1),
    )


def call(kernel, **kwargs):
    return pl.pallas_call(
        kernel,
        compiler_params=pltpu.CompilerParams(
            vmem_limit_bytes=VMEM_BYTES, dimension_semantics=("arbitrary",)
        ),
        **kwargs,
    )


def whole(shape):
    return pl.BlockSpec(shape, lambda *_: (0,) * len(shape))


def cost(flops, moved):
    return pl.CostEstimate(flops=int(flops), transcendentals=0, bytes_accessed=int(moved))


def unpack_kernel(place, here, there, in_out, out_out, router_out, flat, spread, *, shard, experts, n_tp):
    rows = here.shape[1]
    n_dev = 2 * here.shape[0]
    flat[...] = jnp.zeros(flat.shape, f32)
    lane = lane_ids((rows, LANES))
    odd = place[0] % 2 == 1
    for s in range(n_dev):
        exp = s // n_tp
        rel = lax.bitwise_xor(exp // 2, place[0] // 2) * n_tp + lax.bitwise_xor(s % n_tp, place[1])
        start, off = divmod(shard * s, LANES)
        one, other = here[rel].astype(f32), there[rel].astype(f32)
        piece = jnp.where(odd, other, one) if exp % 2 == 0 else jnp.where(odd, one, other)
        if off:
            piece = pltpu.roll(piece, off, 1)
            flat[start : start + rows] += jnp.where(lane >= off, piece, 0.0)
            flat[start + 1 : start + 1 + rows] += jnp.where(lane < off, piece, 0.0)
        else:
            flat[start : start + rows] += piece
    for j in range(9):
        in_out[:, j * LANES : (j + 1) * LANES] = flat[pl.ds(j, D, stride=9), :].astype(bf16)
    for j in range(3):
        out_out[:, j * LANES : (j + 1) * LANES] = flat[pl.ds(9 * D + j, D, stride=3), :].astype(bf16)
    share = LANES // experts
    count = D // share
    for i in range(share):
        spread[pl.ds(i, count, stride=share), :] = flat[12 * D : 12 * D + count, :]
    lanes = lane_ids((D, LANES))
    kept = jnp.where(lanes // experts == row_ids((D, LANES)) % share, spread[...], 0.0).astype(bf16)
    fold_lane = lane_ids((LANES, LANES))
    fold = (row_ids((LANES, LANES)) % experts == lax.bitwise_xor(fold_lane, place[0])) & (
        fold_lane < experts
    )
    router_out[...] = mm(kept, jnp.where(fold, 1.0, 0.0).astype(bf16)).astype(bf16)


def unpack_dense(place, here, there, shard, experts, n_tp):
    total = shard * 2 * here.shape[0] // LANES
    flat_rows = total + here.shape[1] + 8
    return call(
        partial(unpack_kernel, shard=shard, experts=experts, n_tp=n_tp),
        grid_spec=pltpu.PrefetchScalarGridSpec(
            num_scalar_prefetch=1,
            grid=(1,),
            in_specs=[whole(here.shape), whole(there.shape)],
            out_specs=[whole((D, 3 * D)), whole((D, D)), whole((D, LANES))],
            scratch_shapes=[pltpu.VMEM((flat_rows, LANES), f32), pltpu.VMEM((D, LANES), f32)],
        ),
        out_shape=[
            jax.ShapeDtypeStruct((D, 3 * D), bf16),
            jax.ShapeDtypeStruct((D, D), bf16),
            jax.ShapeDtypeStruct((D, LANES), bf16),
        ],
        cost_estimate=cost(1e8, 4e6),
        name="unpack_dense",
    )(place, here, there)


def key_features(marks):
    lane = lane_ids(marks.shape)
    flip = (lane < SEG_IDS) | ((lane >= SEG_IDS + 3 * VAR_IDS) & (lane < LSE_LANE))
    return jnp.where(flip, 1.0 - marks, marks)


def in_windows(win, row, block, step):
    low, count = win[row, 2 * block], win[row, 2 * block + 1]
    for blocks in (2, 3, 4, 5):
        keys = blocks * QB
        fits = count <= 2 if blocks == 2 else count == blocks

        @pl.when(fits)
        def _(keys=keys):
            step(pl.multiple_of(jnp.minimum(low, SEQ - keys), 16), keys)

    @pl.when(count > 5)
    def _():
        step(0, SEQ)


def prepare_kernel(
    place, routes, segs, vars_, positions, small,
    lanes_out, rows_out, table_out, win_out, marks_out, cos_out, sin_out, biases_out, *, experts,
):
    tok = routes.shape[1]
    blocks = tok // CH
    above = jnp.where(row_ids((CH, CH)) < lane_ids((CH, CH)), 1.0, 0.0).astype(bf16)
    base = jnp.zeros((experts, 1), f32)
    lane = lane_ids((experts, LANES))
    table = jnp.zeros((experts, LANES), f32)
    rel = lax.bitwise_xor(row_ids((experts, CH)), place[0])
    fill = jnp.full((LANES - experts, CH), -1.0, f32)
    for b in range(blocks):
        at = slice(b * CH, (b + 1) * CH)
        named = (routes[0:1, at] == rel) | (routes[1:2, at] == rel)
        ones = jnp.where(named, 1.0, 0.0)
        rank = mm(ones.astype(bf16), above)
        odd = base - 16.0 * jnp.floor(base * (1.0 / 16.0))
        spot = jnp.where(named, rank + odd, -1.0)
        lanes_out[:, at] = spot
        rows_out[at, :] = jnp.concatenate([spot, fill], axis=0).T
        count = jnp.sum(ones, axis=1, keepdims=True)
        windows = jnp.floor((odd + count) * (1.0 / WIN)) + 1.0
        table = jnp.where(lane == b, base - odd, jnp.where(lane == WIN_LANE + b, windows, table))
        base = base + count
    steps = jnp.floor((base + (SLOT - 1)) * (1.0 / SLOT))
    table_out[...] = jnp.where(lane == 2 * WIN_LANE - 1, steps, table).astype(jnp.int32)

    identity = jnp.where(row_ids((LANES, LANES)) == lane_ids((LANES, LANES)), 1.0, 0.0).astype(bf16)
    feature = row_ids((LANES, SEQ))
    two = row_ids((8, SEQ))
    spread = jnp.where(row_ids((8, LANES)) < 2, 1.0, 0.0).astype(bf16)
    lane = lane_ids((1, LANES))
    frequency = jnp.exp(
        (lane % (HD // 2)).astype(f32) * (-2.0 * math.log(10000.0) / HD)
    )
    sign = jnp.where(lane % HD < HD // 2, -1.0, 1.0)
    win = jnp.zeros(win_out.shape, f32)
    win_row, win_lane = row_ids(win_out.shape), lane_ids(win_out.shape)
    for i in range(segs.shape[0]):
        at = slice(i * SEQ, (i + 1) * SEQ)
        seg, var = segs[i : i + 1, :], vars_[i : i + 1, :]
        marks = jnp.where(
            feature < SEG_IDS,
            jnp.where(seg == feature, 1.0, 0.0),
            jnp.where(
                feature < LSE_LANE,
                jnp.where(var == feature % VAR_IDS, 1.0, 0.0),
                jnp.where(feature < END_LANE, 1.0, 0.0),
            ),
        ).astype(bf16)
        marks_out[at, :] = mm_tn(marks, identity).astype(bf16)
        place_in_time = positions[i : i + 1, :]
        low = lax.bitwise_and(place_in_time, 31)
        halves = jnp.where(
            two == 0, (place_in_time - low).astype(f32), jnp.where(two == 1, low.astype(f32), 0.0)
        ).astype(bf16)
        angles = mm_tn(halves, spread) * frequency
        cos_out[at, :] = jnp.cos(angles)
        sin_out[at, :] = jnp.sin(angles) * sign
        for q in range(NBLK):
            head_id, tail_id = seg[:, q * QB : q * QB + 1], seg[:, (q + 1) * QB - 1 : (q + 1) * QB]
            first = jnp.sum(jnp.where(seg < head_id, 1.0, 0.0), axis=1, keepdims=True)
            last = jnp.sum(jnp.where(seg <= tail_id, 1.0, 0.0), axis=1, keepdims=True)
            first = 16.0 * jnp.floor(first * (1.0 / 16.0))
            keys = jnp.floor((last - first + (QB - 1)) * (1.0 / QB))
            win = jnp.where(
                (win_row == i) & (win_lane == 2 * q),
                first,
                jnp.where((win_row == i) & (win_lane == 2 * q + 1), keys, win),
            )
    win_out[...] = win.astype(jnp.int32)

    shape = (8, LANES)
    head, lanes = row_ids(shape), lane_ids(shape)
    bias = jnp.broadcast_to(small[0:1, 2 * D : 2 * D + 2 * HEADS], (8, 2 * HEADS))
    bias_row, bias_lane = row_ids(bias.shape), lane_ids(bias.shape)
    filled = jnp.where(lanes < SEG_IDS, -FAR, 0.0)
    for kind in range(2):
        own = jnp.sum(
            jnp.where(bias_lane == kind * HEADS + bias_row, bias, 0.0), axis=1, keepdims=True
        )
        for i, piece in enumerate(three_pieces(own)):
            first = SEG_IDS + (3 * kind + i) * VAR_IDS
            filled = jnp.where((lanes >= first) & (lanes < first + VAR_IDS), piece, filled)
    biases_out[...] = jnp.where(head < HEADS, filled, 0.0)


def prepare(place, routes, segs, vars_, positions, small, experts):
    tok = routes.shape[1]
    seqs = segs.shape[0]
    shapes = [
        ((experts, tok), f32), ((tok, LANES), f32), ((experts, LANES), jnp.int32),
        ((-(-seqs // 8) * 8, LANES), jnp.int32), ((tok, LANES), bf16), ((tok, LANES), f32),
        ((tok, LANES), f32), ((8, LANES), f32),
    ]
    return call(
        partial(prepare_kernel, experts=experts),
        grid_spec=pltpu.PrefetchScalarGridSpec(
            num_scalar_prefetch=1,
            grid=(1,),
            in_specs=[whole(a.shape) for a in (routes, segs, vars_, positions, small)],
            out_specs=[whole(shape) for shape, _ in shapes],
        ),
        out_shape=[jax.ShapeDtypeStruct(shape, dtype) for shape, dtype in shapes],
        cost_estimate=cost(1e9, 8e6),
        name="prepare",
    )(place, routes, segs, vars_, positions, small)


def forward_kernel(
    win, tokens, cot, cos_ref, sin_ref, marks_ref, place_rows, small, biases,
    in_proj, out_proj, router,
    q_out, k_out, v_out, lse_out, mixed_out, middle_out, rows_out, probs_out,
    keys_aug, values_aug, *, experts,
):
    row = pl.program_id(0)
    gain_one, gain_two = small[0:1, :D], small[0:1, D : 2 * D]
    for p in range(PAIRS):
        values_aug[p, :, LANES:] = jnp.ones((SEQ, LANES), bf16)

    def project(c, carry):
        at = pl.ds(pl.multiple_of(c * CH, CH), CH)
        x = tokens[at, :].astype(f32)
        factor = lax.rsqrt(jnp.mean(x * x, axis=-1, keepdims=True) + norm_epsilon)
        normed = (x * factor * gain_one).astype(bf16)
        projected = mm(normed, in_proj[...])
        cosine, sine = cos_ref[at, :], sin_ref[at, :]
        features = key_features(marks_ref[at, :].astype(f32)).astype(bf16)
        for j in range(2 * PAIRS):
            part = projected[:, j * LANES : (j + 1) * LANES]
            turned = part * cosine + swap_halves(part) * sine
            if j < PAIRS:
                q_out[at, j * LANES : (j + 1) * LANES] = (
                    turned.astype(bf16) * jnp.asarray(HD**-0.5, bf16)
                )
            else:
                p = j - PAIRS
                turned = turned.astype(bf16)
                k_out[at, p * LANES : (p + 1) * LANES] = turned
                keys_aug[p, at, :LANES] = turned
                keys_aug[p, at, LANES:] = features
        for p in range(PAIRS):
            part = projected[:, 2 * D + p * LANES : 2 * D + (p + 1) * LANES].astype(bf16)
            v_out[at, p * LANES : (p + 1) * LANES] = part
            values_aug[p, at, :LANES] = part
        return carry

    lax.fori_loop(0, SEQ // CH, project, 0)

    lane = lane_ids((QB, LANES))
    first = jnp.where(lane_ids((1, LANES)) < HD, 1.0, 0.0).astype(bf16)
    second = jnp.where(lane_ids((1, LANES)) >= HD, 1.0, 0.0).astype(bf16)

    def attend(block, carry):
        at = pl.ds(pl.multiple_of(block * QB, QB), QB)
        marks = marks_ref[at, :].astype(f32)

        def step(key_start, keys):
            key_at = pl.ds(key_start, keys)
            logs = jnp.zeros((QB, LANES), f32)
            for p in range(PAIRS):
                queries = q_out[at, p * LANES : (p + 1) * LANES]
                feat = [
                    (marks * biases[2 * p + i : 2 * p + i + 1, :]).astype(bf16) for i in range(2)
                ]
                stacked = jnp.concatenate(
                    [
                        jnp.concatenate([queries * first, feat[0]], axis=1),
                        jnp.concatenate([queries * second, feat[1]], axis=1),
                    ],
                    axis=0,
                )
                scores = mm_nt(stacked, keys_aug[p, key_at, :])
                top = jnp.max(scores, axis=1, keepdims=True)
                weights = jnp.exp(scores - top).astype(bf16)
                sums = mm(weights, values_aug[p, key_at, :])
                total = sums[:, LANES:]
                mixed = sums[:, :LANES] / total
                mixed_out[at, p * LANES : (p + 1) * LANES] = jnp.where(
                    lane < HD, mixed[:QB], mixed[QB:]
                ).astype(bf16)
                pieces = three_pieces(-(top + jnp.log(total)))
                for i in range(2):
                    for j, piece in enumerate(pieces):
                        logs = jnp.where(
                            lane == LSE_LANE + 3 * (2 * p + i) + j,
                            piece[i * QB : (i + 1) * QB],
                            logs,
                        )
            lse_out[at, :] = logs.astype(bf16)

        in_windows(win, row, block, step)
        return carry

    lax.fori_loop(0, NBLK, attend, 0)

    def finish(c, carry):
        at = pl.ds(pl.multiple_of(c * CH, CH), CH)
        middle = tokens[at, :].astype(f32) + mm(mixed_out[at, :], out_proj[...])
        middle_out[at, :] = middle
        factor = lax.rsqrt(jnp.mean(middle * middle, axis=-1, keepdims=True) + norm_epsilon)
        normed = (middle * factor * gain_two).astype(bf16)
        rows_out[at, :D] = normed
        rows_out[at, D : 2 * D] = cot[at, :]
        logits = mm(normed, router[...])
        named = place_rows[at, :] >= 0.0
        top = jnp.max(jnp.where(named, logits, -3.0e38), axis=1, keepdims=True)
        weights = jnp.where(named, jnp.exp(jnp.where(named, logits - top, 0.0)), 0.0)
        probs = weights / jnp.sum(weights, axis=1, keepdims=True)
        probs_out[at, :] = probs
        high, mid, low = three_pieces(probs)
        rows_out[at, 2 * D :] = (
            high + pltpu.roll(mid, experts, 1) + pltpu.roll(low, 2 * experts, 1)
        ).astype(bf16)
        return carry

    lax.fori_loop(0, SEQ // CH, finish, 0)


def forward(win, tokens, cot, cosine, sine, marks, place_rows, small, biases, weights, experts):
    tok = tokens.shape[0]
    seqs = tok // SEQ

    def rows(width):
        return pl.BlockSpec((SEQ, width), lambda i, *_: (i, 0))

    in_proj, out_proj, router = weights
    return call(
        partial(forward_kernel, experts=experts),
        grid_spec=pltpu.PrefetchScalarGridSpec(
            num_scalar_prefetch=1,
            grid=(seqs,),
            in_specs=[
                rows(D), rows(D), rows(LANES), rows(LANES), rows(LANES), rows(LANES),
                whole(small.shape), whole((8, LANES)),
                whole((D, 3 * D)), whole((D, D)), whole((D, LANES)),
            ],
            out_specs=[
                rows(D), rows(D), rows(D), rows(LANES), rows(D), rows(D), rows(XW), rows(LANES),
            ],
            scratch_shapes=[
                pltpu.VMEM((PAIRS, SEQ, 2 * LANES), bf16),
                pltpu.VMEM((PAIRS, SEQ, 2 * LANES), bf16),
            ],
        ),
        out_shape=[
            jax.ShapeDtypeStruct((tok, D), bf16),
            jax.ShapeDtypeStruct((tok, D), bf16),
            jax.ShapeDtypeStruct((tok, D), bf16),
            jax.ShapeDtypeStruct((tok, LANES), bf16),
            jax.ShapeDtypeStruct((tok, D), bf16),
            jax.ShapeDtypeStruct((tok, D), f32),
            jax.ShapeDtypeStruct((tok, XW), bf16),
            jax.ShapeDtypeStruct((tok, LANES), f32),
        ],
        cost_estimate=cost(2e10, 2e7),
        name="attention_forward",
    )(win, tokens, cot, cosine, sine, marks, place_rows, small, biases, *weights)


def experts_kernel(table, *refs, group, experts, blocks):
    size = len(group)
    weights_hbm = refs[:size]
    rows, place_lanes, place_rows = refs[size : size + 3]
    part_out = refs[size + 3]
    grads_hbm = refs[size + 4 : 2 * size + 4]
    slots, weights, grads, grad_in, grad_down, total, in_sems, out_sems = refs[2 * size + 4 :]
    ff = grad_down.shape[0]
    cuts = ff // LANES
    arrivals = [
        pltpu.make_async_copy(weights_hbm[g], weights.at[g], in_sems.at[g]) for g in range(size)
    ]
    departures = [
        pltpu.make_async_copy(grads.at[g], grads_hbm[g], out_sems.at[g]) for g in range(size)
    ]
    for copy in arrivals:
        copy.start()

    def first_slot(block, r):
        return pl.multiple_of(table[r, block], 16)

    for g in range(size):
        slots[g, 0:16, :] = jnp.zeros((16, XW), bf16)

    def gather(block, carry):
        at = pl.ds(pl.multiple_of(block * CH, CH), CH)
        source = rows[at, :]
        slot = row_ids((WIN, CH)).astype(f32)

        def picks(r, first):
            return jnp.where(place_lanes[r : r + 1, at] - first == slot, 1.0, 0.0).astype(bf16)

        moved = mm(jnp.concatenate([picks(r, 0.0) for r in group], axis=0), source).astype(bf16)
        for g, r in enumerate(group):
            start = first_slot(block, r)
            slots[g, pl.ds(start, 16), :] += moved[g * WIN : g * WIN + 16]
            slots[g, pl.ds(start + 16, WIN - 16), :] = moved[g * WIN + 16 : (g + 1) * WIN]

            def more(w, inner, g=g, r=r, start=start):
                slots[g, pl.ds(start + w * WIN, WIN), :] = mm(
                    picks(r, (w * WIN).astype(f32)), source
                ).astype(bf16)
                return inner

            lax.fori_loop(1, table[r, WIN_LANE + block], more, 0)
        return carry

    lax.fori_loop(0, blocks, gather, 0)

    for g, r in enumerate(group):
        end = first_slot(blocks - 1, r) + table[r, WIN_LANE + blocks - 1] * WIN
        slots[g, pl.ds(end, SLOT), :] = jnp.zeros((SLOT, XW), bf16)
        arrivals[g].wait()
        gate_w = jnp.concatenate([weights[g, z, :D, :] for z in range(cuts)], axis=1)
        up_w = jnp.concatenate([weights[g, z, D : 2 * D, :] for z in range(cuts)], axis=1)
        down_w = jnp.concatenate(
            [
                jnp.concatenate(
                    [weights[g, z, (6 + j) * LANES : (7 + j) * LANES, :] for j in range(3)], axis=1
                )
                for z in range(cuts)
            ],
            axis=0,
        )
        grad_in[...] = jnp.zeros(grad_in.shape, f32)
        grad_down[...] = jnp.zeros(grad_down.shape, f32)

        def step(i, carry, g=g, r=r, gate_w=gate_w, up_w=up_w, down_w=down_w):
            at = pl.ds(pl.multiple_of(i * SLOT, SLOT), SLOT)
            x = slots[g, at, :D]
            cot = slots[g, at, D : 2 * D].astype(f32)
            parts = slots[g, at, 2 * D :].astype(f32)
            prob = (
                parts[:, r : r + 1]
                + parts[:, experts + r : experts + r + 1]
                + parts[:, 2 * experts + r : 2 * experts + r + 1]
            )
            gate_pre = mm(x, gate_w)
            up_pre = mm(x, up_w)
            sigmoid = 1.0 / (1.0 + jnp.exp(-gate_pre))
            silu = gate_pre * sigmoid
            hidden = (silu * up_pre).astype(bf16)
            result = mm(hidden, down_w).astype(bf16).astype(f32)
            grad_result = (prob * cot).astype(bf16)
            grad_hidden = mm_nt(grad_result, down_w)
            grad_gate = (
                grad_hidden * up_pre * sigmoid * (1.0 + gate_pre * (1.0 - sigmoid))
            ).astype(bf16)
            grad_up = (grad_hidden * silu).astype(bf16)
            grad_rows = mm_nt(grad_gate, gate_w) + mm_nt(grad_up, up_w)
            grad_in[:, :ff] += mm_tn(x, grad_gate)
            grad_in[:, ff:] += mm_tn(x, grad_up)
            grad_down[...] += mm_tn(hidden, grad_result)
            score = jnp.sum(cot * result, axis=1, keepdims=True)
            high, mid, _ = three_pieces(jnp.broadcast_to(score, (SLOT, LANES)))
            lane = lane_ids((SLOT, LANES))
            slots[g, at, :D] = (prob * result).astype(bf16)
            slots[g, at, D : 2 * D] = grad_rows.astype(bf16)
            slots[g, at, 2 * D :] = jnp.where(
                lane == r, high, jnp.where(lane == experts + r, mid, 0.0)
            ).astype(bf16)
            return carry

        lax.fori_loop(0, table[r, 2 * WIN_LANE - 1], step, 0)
        for z in range(cuts):
            cols = slice(z * LANES, (z + 1) * LANES)
            grads[g, z, :D, :] = grad_in[:, cols].astype(bf16)
            grads[g, z, D : 2 * D, :] = grad_in[:, ff + z * LANES : ff + (z + 1) * LANES].astype(bf16)
            for j in range(3):
                grads[g, z, (6 + j) * LANES : (7 + j) * LANES, :] = grad_down[
                    cols, j * LANES : (j + 1) * LANES
                ].astype(bf16)
        departures[g].start()

    def scatter(block, carry):
        at = pl.ds(pl.multiple_of(block * CH, CH), CH)
        places = place_rows[at, :]
        slot = lane_ids((CH, WIN)).astype(f32)

        def picks(r, first):
            return jnp.where(places[:, r : r + 1] - first == slot, 1.0, 0.0).astype(bf16)

        source = jnp.concatenate(
            [slots[g, pl.ds(first_slot(block, r), WIN), :] for g, r in enumerate(group)], axis=0
        )
        total[...] = mm(jnp.concatenate([picks(r, 0.0) for r in group], axis=1), source)
        for g, r in enumerate(group):

            def more(w, inner, g=g, r=r):
                total[...] += mm(
                    picks(r, (w * WIN).astype(f32)),
                    slots[g, pl.ds(first_slot(block, r) + w * WIN, WIN), :],
                )
                return inner

            lax.fori_loop(1, table[r, WIN_LANE + block], more, 0)
        part_out[at, :] = total[...].astype(bf16)
        return carry

    lax.fori_loop(0, blocks, scatter, 0)
    for copy in departures:
        copy.wait()


def run_experts(table, weights, rows, place_lanes, place_rows, group, experts, cap):
    tok = rows.shape[0]
    ff = weights[0].shape[0] * LANES
    blocks = tok // CH
    shape = weights[0].shape
    size = len(group)
    there = [pl.BlockSpec(memory_space=pl.ANY)] * size
    out = call(
        partial(experts_kernel, group=group, experts=experts, blocks=blocks),
        grid_spec=pltpu.PrefetchScalarGridSpec(
            num_scalar_prefetch=1,
            grid=(1,),
            in_specs=there + [whole((tok, XW)), whole(place_lanes.shape), whole((tok, LANES))],
            out_specs=[whole((tok, XW))] + there,
            scratch_shapes=[
                pltpu.VMEM((size, cap + 4 * WIN + SLOT, XW), bf16),
                pltpu.VMEM((size, *shape), bf16),
                pltpu.VMEM((size, *shape), bf16),
                pltpu.VMEM((D, 2 * ff), f32),
                pltpu.VMEM((ff, D), f32),
                pltpu.VMEM((CH, XW), f32),
                pltpu.SemaphoreType.DMA((size,)),
                pltpu.SemaphoreType.DMA((size,)),
            ],
        ),
        out_shape=[jax.ShapeDtypeStruct((tok, XW), bf16)] + [jax.ShapeDtypeStruct(shape, bf16)] * size,
        cost_estimate=cost(4e9 * size, 3e6 * size + 8e6),
        name="experts",
    )(table, *weights, rows, place_lanes, place_rows)
    return out[0], out[1:]


def backward_kernel(
    win, place, *refs, experts, n_tp, parts, shard,
):
    part_refs = refs[:parts]
    (
        tokens, cot_ref, probs_ref, middle_ref, mixed_ref, q_ref, k_ref, v_ref, lse_ref, marks_ref,
        cos_ref, sin_ref, small, biases, in_proj, out_proj, router,
        block_out, grad_in_out, dense_out,
        grad_middle, grad_mixed, keys_aug, values_aug, grad_q, grad_k, grad_v,
        grad_in_proj, grad_out_proj, grad_router, flat, gain_out, bias_out,
    ) = refs[parts:]
    row = pl.program_id(0)
    gain_one, gain_two = small[0:1, :D], small[0:1, D : 2 * D]

    @pl.when(row == 0)
    def _():
        grad_in_proj[...] = jnp.zeros(grad_in_proj.shape, f32)
        grad_out_proj[...] = jnp.zeros(grad_out_proj.shape, f32)
        grad_router[...] = jnp.zeros(grad_router.shape, f32)
        gain_out[...] = jnp.zeros(gain_out.shape, f32)
        bias_out[...] = jnp.zeros(bias_out.shape, f32)

    fold_row, fold_lane = row_ids((LANES, LANES)), lane_ids((LANES, LANES))
    tile = jnp.where(
        (lax.bitwise_xor(fold_row, place[0]) == fold_lane % experts) & (fold_row < experts), 1.0, 0.0
    ).astype(bf16)

    def head(c, carry):
        at = pl.ds(pl.multiple_of(c * CH, CH), CH)
        back = part_refs[0][at, :].astype(f32)
        for ref in part_refs[1:]:
            back = back + ref[at, :].astype(f32)
        middle = middle_ref[at, :]
        block_out[at, :] = (middle + back[:, :D]).astype(bf16)
        scores = back[:, 2 * D :]
        scores = scores + pltpu.roll(scores, LANES - experts, 1)
        probs = probs_ref[at, :]
        inner = jnp.sum(probs * scores, axis=1, keepdims=True)
        grad_logits = (probs * (scores - inner)).astype(bf16)
        grad_normed = mm_nt(grad_logits, router[...]) + back[:, D : 2 * D]
        factor = lax.rsqrt(jnp.mean(middle * middle, axis=-1, keepdims=True) + norm_epsilon)
        normed = (middle * factor * gain_two).astype(bf16)
        grad_router[...] += mm_tn(normed, mm(grad_logits, tile).astype(bf16))
        weighted = grad_normed * gain_two
        gain_out[1:2, :] += jnp.sum(grad_normed * middle * factor, axis=0, keepdims=True)
        cot = cot_ref[at, :].astype(f32)
        grad = (
            cot
            + factor * weighted
            - middle
            * (factor * factor * factor)
            * jnp.mean(weighted * middle, axis=-1, keepdims=True)
        )
        grad_middle[at, :] = grad
        branch = grad.astype(bf16)
        grad_out_proj[...] += mm_tn(mixed_ref[at, :], branch)
        grad_mixed[at, :] = mm_nt(branch, out_proj[...]).astype(bf16)
        features = key_features(marks_ref[at, :].astype(f32)).astype(bf16)
        for p in range(PAIRS):
            cols = slice(p * LANES, (p + 1) * LANES)
            keys_aug[p, at, :LANES] = k_ref[at, cols]
            keys_aug[p, at, LANES:] = features
            values_aug[p, at, :LANES] = v_ref[at, cols]
            values_aug[p, at, LANES:] = features
        return carry

    lax.fori_loop(0, SEQ // CH, head, 0)
    grad_k[...] = jnp.zeros(grad_k.shape, f32)
    grad_v[...] = jnp.zeros(grad_v.shape, f32)

    lane = lane_ids((QB, LANES))
    first = jnp.where(lane_ids((1, LANES)) < HD, 1.0, 0.0).astype(bf16)
    second = jnp.where(lane_ids((1, LANES)) >= HD, 1.0, 0.0).astype(bf16)

    def attend(block, carry):
        at = pl.ds(pl.multiple_of(block * QB, QB), QB)
        marks = marks_ref[at, :].astype(f32)
        logs = lse_ref[at, :].astype(f32)

        def step(key_start, keys):
            key_at = pl.ds(key_start, keys)
            for p in range(PAIRS):
                cols = slice(p * LANES, (p + 1) * LANES)
                queries = q_ref[at, cols]
                out_grad = grad_mixed[at, cols]
                product = out_grad.astype(f32) * mixed_ref[at, cols].astype(f32)
                q_rows, g_rows = [], []
                for i, mask in enumerate((first, second)):
                    inside = (lane < HD) if i == 0 else (lane >= HD)
                    inner = -jnp.sum(jnp.where(inside, product, 0.0), axis=1, keepdims=True)
                    high, middle, low = three_pieces(jnp.broadcast_to(inner, (QB, LANES)))
                    extra = jnp.where(
                        lane == LSE_LANE,
                        high,
                        jnp.where(
                            lane == LSE_LANE + 1,
                            middle,
                            jnp.where(lane == LSE_LANE + 2, low, 0.0),
                        ),
                    ).astype(bf16)
                    h = 2 * p + i
                    mine = (lane >= LSE_LANE + 3 * h) & (lane < LSE_LANE + 3 * h + 3)
                    feat = jnp.where(mine, logs, marks * biases[h : h + 1, :]).astype(bf16)
                    q_rows.append(jnp.concatenate([queries * mask, feat], axis=1))
                    g_rows.append(jnp.concatenate([out_grad * mask, extra], axis=1))
                stacked = jnp.concatenate(q_rows, axis=0)
                grads = jnp.concatenate(g_rows, axis=0)
                keys_here = keys_aug[p, key_at, :]
                probs = jnp.exp(mm_nt(keys_here, stacked))
                shifted = mm_nt(values_aug[p, key_at, :], grads)
                grad_scores = (probs * shifted).astype(bf16)
                grad_v[key_at, cols] += mm(probs.astype(bf16), grads[:, :LANES])
                grad_k[key_at, cols] += mm(grad_scores, stacked[:, :LANES])
                back = mm_tn(grad_scores, keys_here)
                grad_q[at, cols] = (
                    jnp.where(lane < HD, back[:QB, :LANES], back[QB:, :LANES]) * HD**-0.5
                )
                for i in range(2):
                    bias_out[2 * p + i : 2 * p + i + 1, :] += jnp.sum(
                        marks * back[i * QB : (i + 1) * QB, LANES:], axis=0, keepdims=True
                    )

        in_windows(win, row, block, step)
        return carry

    lax.fori_loop(0, NBLK, attend, 0)

    def tail(c, carry):
        at = pl.ds(pl.multiple_of(c * CH, CH), CH)
        cosine, sine = cos_ref[at, :], sin_ref[at, :]
        pieces = []
        for ref in (grad_q, grad_k):
            for p in range(PAIRS):
                part = ref[at, p * LANES : (p + 1) * LANES]
                pieces.append((part * cosine - swap_halves(part) * sine).astype(bf16))
        pieces.append(grad_v[at, :].astype(bf16))
        grad_projected = jnp.concatenate(pieces, axis=1)
        x = tokens[at, :].astype(f32)
        factor = lax.rsqrt(jnp.mean(x * x, axis=-1, keepdims=True) + norm_epsilon)
        normed = (x * factor * gain_one).astype(bf16)
        grad_in_proj[...] += mm_tn(normed, grad_projected)
        grad_normed = mm_nt(grad_projected, in_proj[...])
        weighted = grad_normed * gain_one
        gain_out[0:1, :] += jnp.sum(grad_normed * x * factor, axis=0, keepdims=True)
        grad_in_out[at, :] = (
            grad_middle[at, :]
            + factor * weighted
            - x * (factor * factor * factor) * jnp.mean(weighted * x, axis=-1, keepdims=True)
        ).astype(bf16)
        return carry

    lax.fori_loop(0, SEQ // CH, tail, 0)

    @pl.when(row == pl.num_programs(0) - 1)
    def _():
        for j in range(9):
            flat[pl.ds(j, D, stride=9), :] = grad_in_proj[:, j * LANES : (j + 1) * LANES]
        for j in range(3):
            flat[pl.ds(9 * D + j, D, stride=3), :] = grad_out_proj[:, j * LANES : (j + 1) * LANES]
        share = LANES // experts
        count = D // share
        lanes = lane_ids((D, LANES))
        grad_router[...] = jnp.where(
            lanes // experts == row_ids((D, LANES)) % share, grad_router[...], 0.0
        )
        merged = grad_router[pl.ds(0, count, stride=share), :]
        for i in range(1, share):
            merged = merged + grad_router[pl.ds(i, count, stride=share), :]
        flat[12 * D : 12 * D + count, :] = merged
        spare = flat.shape[0] - (12 * D + count)
        flat[12 * D + count :, :] = jnp.zeros((spare, LANES), f32)
        n_dev = dense_out.shape[0]
        rows = dense_out.shape[1]
        half = n_dev // 2
        piece_lane = lane_ids((rows, LANES))
        for s in range(n_dev):
            exp_rel = lax.bitwise_xor(s // n_tp, place[0])
            rel = (
                (exp_rel % 2) * half + (exp_rel // 2) * n_tp + lax.bitwise_xor(s % n_tp, place[1])
            )
            start, off = divmod(shard * s, LANES)
            piece = flat[start : start + rows, :]
            if off:
                piece = jnp.where(
                    piece_lane < LANES - off,
                    pltpu.roll(piece, LANES - off, 1),
                    pltpu.roll(flat[start + 1 : start + 1 + rows, :], LANES - off, 1),
                )
            dense_out[rel] = piece.astype(bf16)
        shape = (8, LANES)
        bias_rows, bias_lanes = row_ids(shape), lane_ids(shape)
        sums = bias_out[...]
        extra = jnp.zeros((1, LANES), f32)
        for kind in range(2):
            first_lane = SEG_IDS + 3 * kind * VAR_IDS
            own = jnp.sum(
                jnp.where((bias_lanes >= first_lane) & (bias_lanes < first_lane + VAR_IDS), sums, 0.0),
                axis=1,
                keepdims=True,
            )
            extra = extra + jnp.sum(
                jnp.where((bias_lanes == bias_rows + kind * HEADS) & (bias_rows < HEADS), own, 0.0),
                axis=0,
                keepdims=True,
            )
        spare_rows = jnp.concatenate(
            [gain_out[i : i + 1, j * LANES : (j + 1) * LANES] for i in range(2) for j in range(3)]
            + [extra, jnp.zeros((1, LANES), f32)],
            axis=0,
        ).astype(bf16)
        for s in range(n_dev):
            dense_out[s, rows - 8 :, :] = spare_rows


def backward(win, place, parts, tokens, cot, saved, marks, cosine, sine, small, biases, weights, sizes):
    experts, n_exp, n_tp, shard, shard_rows = sizes
    q, k, v, lse, mixed, middle, _, probs = saved
    tok = tokens.shape[0]

    def rows(width):
        return pl.BlockSpec((SEQ, width), lambda i, *_: (i, 0))

    flat_rows = shard * n_exp * n_tp // LANES + shard_rows + 8
    return call(
        partial(backward_kernel, experts=experts, n_tp=n_tp, parts=len(parts), shard=shard),
        grid_spec=pltpu.PrefetchScalarGridSpec(
            num_scalar_prefetch=2,
            grid=(tok // SEQ,),
            in_specs=[rows(XW)] * len(parts)
            + [
                rows(D), rows(D), rows(LANES), rows(D), rows(D), rows(D), rows(D), rows(D),
                rows(LANES), rows(LANES), rows(LANES), rows(LANES), whole(small.shape),
                whole((8, LANES)), whole((D, 3 * D)), whole((D, D)), whole((D, LANES)),
            ],
            out_specs=[rows(D), rows(D), whole((n_exp * n_tp, shard_rows, LANES))],
            scratch_shapes=[
                pltpu.VMEM((SEQ, D), f32),
                pltpu.VMEM((SEQ, D), bf16),
                pltpu.VMEM((PAIRS, SEQ, 2 * LANES), bf16),
                pltpu.VMEM((PAIRS, SEQ, 2 * LANES), bf16),
                pltpu.VMEM((SEQ, D), f32),
                pltpu.VMEM((SEQ, D), f32),
                pltpu.VMEM((SEQ, D), f32),
                pltpu.VMEM((D, 3 * D), f32),
                pltpu.VMEM((D, D), f32),
                pltpu.VMEM((D, LANES), f32),
                pltpu.VMEM((flat_rows, LANES), f32),
                pltpu.VMEM((8, D), f32),
                pltpu.VMEM((8, LANES), f32),
            ],
        ),
        out_shape=[
            jax.ShapeDtypeStruct((tok, D), bf16),
            jax.ShapeDtypeStruct((tok, D), bf16),
            jax.ShapeDtypeStruct((n_exp * n_tp, shard_rows, LANES), bf16),
        ],
        cost_estimate=cost(4e10, 3e7),
        name="attention_backward",
    )(
        win, place, *parts, tokens, cot, probs, middle, mixed, q, k, v, lse, marks,
        cosine, sine, small, biases, *weights,
    )


def swap(values, axis, mask):
    size = lax.axis_size(axis)
    return lax.ppermute(values, axis, [(i, i ^ mask) for i in range(size)])


def add_up(parts):
    parts = [part.astype(f32) for part in parts]
    while len(parts) > 1:
        parts = [sum(parts[i + 1 : i + 2], parts[i]) for i in range(0, len(parts), 2)]
    return parts[0]


def adamw_update(old_state, grad_value, rate, decay, step_value):
    moment_one = moment_rate * old_state[1] + (1.0 - moment_rate) * grad_value
    moment_two = moment_rate * old_state[2] + (1.0 - moment_rate) * grad_value * grad_value
    correction = 1.0 - jnp.power(moment_rate, step_value)
    master = old_state[0] - rate * (
        moment_one / correction / (jnp.sqrt(moment_two / correction) + adam_epsilon)
        + decay * old_state[0]
    )
    average = average_rate * old_state[3] + (1.0 - average_rate) * master
    return jnp.stack([master, moment_one, moment_two, average])


def local(
    tokens, cotangent, routes, segments, variates, positions, step_count,
    dense_state, gate_up_state, down_state, small_state,
):
    tok = tokens.shape[0]
    n_exp, n_tp = lax.axis_size("exp"), lax.axis_size("tp")
    experts = n_exp * gate_up_state.shape[1]
    cap = 2 * tok * TOP // experts
    my_exp, my_tp = lax.axis_index("exp"), lax.axis_index("tp")
    place = jnp.stack([my_exp, my_tp]).astype(jnp.int32)
    shard = dense_state.shape[1]
    shard_rows = -(-(-(-shard // LANES) + 8) // 16) * 16

    def in_line(values):
        return [values] + [swap(values, "tp", j) for j in range(1, n_tp)]

    def in_plane(values):
        return [values] + [swap(values, "exp", m) for m in range(2, n_exp, 2)]

    own = jnp.pad(dense_state[0].astype(bf16), (0, shard_rows * LANES - shard))
    line = jnp.concatenate(in_line(own.reshape(1, shard_rows, LANES)), axis=0)
    routes_later, _ = lax.optimization_barrier((routes.T, line))
    prepared = prepare(place, routes_later, segments, variates, positions, small_state, experts)
    here = jnp.concatenate(in_plane(line), axis=0)

    gate_up = gate_up_state[0, 0].astype(bf16)
    down = down_state[0, 0].astype(bf16)
    slice_ff = gate_up.shape[2]
    ff = slice_ff * n_tp
    cuts = ff // LANES

    def pack(gate_up, down):
        count = gate_up.shape[2] // LANES
        return jnp.concatenate(
            [
                gate_up.reshape(2 * D, count, LANES).transpose(1, 0, 2),
                down.reshape(count, LANES, 3, LANES).transpose(0, 2, 1, 3).reshape(count, D, LANES),
            ],
            axis=1,
        )

    def unpack(packed):
        count = packed.shape[0]
        return (
            packed[:, : 2 * D].transpose(1, 0, 2).reshape(2, D, count * LANES),
            packed[:, 2 * D :].reshape(count, 3, LANES, LANES).transpose(0, 2, 1, 3)
            .reshape(count * LANES, D),
        )

    if slice_ff % LANES == 0:
        packed = jnp.concatenate(in_line(pack(gate_up, down)), axis=0)
    else:
        packed = pack(
            jnp.concatenate(in_line(gate_up), axis=2), jnp.concatenate(in_line(down), axis=0)
        )
    here, packed, prepared = lax.optimization_barrier((here, packed, prepared))
    place_lanes, place_rows, table, win, marks, cosine, sine, biases = prepared
    there = swap(here, "exp", 1)
    weights = unpack_dense(place, here, there, shard, experts, n_tp)
    expert_weights = {2 * i: values for i, values in enumerate(in_plane(packed))}
    expert_weights[1] = swap(packed, "exp", 1)
    saved = forward(
        win, tokens, cotangent, cosine, sine, marks, place_rows, small_state, biases, weights, experts
    )
    routed = saved[6]
    groups = [(0, 1)] + [tuple(range(i, min(i + 4, n_exp))) for i in range(2, n_exp, 4)]
    parts, expert_grads = [], {}
    for group in groups:
        part, grads = run_experts(
            table, [expert_weights[r] for r in group], routed, place_lanes, place_rows, group, experts, cap
        )
        parts.append(part)
        expert_grads.update(zip(group, grads))
        if len(parts) == 1:
            for m in range(2, n_exp, 2):
                values, _ = lax.optimization_barrier((expert_weights[m], part))
                expert_weights[m + 1] = swap(values, "exp", 1)
    if len(parts) > 3:
        parts = [add_up(parts).astype(bf16)]
    halves = [
        add_up([expert_grads[m], swap(expert_grads[m + 1], "exp", 1)]).astype(bf16)
        for m in range(0, n_exp, 2)
    ]
    parts, halves = lax.optimization_barrier((parts, halves))

    block_out, grad_in, dense_grad = backward(
        win, place, parts, tokens, cotangent, saved, marks, cosine, sine, small_state, biases, weights,
        (experts, n_exp, n_tp, shard, shard_rows),
    )

    mine = add_up(
        [halves[0]] + [swap(halves[m // 2], "exp", m) for m in range(2, n_exp, 2)]
    ).astype(bf16)
    dense_grad, mine = lax.optimization_barrier((dense_grad, mine))
    if slice_ff % LANES == 0:
        mine = mine.reshape(n_tp, slice_ff // LANES, 3 * D, LANES)
        arrived = [[mine[0]] + [swap(mine[j], "tp", j) for j in range(1, n_tp)]]
    else:
        mine_in, mine_down = unpack(mine)
        mine_in = mine_in.reshape(2, D, n_tp, slice_ff)
        mine_down = mine_down.reshape(n_tp, slice_ff, D)
        arrived = [
            [mine_in[:, :, 0]] + [swap(mine_in[:, :, j], "tp", j) for j in range(1, n_tp)],
            [mine_down[0]] + [swap(mine_down[j], "tp", j) for j in range(1, n_tp)],
        ]

    dense_grad = dense_grad.reshape(2, n_exp // 2, n_tp, shard_rows, LANES)
    dense_half = add_up([dense_grad[0], swap(dense_grad[1], "exp", 1)]).astype(bf16)
    dense_line = add_up(
        [dense_half[0]] + [swap(dense_half[m // 2], "exp", m) for m in range(2, n_exp, 2)]
    ).astype(bf16)
    arrived, _ = lax.optimization_barrier((arrived, dense_line))
    dense_mine = add_up(
        [dense_line[0]] + [swap(dense_line[j], "tp", j) for j in range(1, n_tp)]
    )
    small_grad = dense_mine[shard_rows - 8 :].reshape(-1)[: small_state.shape[1]]
    dense_mine = dense_mine[: shard_rows - 8].reshape(-1)[:shard]
    if slice_ff % LANES == 0:
        grad_gate_up, grad_down = unpack(add_up(arrived[0]))
    else:
        grad_gate_up, grad_down = add_up(arrived[0]), add_up(arrived[1])
    grad_gate_up, grad_down = grad_gate_up[None], grad_down[None]

    step_value = step_count[0].astype(f32)
    dense_new = adamw_update(dense_state, dense_mine, rate_dense, weight_decay, step_value)
    gate_up_new = adamw_update(gate_up_state, grad_gate_up, rate_expert, weight_decay, step_value)
    down_new = adamw_update(down_state, grad_down, rate_expert, weight_decay, step_value)
    small_new = adamw_update(small_state, small_grad, rate_small, 0.0, step_value)
    return (
        block_out,
        grad_in,
        dense_new,
        dense_new[0].astype(bf16),
        gate_up_new,
        gate_up_new[0].astype(bf16),
        down_new,
        down_new[0].astype(bf16),
        small_new,
    )


def solution(mesh):
    in_specs = (
        P(("exp", "tp"), None),
        P(("exp", "tp"), None),
        P(("exp", "tp"), None),
        P(("exp", "tp"), None),
        P(("exp", "tp"), None),
        P(("exp", "tp"), None),
        P(),
        P(None, ("exp", "tp")),
        P(None, "exp", None, None, "tp"),
        P(None, "exp", "tp", None),
        P(),
    )
    out_specs = (
        P(("exp", "tp"), None),
        P(("exp", "tp"), None),
        P(None, ("exp", "tp")),
        P(("exp", "tp")),
        P(None, "exp", None, None, "tp"),
        P("exp", None, None, "tp"),
        P(None, "exp", "tp", None),
        P("exp", "tp", None),
        P(),
    )
    return jax.shard_map(local, mesh=mesh, in_specs=in_specs, out_specs=out_specs, check_vma=False)
```

```python
from functools import partial
import math

import jax
import jax.numpy as jnp
from jax import lax
from jax.experimental import pallas as pl
from jax.experimental.pallas import tpu as pltpu
from jax.sharding import PartitionSpec as P

D = 384
HEADS = 6
HD = 64
PAIRS = HEADS // 2
TOP = 2
SEQ = 1024
LANES = 128
QB = 128
CH = 256
NBLK = SEQ // QB
WIN = 128
SLOT = 256
XW = 2 * D + LANES
SEG_IDS = 8
VAR_IDS = 4
BIAS_END = SEG_IDS + 6 * VAR_IDS
SUM_LANE = 36
WIN_LANE = 64
FAR = 2.0**100

norm_epsilon = 1e-06
moment_rate = 0.5
average_rate = 0.9
adam_epsilon = 1e-08
weight_decay = 0.1
rate_dense = 0.05
rate_expert = 0.04
rate_small = 0.2

bf16 = jnp.bfloat16
f32 = jnp.float32


def mm(left, right):
    return lax.dot_general(left, right, (((1,), (0,)), ((), ())), preferred_element_type=f32)


def mm_nt(left, right):
    return lax.dot_general(left, right, (((1,), (1,)), ((), ())), preferred_element_type=f32)


def mm_tn(left, right):
    return lax.dot_general(left, right, (((0,), (0,)), ((), ())), preferred_element_type=f32)


def lane_ids(shape):
    return lax.broadcasted_iota(jnp.int32, shape, len(shape) - 1)


def row_ids(shape):
    return lax.broadcasted_iota(jnp.int32, shape, 0)


def three_pieces(value):
    high = value.astype(bf16)
    rest = value - high.astype(f32)
    middle = rest.astype(bf16)
    low = (rest - middle.astype(f32)).astype(bf16)
    return high.astype(f32), middle.astype(f32), low.astype(f32)


def own_summand(value):
    high, middle, low = three_pieces(value)
    lane = lane_ids(value.shape) % HD
    return jnp.where(
        lane == SUM_LANE,
        high,
        jnp.where(lane == SUM_LANE + 1, middle, jnp.where(lane == SUM_LANE + 2, low, 0.0)),
    ).astype(bf16)


def half_masks():
    lane = lane_ids((1, LANES))
    return [jnp.where(mask, 1.0, 0.0).astype(bf16) for mask in (lane < HD, lane >= HD)]


def swap_halves(values):
    lane = lane_ids(values.shape)
    return jnp.where(
        lane % HD < HD // 2,
        pltpu.roll(values, LANES - HD // 2, 1),
        pltpu.roll(values, HD // 2, 1),
    )


def call(kernel, mib, **kwargs):
    return pl.pallas_call(
        kernel,
        compiler_params=pltpu.CompilerParams(
            vmem_limit_bytes=mib * 1024 * 1024, dimension_semantics=("arbitrary",)
        ),
        **kwargs,
    )


def whole(shape):
    return pl.BlockSpec(shape, lambda *_: (0,) * len(shape))


def resident(count):
    return [pl.BlockSpec(memory_space=pltpu.VMEM)] * count


def cost(flops, moved):
    return pl.CostEstimate(flops=int(flops), transcendentals=0, bytes_accessed=int(moved))


def unpack_kernel(place, here, there, in_out, out_out, router_out, flat, spread, *, shard, experts, n_tp):
    rows = here.shape[1]
    n_dev = 2 * here.shape[0]
    flat[...] = jnp.zeros(flat.shape, f32)
    lane = lane_ids((rows, LANES))
    odd = place[0] % 2 == 1
    for s in range(n_dev):
        exp = s // n_tp
        rel = lax.bitwise_xor(exp // 2, place[0] // 2) * n_tp + lax.bitwise_xor(s % n_tp, place[1])
        start, off = divmod(shard * s, LANES)
        one, other = here[rel].astype(f32), there[rel].astype(f32)
        piece = jnp.where(odd, other, one) if exp % 2 == 0 else jnp.where(odd, one, other)
        if off:
            piece = pltpu.roll(piece, off, 1)
            flat[start : start + rows] += jnp.where(lane >= off, piece, 0.0)
            flat[start + 1 : start + 1 + rows] += jnp.where(lane < off, piece, 0.0)
        else:
            flat[start : start + rows] += piece
    for j in range(9):
        in_out[:, j * LANES : (j + 1) * LANES] = flat[pl.ds(j, D, stride=9), :].astype(bf16)
    for j in range(3):
        out_out[:, j * LANES : (j + 1) * LANES] = flat[pl.ds(9 * D + j, D, stride=3), :].astype(bf16)
    share = LANES // experts
    count = D // share
    for i in range(share):
        spread[pl.ds(i, count, stride=share), :] = flat[12 * D : 12 * D + count, :]
    lanes = lane_ids((D, LANES))
    kept = jnp.where(lanes // experts == row_ids((D, LANES)) % share, spread[...], 0.0).astype(bf16)
    fold_lane = lane_ids((LANES, LANES))
    fold = (row_ids((LANES, LANES)) % experts == lax.bitwise_xor(fold_lane, place[0])) & (
        fold_lane < experts
    )
    router_out[...] = mm(kept, jnp.where(fold, 1.0, 0.0).astype(bf16)).astype(bf16)


def unpack_dense(place, here, there, shard, experts, n_tp):
    total = shard * 2 * here.shape[0] // LANES
    flat_rows = total + here.shape[1] + 8
    return call(
        partial(unpack_kernel, shard=shard, experts=experts, n_tp=n_tp),
        6,
        grid_spec=pltpu.PrefetchScalarGridSpec(
            num_scalar_prefetch=1,
            grid=(1,),
            in_specs=resident(2),
            out_specs=resident(3),
            scratch_shapes=[pltpu.VMEM((flat_rows, LANES), f32), pltpu.VMEM((D, LANES), f32)],
        ),
        out_shape=[
            jax.ShapeDtypeStruct((D, 3 * D), bf16),
            jax.ShapeDtypeStruct((D, D), bf16),
            jax.ShapeDtypeStruct((D, LANES), bf16),
        ],
        cost_estimate=cost(1e8, 4e6),
        name="unpack_dense",
    )(place, here, there)


def key_features(marks):
    lane = lane_ids(marks.shape)
    flip = (lane < SEG_IDS) | ((lane >= SEG_IDS + 3 * VAR_IDS) & (lane < BIAS_END))
    return jnp.where(flip, 1.0 - marks, marks)


def in_windows(win, row, first, count, step):
    need = win[row, 2 * first + 1]
    for i in range(1, count):
        need = jnp.maximum(need, win[row, 2 * (first + i) + 1])

    def run(keys):
        for i in range(count):
            low = win[row, 2 * (first + i)]
            step(first + i, pl.multiple_of(jnp.minimum(low, SEQ - keys), 16), keys)

    for blocks in (2, 3, 4, 5):
        fits = need <= 2 if blocks == 2 else need == blocks
        pl.when(fits)(partial(run, blocks * QB))
    pl.when(need > 5)(partial(run, SEQ))


def prepare_kernel(
    place, routes, segs, vars_, positions, small,
    lanes_out, rows_out, table_out, win_out, marks_out, cos_out, sin_out, biases_out, *, experts,
):
    tok = routes.shape[1]
    blocks = tok // CH
    above = jnp.where(row_ids((CH, CH)) < lane_ids((CH, CH)), 1.0, 0.0).astype(bf16)
    base = jnp.zeros((experts, 1), f32)
    lane = lane_ids((experts, LANES))
    table = jnp.zeros((experts, LANES), f32)
    rel = lax.bitwise_xor(row_ids((experts, CH)), place[0])
    fill = jnp.full((LANES - experts, CH), -1.0, f32)
    for b in range(blocks):
        at = slice(b * CH, (b + 1) * CH)
        named = (routes[0:1, at] == rel) | (routes[1:2, at] == rel)
        ones = jnp.where(named, 1.0, 0.0)
        rank = mm(ones.astype(bf16), above)
        odd = base - 16.0 * jnp.floor(base * (1.0 / 16.0))
        spot = jnp.where(named, rank + odd, -1.0)
        lanes_out[:, at] = spot
        rows_out[at, :] = jnp.concatenate([spot, fill], axis=0).T
        count = jnp.sum(ones, axis=1, keepdims=True)
        windows = jnp.floor((odd + count) * (1.0 / WIN)) + 1.0
        table = jnp.where(lane == b, base - odd, jnp.where(lane == WIN_LANE + b, windows, table))
        base = base + count
    steps = jnp.floor((base + (SLOT - 1)) * (1.0 / SLOT))
    table_out[...] = jnp.where(lane == 2 * WIN_LANE - 1, steps, table).astype(jnp.int32)

    identity = jnp.where(row_ids((LANES, LANES)) == lane_ids((LANES, LANES)), 1.0, 0.0).astype(bf16)
    feature = row_ids((LANES, SEQ))
    two = row_ids((8, SEQ))
    spread = jnp.where(row_ids((8, LANES)) < 2, 1.0, 0.0).astype(bf16)
    lane = lane_ids((1, LANES))
    frequency = jnp.exp(
        (lane % (HD // 2)).astype(f32) * (-2.0 * math.log(10000.0) / HD)
    )
    sign = jnp.where(lane % HD < HD // 2, -1.0, 1.0)
    win = jnp.zeros(win_out.shape, f32)
    win_row, win_lane = row_ids(win_out.shape), lane_ids(win_out.shape)
    for i in range(segs.shape[0]):
        at = slice(i * SEQ, (i + 1) * SEQ)
        seg, var = segs[i : i + 1, :], vars_[i : i + 1, :]
        marks = jnp.where(
            feature < SEG_IDS,
            jnp.where(seg == feature, 1.0, 0.0),
            jnp.where(
                feature < BIAS_END,
                jnp.where(var == feature % VAR_IDS, 1.0, 0.0),
                jnp.where(
                    (feature % HD >= SUM_LANE) & (feature % HD < SUM_LANE + 3), 1.0, 0.0
                ),
            ),
        ).astype(bf16)
        marks_out[at, :] = mm_tn(marks, identity).astype(bf16)
        place_in_time = positions[i : i + 1, :]
        low = lax.bitwise_and(place_in_time, 31)
        halves = jnp.where(
            two == 0, (place_in_time - low).astype(f32), jnp.where(two == 1, low.astype(f32), 0.0)
        ).astype(bf16)
        angles = mm_tn(halves, spread) * frequency
        cos_out[at, :] = jnp.cos(angles)
        sin_out[at, :] = jnp.sin(angles) * sign
        for q in range(NBLK):
            head_id, tail_id = seg[:, q * QB : q * QB + 1], seg[:, (q + 1) * QB - 1 : (q + 1) * QB]
            first = jnp.sum(jnp.where(seg < head_id, 1.0, 0.0), axis=1, keepdims=True)
            last = jnp.sum(jnp.where(seg <= tail_id, 1.0, 0.0), axis=1, keepdims=True)
            first = 16.0 * jnp.floor(first * (1.0 / 16.0))
            keys = jnp.floor((last - first + (QB - 1)) * (1.0 / QB))
            win = jnp.where(
                (win_row == i) & (win_lane == 2 * q),
                first,
                jnp.where((win_row == i) & (win_lane == 2 * q + 1), keys, win),
            )
    win_out[...] = win.astype(jnp.int32)

    shape = (8, LANES)
    head, lanes = row_ids(shape), lane_ids(shape)
    bias = jnp.broadcast_to(small[0:1, 2 * D : 2 * D + 2 * HEADS], (8, 2 * HEADS))
    bias_row, bias_lane = row_ids(bias.shape), lane_ids(bias.shape)
    filled = jnp.where(lanes < SEG_IDS, -FAR, 0.0)
    for kind in range(2):
        own = jnp.sum(
            jnp.where(bias_lane == kind * HEADS + bias_row, bias, 0.0), axis=1, keepdims=True
        )
        for i, piece in enumerate(three_pieces(own)):
            first = SEG_IDS + (3 * kind + i) * VAR_IDS
            filled = jnp.where((lanes >= first) & (lanes < first + VAR_IDS), piece, filled)
    biases_out[...] = jnp.where(head < HEADS, filled, 0.0)


def prepare(place, routes, segs, vars_, positions, small, experts):
    tok = routes.shape[1]
    seqs = segs.shape[0]
    shapes = [
        ((experts, tok), f32), ((tok, LANES), f32), ((experts, LANES), jnp.int32),
        ((-(-seqs // 8) * 8, LANES), jnp.int32), ((tok, LANES), bf16), ((tok, LANES), f32),
        ((tok, LANES), f32), ((8, LANES), f32),
    ]
    return call(
        partial(prepare_kernel, experts=experts),
        8,
        grid_spec=pltpu.PrefetchScalarGridSpec(
            num_scalar_prefetch=1,
            grid=(1,),
            in_specs=resident(5),
            out_specs=resident(len(shapes)),
        ),
        out_shape=[jax.ShapeDtypeStruct(shape, dtype) for shape, dtype in shapes],
        cost_estimate=cost(1e9, 8e6),
        name="prepare",
    )(place, routes, segs, vars_, positions, small)


def row_views(refs, row):
    at = pl.ds(pl.multiple_of(row * SEQ, SEQ), SEQ)
    return [ref.at[at, :] for ref in refs]


def forward_kernel(win, *refs, experts):
    arrays, fixed, outs, scratch = refs[:6], refs[6:11], refs[11:19], refs[19:]

    def one(row, carry):
        forward_row(
            row, win, *row_views(arrays, row), *fixed, *row_views(outs, row), *scratch, experts=experts
        )
        return carry

    lax.fori_loop(0, arrays[0].shape[0] // SEQ, one, 0)


def forward_row(
    row, win, tokens, cot, cos_ref, sin_ref, marks_ref, place_rows, small, biases,
    in_proj, out_proj, router,
    q_out, k_out, v_out, lse_out, mixed_out, middle_out, rows_out, probs_out,
    keys_aug, values_aug, totals, tops, sums_out, *, experts,
):
    masks = half_masks()
    bias_low = biases[...].astype(bf16)
    gain_one, gain_two = small[0:1, :D], small[0:1, D : 2 * D]
    for p in range(PAIRS):
        values_aug[p, :, LANES:] = jnp.ones((SEQ, LANES), bf16)

    def project(c, carry):
        at = pl.ds(pl.multiple_of(c * CH, CH), CH)
        x = tokens[at, :].astype(f32)
        factor = lax.rsqrt(jnp.mean(x * x, axis=-1, keepdims=True) + norm_epsilon)
        normed = (x * factor * gain_one).astype(bf16)
        projected = mm(normed, in_proj[...])
        cosine, sine = cos_ref[at, :], sin_ref[at, :]
        features = key_features(marks_ref[at, :].astype(f32)).astype(bf16)
        for j in range(2 * PAIRS):
            part = projected[:, j * LANES : (j + 1) * LANES]
            turned = part * cosine + swap_halves(part) * sine
            if j < PAIRS:
                turned = turned.astype(bf16) * jnp.asarray(HD**-0.5, bf16)
                q_out[at, j * LANES : (j + 1) * LANES] = turned
            else:
                p = j - PAIRS
                turned = turned.astype(bf16)
                k_out[at, p * LANES : (p + 1) * LANES] = turned
                keys_aug[p, at, :LANES] = turned
                keys_aug[p, at, LANES:] = features
        for p in range(PAIRS):
            part = projected[:, 2 * D + p * LANES : 2 * D + (p + 1) * LANES].astype(bf16)
            v_out[at, p * LANES : (p + 1) * LANES] = part
            values_aug[p, at, :LANES] = part
        return carry

    lax.fori_loop(0, SEQ // CH, project, 0)

    lane = lane_ids((QB, LANES))

    def attend(quad, carry):
        def step(block, key_start, keys):
            at = pl.ds(pl.multiple_of(block * QB, QB), QB)
            key_at = pl.ds(key_start, keys)
            marks = marks_ref[at, :]
            for p in range(PAIRS):
                cols = slice(p * LANES, (p + 1) * LANES)
                queries = q_out[at, cols]
                stacked = jnp.concatenate(
                    [
                        jnp.concatenate(
                            [queries * masks[i], marks * bias_low[2 * p + i : 2 * p + i + 1, :]], axis=1
                        )
                        for i in range(2)
                    ],
                    axis=0,
                )
                scores = mm_nt(stacked, keys_aug[p, key_at, :])
                top = jnp.max(scores, axis=1, keepdims=True)
                weights = jnp.exp(scores - top).astype(bf16)
                sums = mm(weights, values_aug[p, key_at, :])
                sums_out[at, cols] = jnp.where(lane < HD, sums[:QB, :LANES], sums[QB:, :LANES])
                totals[at, cols] = jnp.where(lane < HD, sums[:QB, LANES:], sums[QB:, LANES:])
                tops[at, cols] = jnp.where(lane < HD, top[:QB], top[QB:])

        in_windows(win, row, 4 * quad, 4, step)
        return carry

    lax.fori_loop(0, NBLK // 4, attend, 0)

    def finish(c, carry):
        at = pl.ds(pl.multiple_of(c * CH, CH), CH)
        for p in range(PAIRS):
            cols = slice(p * LANES, (p + 1) * LANES)
            total = totals[at, cols]
            mixed_out[at, cols] = (sums_out[at, cols] / total).astype(bf16)
            lse_out[at, cols] = own_summand(-(tops[at, cols] + jnp.log(total)))
        middle = tokens[at, :].astype(f32) + mm(mixed_out[at, :], out_proj[...])
        middle_out[at, :] = middle
        factor = lax.rsqrt(jnp.mean(middle * middle, axis=-1, keepdims=True) + norm_epsilon)
        normed = (middle * factor * gain_two).astype(bf16)
        rows_out[at, :D] = normed
        rows_out[at, D : 2 * D] = cot[at, :]
        logits = mm(normed, router[...])
        named = place_rows[at, :] >= 0.0
        top = jnp.max(jnp.where(named, logits, -3.0e38), axis=1, keepdims=True)
        weights = jnp.where(named, jnp.exp(jnp.where(named, logits - top, 0.0)), 0.0)
        probs = weights / jnp.sum(weights, axis=1, keepdims=True)
        probs_out[at, :] = probs
        high, mid, low = three_pieces(probs)
        rows_out[at, 2 * D :] = (
            high + pltpu.roll(mid, experts, 1) + pltpu.roll(low, 2 * experts, 1)
        ).astype(bf16)
        return carry

    lax.fori_loop(0, SEQ // CH, finish, 0)


def forward(win, tokens, cot, cosine, sine, marks, place_rows, small, biases, weights, experts):
    tok = tokens.shape[0]
    return call(
        partial(forward_kernel, experts=experts),
        12,
        grid_spec=pltpu.PrefetchScalarGridSpec(
            num_scalar_prefetch=1,
            grid=(1,),
            in_specs=resident(11),
            out_specs=resident(8),
            scratch_shapes=[
                pltpu.VMEM((PAIRS, SEQ, 2 * LANES), bf16),
                pltpu.VMEM((PAIRS, SEQ, 2 * LANES), bf16),
                pltpu.VMEM((SEQ, D), f32),
                pltpu.VMEM((SEQ, D), f32),
                pltpu.VMEM((SEQ, D), f32),
            ],
        ),
        out_shape=[
            jax.ShapeDtypeStruct((tok, D), bf16),
            jax.ShapeDtypeStruct((tok, D), bf16),
            jax.ShapeDtypeStruct((tok, D), bf16),
            jax.ShapeDtypeStruct((tok, D), bf16),
            jax.ShapeDtypeStruct((tok, D), bf16),
            jax.ShapeDtypeStruct((tok, D), f32),
            jax.ShapeDtypeStruct((tok, XW), bf16),
            jax.ShapeDtypeStruct((tok, LANES), f32),
        ],
        cost_estimate=cost(2e10, 2e7),
        name="attention_forward",
    )(win, tokens, cot, cosine, sine, marks, place_rows, small, biases, *weights)


def experts_kernel(table, *refs, group, experts, blocks, chained):
    size = len(group)
    weights_hbm = refs[:size]
    rows, place_lanes, place_rows = refs[size : size + 3]
    earlier = refs[size + 3 : size + 3 + chained]
    part_out, *grads_hbm = refs[size + 3 + chained : 2 * size + 4 + chained]
    slots, weights, grads, grad_in, grad_down, total, in_sems, out_sems = refs[
        2 * size + 4 + chained :
    ]
    ff = grad_down.shape[0]
    cuts = ff // LANES
    arrivals = [
        pltpu.make_async_copy(weights_hbm[g], weights.at[g % 2], in_sems.at[g]) for g in range(size)
    ]
    departures = [
        pltpu.make_async_copy(grads.at[g % 2], grads_hbm[g], out_sems.at[g]) for g in range(size)
    ]
    for copy in arrivals[:2]:
        copy.start()

    def first_slot(block, r):
        return pl.multiple_of(table[r, block], 16)

    for g in range(size):
        slots[g, 0:16, :] = jnp.zeros((16, XW), bf16)

    def gather(block, carry):
        at = pl.ds(pl.multiple_of(block * CH, CH), CH)
        source = rows[at, :]
        slot = row_ids((WIN, CH)).astype(f32)

        def picks(r, first):
            return jnp.where(place_lanes[r : r + 1, at] - first == slot, 1.0, 0.0).astype(bf16)

        moved = mm(jnp.concatenate([picks(r, 0.0) for r in group], axis=0), source).astype(bf16)
        for g, r in enumerate(group):
            start = first_slot(block, r)
            slots[g, pl.ds(start, 16), :] += moved[g * WIN : g * WIN + 16]
            slots[g, pl.ds(start + 16, WIN - 16), :] = moved[g * WIN + 16 : (g + 1) * WIN]

            def more(w, inner, g=g, r=r, start=start):
                slots[g, pl.ds(start + w * WIN, WIN), :] = mm(
                    picks(r, (w * WIN).astype(f32)), source
                ).astype(bf16)
                return inner

            lax.fori_loop(1, table[r, WIN_LANE + block], more, 0)
        return carry

    lax.fori_loop(0, blocks, gather, 0)

    for g, r in enumerate(group):
        end = first_slot(blocks - 1, r) + table[r, WIN_LANE + blocks - 1] * WIN
        slots[g, pl.ds(end, SLOT), :] = jnp.zeros((SLOT, XW), bf16)
        arrivals[g].wait()
        gate_w = jnp.concatenate([weights[g % 2, z, :D, :] for z in range(cuts)], axis=1)
        up_w = jnp.concatenate([weights[g % 2, z, D : 2 * D, :] for z in range(cuts)], axis=1)
        down_w = jnp.concatenate(
            [
                jnp.concatenate(
                    [weights[g % 2, z, (6 + j) * LANES : (7 + j) * LANES, :] for j in range(3)], axis=1
                )
                for z in range(cuts)
            ],
            axis=0,
        )
        grad_in[...] = jnp.zeros(grad_in.shape, f32)
        grad_down[...] = jnp.zeros(grad_down.shape, f32)

        def step(i, carry, g=g, r=r, gate_w=gate_w, up_w=up_w, down_w=down_w):
            at = pl.ds(pl.multiple_of(i * SLOT, SLOT), SLOT)
            x = slots[g, at, :D]
            cot = slots[g, at, D : 2 * D].astype(f32)
            parts = slots[g, at, 2 * D :].astype(f32)
            prob = (
                parts[:, r : r + 1]
                + parts[:, experts + r : experts + r + 1]
                + parts[:, 2 * experts + r : 2 * experts + r + 1]
            )
            gate_pre = mm(x, gate_w)
            up_pre = mm(x, up_w)
            sigmoid = 1.0 / (1.0 + jnp.exp(-gate_pre))
            silu = gate_pre * sigmoid
            hidden = (silu * up_pre).astype(bf16)
            result = mm(hidden, down_w).astype(bf16).astype(f32)
            grad_result = (prob * cot).astype(bf16)
            grad_hidden = mm_nt(grad_result, down_w)
            grad_gate = (
                grad_hidden * up_pre * sigmoid * (1.0 + gate_pre * (1.0 - sigmoid))
            ).astype(bf16)
            grad_up = (grad_hidden * silu).astype(bf16)
            grad_rows = mm_nt(grad_gate, gate_w) + mm_nt(grad_up, up_w)
            grad_in[:, :ff] += mm_tn(x, grad_gate)
            grad_in[:, ff:] += mm_tn(x, grad_up)
            grad_down[...] += mm_tn(hidden, grad_result)
            score = jnp.sum(cot * result, axis=1, keepdims=True)
            high, mid, _ = three_pieces(jnp.broadcast_to(score, (SLOT, LANES)))
            lane = lane_ids((SLOT, LANES))
            slots[g, at, :D] = (prob * result).astype(bf16)
            slots[g, at, D : 2 * D] = grad_rows.astype(bf16)
            slots[g, at, 2 * D :] = jnp.where(
                lane == r, high, jnp.where(lane == experts + r, mid, 0.0)
            ).astype(bf16)
            return carry

        lax.fori_loop(0, table[r, 2 * WIN_LANE - 1], step, 0)
        if g + 2 < size:
            arrivals[g + 2].start()
        if g >= 2:
            departures[g - 2].wait()
        for z in range(cuts):
            cols = slice(z * LANES, (z + 1) * LANES)
            grads[g % 2, z, :D, :] = grad_in[:, cols].astype(bf16)
            grads[g % 2, z, D : 2 * D, :] = grad_in[:, ff + z * LANES : ff + (z + 1) * LANES].astype(bf16)
            for j in range(3):
                grads[g % 2, z, (6 + j) * LANES : (7 + j) * LANES, :] = grad_down[
                    cols, j * LANES : (j + 1) * LANES
                ].astype(bf16)
        departures[g].start()

    def scatter(block, carry):
        at = pl.ds(pl.multiple_of(block * CH, CH), CH)
        places = place_rows[at, :]
        slot = lane_ids((CH, WIN)).astype(f32)

        def picks(r, first):
            return jnp.where(places[:, r : r + 1] - first == slot, 1.0, 0.0).astype(bf16)

        source = jnp.concatenate(
            [slots[g, pl.ds(first_slot(block, r), WIN), :] for g, r in enumerate(group)], axis=0
        )
        total[...] = mm(jnp.concatenate([picks(r, 0.0) for r in group], axis=1), source)
        for g, r in enumerate(group):

            def more(w, inner, g=g, r=r):
                total[...] += mm(
                    picks(r, (w * WIN).astype(f32)),
                    slots[g, pl.ds(first_slot(block, r) + w * WIN, WIN), :],
                )
                return inner

            lax.fori_loop(1, table[r, WIN_LANE + block], more, 0)
        result = total[...]
        for ref in earlier:
            result = result + ref[at, :].astype(f32)
        part_out[at, :] = result.astype(bf16)
        return carry

    lax.fori_loop(0, blocks, scatter, 0)
    for copy in departures[-2:]:
        copy.wait()


def run_experts(table, weights, rows, place_lanes, place_rows, earlier, group, experts, cap):
    tok = rows.shape[0]
    ff = weights[0].shape[0] * LANES
    blocks = tok // CH
    shape = weights[0].shape
    size = len(group)
    there = [pl.BlockSpec(memory_space=pltpu.HBM)] * size
    out = call(
        partial(
            experts_kernel, group=group, experts=experts, blocks=blocks, chained=len(earlier)
        ),
        11 + 5 * size // 2,
        grid_spec=pltpu.PrefetchScalarGridSpec(
            num_scalar_prefetch=1,
            grid=(1,),
            in_specs=there + resident(3 + len(earlier)),
            out_specs=resident(1) + there,
            scratch_shapes=[
                pltpu.VMEM((size, cap + WIN + SLOT, XW), bf16),
                pltpu.VMEM((2, *shape), bf16),
                pltpu.VMEM((2, *shape), bf16),
                pltpu.VMEM((D, 2 * ff), f32),
                pltpu.VMEM((ff, D), f32),
                pltpu.VMEM((CH, XW), f32),
                pltpu.SemaphoreType.DMA((size,)),
                pltpu.SemaphoreType.DMA((size,)),
            ],
        ),
        out_shape=[jax.ShapeDtypeStruct((tok, XW), bf16)] + [jax.ShapeDtypeStruct(shape, bf16)] * size,
        cost_estimate=cost(4e9 * size, 3e6 * size + 8e6),
        name="experts",
    )(table, *weights, rows, place_lanes, place_rows, *earlier)
    return out[0], out[1:]


def backward_kernel(win, place, *refs, experts, n_tp, shard):
    arrays, fixed, outs, dense_out = refs[:13], refs[13:18], refs[18:20], refs[20]
    scratch = refs[21:]
    grad_in_proj, grad_out_proj, grad_router, flat, gain_out, bias_out = scratch[-6:]
    for ref in (grad_in_proj, grad_out_proj, grad_router, gain_out, bias_out):
        ref[...] = jnp.zeros(ref.shape, f32)

    def one(row, carry):
        backward_row(
            row, win, place, *row_views(arrays, row), *fixed, *row_views(outs, row), *scratch,
            experts=experts,
        )
        return carry

    lax.fori_loop(0, arrays[0].shape[0] // SEQ, one, 0)
    backward_flush(
        place, dense_out, grad_in_proj, grad_out_proj, grad_router, flat, gain_out, bias_out,
        experts=experts, n_tp=n_tp, shard=shard,
    )


def backward_row(
    row, win, place,
    part_ref, tokens, cot_ref, probs_ref, middle_ref, mixed_ref, q_ref, k_ref, v_ref, lse_ref, marks_ref,
    cos_ref, sin_ref, small, biases, in_proj, out_proj, router,
    block_out, grad_in_out,
    grad_middle, grad_mixed, inner_ref, keys_aug, values_aug, grad_q, grad_k, grad_v,
    grad_in_proj, grad_out_proj, grad_router, flat, gain_out, bias_out, *, experts,
):
    masks = half_masks()
    bias_low = biases[...].astype(bf16)
    pair_sum = jnp.where(
        (row_ids((2 * LANES, LANES)) % LANES < HD) == (lane_ids((2 * LANES, LANES)) < HD), 1.0, 0.0
    ).astype(bf16)
    gain_one, gain_two = small[0:1, :D], small[0:1, D : 2 * D]
    fold_row, fold_lane = row_ids((LANES, LANES)), lane_ids((LANES, LANES))
    tile = jnp.where(
        (lax.bitwise_xor(fold_row, place[0]) == fold_lane % experts) & (fold_row < experts), 1.0, 0.0
    ).astype(bf16)

    def head(c, carry):
        at = pl.ds(pl.multiple_of(c * CH, CH), CH)
        back = part_ref[at, :].astype(f32)
        middle = middle_ref[at, :]
        block_out[at, :] = (middle + back[:, :D]).astype(bf16)
        scores = back[:, 2 * D :]
        scores = scores + pltpu.roll(scores, LANES - experts, 1)
        probs = probs_ref[at, :]
        inner = jnp.sum(probs * scores, axis=1, keepdims=True)
        grad_logits = (probs * (scores - inner)).astype(bf16)
        grad_normed = mm_nt(grad_logits, router[...]) + back[:, D : 2 * D]
        factor = lax.rsqrt(jnp.mean(middle * middle, axis=-1, keepdims=True) + norm_epsilon)
        normed = (middle * factor * gain_two).astype(bf16)
        grad_router[...] += mm_tn(normed, mm(grad_logits, tile).astype(bf16))
        weighted = grad_normed * gain_two
        gain_out[1:2, :] += jnp.sum(grad_normed * middle * factor, axis=0, keepdims=True)
        cot = cot_ref[at, :].astype(f32)
        grad = (
            cot
            + factor * weighted
            - middle
            * (factor * factor * factor)
            * jnp.mean(weighted * middle, axis=-1, keepdims=True)
        )
        grad_middle[at, :] = grad
        branch = grad.astype(bf16)
        grad_out_proj[...] += mm_tn(mixed_ref[at, :], branch)
        mixed_grad = mm_nt(branch, out_proj[...]).astype(bf16)
        grad_mixed[at, :] = mixed_grad
        features = key_features(marks_ref[at, :].astype(f32)).astype(bf16)
        for p in range(PAIRS):
            cols = slice(p * LANES, (p + 1) * LANES)
            product = mixed_grad[:, cols].astype(f32) * mixed_ref[at, cols].astype(f32)
            high, mid, _ = three_pieces(product)
            inner = mm(jnp.concatenate([high, mid], axis=1).astype(bf16), pair_sum)
            inner_ref[at, cols] = own_summand(-inner)
            keys_aug[p, at, :LANES] = k_ref[at, cols]
            keys_aug[p, at, LANES:] = features
            values_aug[p, at, :LANES] = v_ref[at, cols]
            values_aug[p, at, LANES:] = features
        return carry

    lax.fori_loop(0, SEQ // CH, head, 0)
    grad_k[...] = jnp.zeros(grad_k.shape, f32)
    grad_v[...] = jnp.zeros(grad_v.shape, f32)

    lane = lane_ids((QB, LANES))

    def attend(couple, carry):
        def step(block, key_start, keys):
            at = pl.ds(pl.multiple_of(block * QB, QB), QB)
            marks = marks_ref[at, :]
            key_at = pl.ds(key_start, keys)
            for p in range(PAIRS):
                cols = slice(p * LANES, (p + 1) * LANES)
                queries, logs = q_ref[at, cols], lse_ref[at, cols]
                out_grad, inner = grad_mixed[at, cols], inner_ref[at, cols]
                stacked = jnp.concatenate(
                    [
                        jnp.concatenate(
                            [
                                queries * masks[i],
                                marks * bias_low[2 * p + i : 2 * p + i + 1, :] + logs * masks[i],
                            ],
                            axis=1,
                        )
                        for i in range(2)
                    ],
                    axis=0,
                )
                grads = jnp.concatenate(
                    [
                        jnp.concatenate([out_grad * masks[i], inner * masks[i]], axis=1)
                        for i in range(2)
                    ],
                    axis=0,
                )
                keys_here = keys_aug[p, key_at, :]
                probs = jnp.exp(mm_nt(keys_here, stacked))
                shifted = mm_nt(values_aug[p, key_at, :], grads)
                grad_scores = (probs * shifted).astype(bf16)
                grad_v[key_at, cols] += mm(probs.astype(bf16), grads[:, :LANES])
                grad_k[key_at, cols] += mm(grad_scores, stacked[:, :LANES])
                back = mm_tn(grad_scores, keys_here)
                grad_q[at, cols] = (
                    jnp.where(lane < HD, back[:QB, :LANES], back[QB:, :LANES]) * HD**-0.5
                )
                for i in range(2):
                    bias_out[2 * p + i] += jnp.sum(
                        (marks.astype(f32) * back[i * QB : (i + 1) * QB, LANES:]).reshape(QB // 8, 8, LANES),
                        axis=0,
                    )

        in_windows(win, row, 2 * couple, 2, step)
        return carry

    lax.fori_loop(0, NBLK // 2, attend, 0)

    def tail(c, carry):
        at = pl.ds(pl.multiple_of(c * CH, CH), CH)
        cosine, sine = cos_ref[at, :], sin_ref[at, :]
        pieces = []
        for ref in (grad_q, grad_k):
            for p in range(PAIRS):
                part = ref[at, p * LANES : (p + 1) * LANES]
                pieces.append((part * cosine - swap_halves(part) * sine).astype(bf16))
        pieces.append(grad_v[at, :].astype(bf16))
        grad_projected = jnp.concatenate(pieces, axis=1)
        x = tokens[at, :].astype(f32)
        factor = lax.rsqrt(jnp.mean(x * x, axis=-1, keepdims=True) + norm_epsilon)
        normed = (x * factor * gain_one).astype(bf16)
        grad_in_proj[...] += mm_tn(normed, grad_projected)
        grad_normed = mm_nt(grad_projected, in_proj[...])
        weighted = grad_normed * gain_one
        gain_out[0:1, :] += jnp.sum(grad_normed * x * factor, axis=0, keepdims=True)
        grad_in_out[at, :] = (
            grad_middle[at, :]
            + factor * weighted
            - x * (factor * factor * factor) * jnp.mean(weighted * x, axis=-1, keepdims=True)
        ).astype(bf16)
        return carry

    lax.fori_loop(0, SEQ // CH, tail, 0)


def backward_flush(
    place, dense_out, grad_in_proj, grad_out_proj, grad_router, flat, gain_out, bias_out,
    *, experts, n_tp, shard,
):
    for j in range(9):
        flat[pl.ds(j, D, stride=9), :] = grad_in_proj[:, j * LANES : (j + 1) * LANES]
    for j in range(3):
        flat[pl.ds(9 * D + j, D, stride=3), :] = grad_out_proj[:, j * LANES : (j + 1) * LANES]
    share = LANES // experts
    count = D // share
    lanes = lane_ids((D, LANES))
    grad_router[...] = jnp.where(
        lanes // experts == row_ids((D, LANES)) % share, grad_router[...], 0.0
    )
    merged = grad_router[pl.ds(0, count, stride=share), :]
    for i in range(1, share):
        merged = merged + grad_router[pl.ds(i, count, stride=share), :]
    flat[12 * D : 12 * D + count, :] = merged
    spare = flat.shape[0] - (12 * D + count)
    flat[12 * D + count :, :] = jnp.zeros((spare, LANES), f32)
    n_dev = dense_out.shape[0]
    rows = dense_out.shape[1]
    half = n_dev // 2
    piece_lane = lane_ids((rows, LANES))
    for s in range(n_dev):
        exp_rel = lax.bitwise_xor(s // n_tp, place[0])
        rel = (
            (exp_rel % 2) * half + (exp_rel // 2) * n_tp + lax.bitwise_xor(s % n_tp, place[1])
        )
        start, off = divmod(shard * s, LANES)
        piece = flat[start : start + rows, :]
        if off:
            piece = jnp.where(
                piece_lane < LANES - off,
                pltpu.roll(piece, LANES - off, 1),
                pltpu.roll(flat[start + 1 : start + 1 + rows, :], LANES - off, 1),
            )
        dense_out[rel] = piece.astype(bf16)
    shape = (8, LANES)
    bias_rows, bias_lanes = row_ids(shape), lane_ids(shape)
    sums = jnp.concatenate(
        [jnp.sum(bias_out[h], axis=0, keepdims=True) for h in range(HEADS)]
        + [jnp.zeros((8 - HEADS, LANES), f32)],
        axis=0,
    )
    extra = jnp.zeros((1, LANES), f32)
    for kind in range(2):
        first_lane = SEG_IDS + 3 * kind * VAR_IDS
        own = jnp.sum(
            jnp.where((bias_lanes >= first_lane) & (bias_lanes < first_lane + VAR_IDS), sums, 0.0),
            axis=1,
            keepdims=True,
        )
        extra = extra + jnp.sum(
            jnp.where((bias_lanes == bias_rows + kind * HEADS) & (bias_rows < HEADS), own, 0.0),
            axis=0,
            keepdims=True,
        )
    spare_rows = jnp.concatenate(
        [gain_out[i : i + 1, j * LANES : (j + 1) * LANES] for i in range(2) for j in range(3)]
        + [extra, jnp.zeros((1, LANES), f32)],
        axis=0,
    ).astype(bf16)
    for s in range(n_dev):
        dense_out[s, rows - 8 :, :] = spare_rows


def backward(win, place, part, tokens, cot, saved, marks, cosine, sine, small, biases, weights, sizes):
    experts, n_exp, n_tp, shard, shard_rows = sizes
    q, k, v, lse, mixed, middle, _, probs = saved
    tok = tokens.shape[0]

    flat_rows = shard * n_exp * n_tp // LANES + shard_rows + 8
    return call(
        partial(backward_kernel, experts=experts, n_tp=n_tp, shard=shard),
        22,
        grid_spec=pltpu.PrefetchScalarGridSpec(
            num_scalar_prefetch=2,
            grid=(1,),
            in_specs=resident(18),
            out_specs=resident(3),
            scratch_shapes=[
                pltpu.VMEM((SEQ, D), f32),
                pltpu.VMEM((SEQ, D), bf16),
                pltpu.VMEM((SEQ, D), bf16),
                pltpu.VMEM((PAIRS, SEQ, 2 * LANES), bf16),
                pltpu.VMEM((PAIRS, SEQ, 2 * LANES), bf16),
                pltpu.VMEM((SEQ, D), f32),
                pltpu.VMEM((SEQ, D), f32),
                pltpu.VMEM((SEQ, D), f32),
                pltpu.VMEM((D, 3 * D), f32),
                pltpu.VMEM((D, D), f32),
                pltpu.VMEM((D, LANES), f32),
                pltpu.VMEM((flat_rows, LANES), f32),
                pltpu.VMEM((8, D), f32),
                pltpu.VMEM((HEADS, 8, LANES), f32),
            ],
        ),
        out_shape=[
            jax.ShapeDtypeStruct((tok, D), bf16),
            jax.ShapeDtypeStruct((tok, D), bf16),
            jax.ShapeDtypeStruct((n_exp * n_tp, shard_rows, LANES), bf16),
        ],
        cost_estimate=cost(4e10, 3e7),
        name="attention_backward",
    )(
        win, place, part, tokens, cot, probs, middle, mixed, q, k, v, lse, marks,
        cosine, sine, small, biases, *weights,
    )


def swap(values, axis, mask):
    size = lax.axis_size(axis)
    return lax.ppermute(values, axis, [(i, i ^ mask) for i in range(size)])


def add_up(parts):
    parts = [part.astype(f32) for part in parts]
    while len(parts) > 1:
        parts = [sum(parts[i + 1 : i + 2], parts[i]) for i in range(0, len(parts), 2)]
    return parts[0]


def adamw_update(old_state, grad_value, rate, decay, step_value):
    moment_one = moment_rate * old_state[1] + (1.0 - moment_rate) * grad_value
    moment_two = moment_rate * old_state[2] + (1.0 - moment_rate) * grad_value * grad_value
    correction = 1.0 - jnp.power(moment_rate, step_value)
    master = old_state[0] - rate * (
        moment_one / correction / (jnp.sqrt(moment_two / correction) + adam_epsilon)
        + decay * old_state[0]
    )
    average = average_rate * old_state[3] + (1.0 - average_rate) * master
    return jnp.stack([master, moment_one, moment_two, average])


def local(
    tokens, cotangent, routes, segments, variates, positions, step_count,
    dense_state, gate_up_state, down_state, small_state,
):
    tok = tokens.shape[0]
    n_exp, n_tp = lax.axis_size("exp"), lax.axis_size("tp")
    experts = n_exp * gate_up_state.shape[1]
    cap = 2 * tok * TOP // experts
    my_exp, my_tp = lax.axis_index("exp"), lax.axis_index("tp")
    place = jnp.stack([my_exp, my_tp]).astype(jnp.int32)
    shard = dense_state.shape[1]
    shard_rows = -(-(-(-shard // LANES) + 8) // 16) * 16

    def in_line(values):
        return [values] + [swap(values, "tp", j) for j in range(1, n_tp)]

    def in_plane(values):
        return [values] + [swap(values, "exp", m) for m in range(2, n_exp, 2)]

    own = jnp.pad(dense_state[0].astype(bf16), (0, shard_rows * LANES - shard))
    line = jnp.concatenate(in_line(own.reshape(1, shard_rows, LANES)), axis=0)
    routes_later, _ = lax.optimization_barrier((routes.T, line))
    prepared = prepare(place, routes_later, segments, variates, positions, small_state, experts)
    here = jnp.concatenate(in_plane(line), axis=0)

    gate_up = gate_up_state[0, 0].astype(bf16)
    down = down_state[0, 0].astype(bf16)
    slice_ff = gate_up.shape[2]
    ff = slice_ff * n_tp
    cuts = ff // LANES

    def pack(gate_up, down):
        count = gate_up.shape[2] // LANES
        return jnp.concatenate(
            [
                gate_up.reshape(2 * D, count, LANES).transpose(1, 0, 2),
                down.reshape(count, LANES, 3, LANES).transpose(0, 2, 1, 3).reshape(count, D, LANES),
            ],
            axis=1,
        )

    def unpack(packed):
        count = packed.shape[0]
        return (
            packed[:, : 2 * D].transpose(1, 0, 2).reshape(2, D, count * LANES),
            packed[:, 2 * D :].reshape(count, 3, LANES, LANES).transpose(0, 2, 1, 3)
            .reshape(count * LANES, D),
        )

    if slice_ff % LANES == 0:
        packed = jnp.concatenate(in_line(pack(gate_up, down)), axis=0)
    else:
        packed = pack(
            jnp.concatenate(in_line(gate_up), axis=2), jnp.concatenate(in_line(down), axis=0)
        )
    here, packed, prepared = lax.optimization_barrier((here, packed, prepared))
    place_lanes, place_rows, table, win, marks, cosine, sine, biases = prepared
    there = swap(here, "exp", 1)
    weights = unpack_dense(place, here, there, shard, experts, n_tp)
    expert_weights = {2 * i: values for i, values in enumerate(in_plane(packed))}
    expert_weights[1] = swap(packed, "exp", 1)
    saved = forward(
        win, tokens, cotangent, cosine, sine, marks, place_rows, small_state, biases, weights, experts
    )
    routed = saved[6]
    groups = [(0, 1)] + [tuple(range(i, min(i + 4, n_exp))) for i in range(2, n_exp, 4)]
    chain, expert_grads = [], {}
    for group in groups:
        part, grads = run_experts(
            table, [expert_weights[r] for r in group], routed, place_lanes, place_rows, chain, group,
            experts, cap,
        )
        expert_grads.update(zip(group, grads))
        if not chain:
            for m in range(2, n_exp, 2):
                values, _ = lax.optimization_barrier((expert_weights[m], part))
                expert_weights[m + 1] = swap(values, "exp", 1)
        chain = [part]
    halves = [
        add_up([expert_grads[m], swap(expert_grads[m + 1], "exp", 1)]).astype(bf16)
        for m in range(0, n_exp, 2)
    ]
    part, halves = lax.optimization_barrier((part, halves))

    block_out, grad_in, dense_grad = backward(
        win, place, part, tokens, cotangent, saved, marks, cosine, sine, small_state, biases, weights,
        (experts, n_exp, n_tp, shard, shard_rows),
    )

    mine = add_up(
        [halves[0]] + [swap(halves[m // 2], "exp", m) for m in range(2, n_exp, 2)]
    ).astype(bf16)
    dense_grad, mine = lax.optimization_barrier((dense_grad, mine))
    if slice_ff % LANES == 0:
        mine = mine.reshape(n_tp, slice_ff // LANES, 3 * D, LANES)
        arrived = [[mine[0]] + [swap(mine[j], "tp", j) for j in range(1, n_tp)]]
    else:
        mine_in, mine_down = unpack(mine)
        mine_in = mine_in.reshape(2, D, n_tp, slice_ff)
        mine_down = mine_down.reshape(n_tp, slice_ff, D)
        arrived = [
            [mine_in[:, :, 0]] + [swap(mine_in[:, :, j], "tp", j) for j in range(1, n_tp)],
            [mine_down[0]] + [swap(mine_down[j], "tp", j) for j in range(1, n_tp)],
        ]

    dense_grad = dense_grad.reshape(2, n_exp // 2, n_tp, shard_rows, LANES)
    dense_half = add_up([dense_grad[0], swap(dense_grad[1], "exp", 1)]).astype(bf16)
    dense_line = add_up(
        [dense_half[0]] + [swap(dense_half[m // 2], "exp", m) for m in range(2, n_exp, 2)]
    ).astype(bf16)
    dense_parts = [dense_line[0]] + [swap(dense_line[j], "tp", j) for j in range(1, n_tp)]
    arrived, _ = lax.optimization_barrier((arrived, dense_parts[1]))
    dense_mine = add_up(dense_parts)
    small_grad = dense_mine[shard_rows - 8 :].reshape(-1)[: small_state.shape[1]]
    dense_mine = dense_mine[: shard_rows - 8].reshape(-1)[:shard]
    if slice_ff % LANES == 0:
        grad_gate_up, grad_down = unpack(add_up(arrived[0]))
    else:
        grad_gate_up, grad_down = add_up(arrived[0]), add_up(arrived[1])
    grad_gate_up, grad_down = grad_gate_up[None], grad_down[None]

    step_value = step_count[0].astype(f32)
    dense_new = adamw_update(dense_state, dense_mine, rate_dense, weight_decay, step_value)
    gate_up_new = adamw_update(gate_up_state, grad_gate_up, rate_expert, weight_decay, step_value)
    down_new = adamw_update(down_state, grad_down, rate_expert, weight_decay, step_value)
    small_new = adamw_update(small_state, small_grad, rate_small, 0.0, step_value)
    return (
        block_out,
        grad_in,
        dense_new,
        dense_new[0].astype(bf16),
        gate_up_new,
        gate_up_new[0].astype(bf16),
        down_new,
        down_new[0].astype(bf16),
        small_new,
    )


def solution(mesh):
    in_specs = (
        P(("exp", "tp"), None),
        P(("exp", "tp"), None),
        P(("exp", "tp"), None),
        P(("exp", "tp"), None),
        P(("exp", "tp"), None),
        P(("exp", "tp"), None),
        P(),
        P(None, ("exp", "tp")),
        P(None, "exp", None, None, "tp"),
        P(None, "exp", "tp", None),
        P(),
    )
    out_specs = (
        P(("exp", "tp"), None),
        P(("exp", "tp"), None),
        P(None, ("exp", "tp")),
        P(("exp", "tp")),
        P(None, "exp", None, None, "tp"),
        P("exp", None, None, "tp"),
        P(None, "exp", "tp", None),
        P("exp", "tp", None),
        P(),
    )
    return jax.shard_map(local, mesh=mesh, in_specs=in_specs, out_specs=out_specs, check_vma=False)
```

```python
from functools import partial
import math

import jax
import jax.numpy as jnp
from jax import lax
from jax.experimental import pallas as pl
from jax.experimental.pallas import tpu as pltpu
from jax.sharding import PartitionSpec as P

D = 384
HEADS = 6
HD = 64
PAIRS = HEADS // 2
TOP = 2
SEQ = 1024
LANES = 128
QB = 128
CH = 256
NBLK = SEQ // QB
WIN = 128
SLOT = 256
XW = 2 * D + LANES
SEG_IDS = 8
VAR_IDS = 4
BIAS_END = SEG_IDS + 6 * VAR_IDS
SUM_LANE = 36
WIN_LANE = 64
FAR = 2.0**100

norm_epsilon = 1e-06
moment_rate = 0.5
average_rate = 0.9
adam_epsilon = 1e-08
weight_decay = 0.1
rate_dense = 0.05
rate_expert = 0.04
rate_small = 0.2

bf16 = jnp.bfloat16
f32 = jnp.float32


def mm(left, right):
    return lax.dot_general(left, right, (((1,), (0,)), ((), ())), preferred_element_type=f32)


def mm_nt(left, right):
    return lax.dot_general(left, right, (((1,), (1,)), ((), ())), preferred_element_type=f32)


def mm_tn(left, right):
    return lax.dot_general(left, right, (((0,), (0,)), ((), ())), preferred_element_type=f32)


def lane_ids(shape):
    return lax.broadcasted_iota(jnp.int32, shape, len(shape) - 1)


def row_ids(shape):
    return lax.broadcasted_iota(jnp.int32, shape, 0)


def three_pieces(value):
    high = value.astype(bf16)
    rest = value - high.astype(f32)
    middle = rest.astype(bf16)
    low = (rest - middle.astype(f32)).astype(bf16)
    return high.astype(f32), middle.astype(f32), low.astype(f32)


def own_summand(value):
    high, middle, low = three_pieces(value)
    lane = lane_ids(value.shape) % HD
    return jnp.where(
        lane == SUM_LANE,
        high,
        jnp.where(lane == SUM_LANE + 1, middle, jnp.where(lane == SUM_LANE + 2, low, 0.0)),
    ).astype(bf16)


def half_masks():
    lane = lane_ids((1, LANES))
    return [jnp.where(mask, 1.0, 0.0).astype(bf16) for mask in (lane < HD, lane >= HD)]


def swap_halves(values):
    lane = lane_ids(values.shape)
    return jnp.where(
        lane % HD < HD // 2,
        pltpu.roll(values, LANES - HD // 2, 1),
        pltpu.roll(values, HD // 2, 1),
    )


def call(kernel, mib, **kwargs):
    return pl.pallas_call(
        kernel,
        compiler_params=pltpu.CompilerParams(
            vmem_limit_bytes=mib * 1024 * 1024, dimension_semantics=("arbitrary",)
        ),
        **kwargs,
    )


def whole(shape):
    return pl.BlockSpec(shape, lambda *_: (0,) * len(shape))


def resident(count):
    return [pl.BlockSpec(memory_space=pltpu.VMEM)] * count


def cost(flops, moved):
    return pl.CostEstimate(flops=int(flops), transcendentals=0, bytes_accessed=int(moved))


def unpack_kernel(place, here, there, in_out, out_out, router_out, flat, spread, *, shard, experts, n_tp):
    rows = here.shape[1]
    n_dev = 2 * here.shape[0]
    flat[...] = jnp.zeros(flat.shape, f32)
    lane = lane_ids((rows, LANES))
    odd = place[0] % 2 == 1
    for s in range(n_dev):
        exp = s // n_tp
        rel = lax.bitwise_xor(exp // 2, place[0] // 2) * n_tp + lax.bitwise_xor(s % n_tp, place[1])
        start, off = divmod(shard * s, LANES)
        one, other = here[rel].astype(f32), there[rel].astype(f32)
        piece = jnp.where(odd, other, one) if exp % 2 == 0 else jnp.where(odd, one, other)
        if off:
            piece = pltpu.roll(piece, off, 1)
            flat[start : start + rows] += jnp.where(lane >= off, piece, 0.0)
            flat[start + 1 : start + 1 + rows] += jnp.where(lane < off, piece, 0.0)
        else:
            flat[start : start + rows] += piece
    for j in range(9):
        in_out[:, j * LANES : (j + 1) * LANES] = flat[pl.ds(j, D, stride=9), :].astype(bf16)
    for j in range(3):
        out_out[:, j * LANES : (j + 1) * LANES] = flat[pl.ds(9 * D + j, D, stride=3), :].astype(bf16)
    share = LANES // experts
    count = D // share
    for i in range(share):
        spread[pl.ds(i, count, stride=share), :] = flat[12 * D : 12 * D + count, :]
    lanes = lane_ids((D, LANES))
    kept = jnp.where(lanes // experts == row_ids((D, LANES)) % share, spread[...], 0.0).astype(bf16)
    fold_lane = lane_ids((LANES, LANES))
    fold = (row_ids((LANES, LANES)) % experts == lax.bitwise_xor(fold_lane, place[0])) & (
        fold_lane < experts
    )
    router_out[...] = mm(kept, jnp.where(fold, 1.0, 0.0).astype(bf16)).astype(bf16)


def unpack_dense(place, here, there, shard, experts, n_tp):
    total = shard * 2 * here.shape[0] // LANES
    flat_rows = total + here.shape[1] + 8
    return call(
        partial(unpack_kernel, shard=shard, experts=experts, n_tp=n_tp),
        6,
        grid_spec=pltpu.PrefetchScalarGridSpec(
            num_scalar_prefetch=1,
            grid=(1,),
            in_specs=resident(2),
            out_specs=resident(3),
            scratch_shapes=[pltpu.VMEM((flat_rows, LANES), f32), pltpu.VMEM((D, LANES), f32)],
        ),
        out_shape=[
            jax.ShapeDtypeStruct((D, 3 * D), bf16),
            jax.ShapeDtypeStruct((D, D), bf16),
            jax.ShapeDtypeStruct((D, LANES), bf16),
        ],
        cost_estimate=cost(1e8, 4e6),
        name="unpack_dense",
    )(place, here, there)


def key_features(marks):
    lane = lane_ids(marks.shape)
    flip = (lane < SEG_IDS) | ((lane >= SEG_IDS + 3 * VAR_IDS) & (lane < BIAS_END))
    return jnp.where(flip, 1.0 - marks, marks)


def in_windows(win, row, first, count, step):
    need = win[row, 2 * first + 1]
    for i in range(1, count):
        need = jnp.maximum(need, win[row, 2 * (first + i) + 1])

    def run(keys):
        for i in range(count):
            low = win[row, 2 * (first + i)]
            step(first + i, pl.multiple_of(jnp.minimum(low, SEQ - keys), 16), keys)

    for blocks in (2, 3, 4, 5):
        fits = need <= 2 if blocks == 2 else need == blocks
        pl.when(fits)(partial(run, blocks * QB))
    pl.when(need > 5)(partial(run, SEQ))


def prepare_kernel(
    place, routes, segs, vars_, positions, small,
    lanes_out, rows_out, table_out, win_out, marks_out, cos_out, sin_out, biases_out, *, experts,
):
    tok = routes.shape[1]
    blocks = tok // CH
    above = jnp.where(row_ids((CH, CH)) < lane_ids((CH, CH)), 1.0, 0.0).astype(bf16)
    base = jnp.zeros((experts, 1), f32)
    lane = lane_ids((experts, LANES))
    table = jnp.zeros((experts, LANES), f32)
    rel = lax.bitwise_xor(row_ids((experts, CH)), place[0])
    fill = jnp.full((LANES - experts, CH), -1.0, f32)
    for b in range(blocks):
        at = slice(b * CH, (b + 1) * CH)
        named = (routes[0:1, at] == rel) | (routes[1:2, at] == rel)
        ones = jnp.where(named, 1.0, 0.0)
        rank = mm(ones.astype(bf16), above)
        odd = base - 16.0 * jnp.floor(base * (1.0 / 16.0))
        spot = jnp.where(named, rank + odd, -1.0)
        lanes_out[:, at] = spot
        rows_out[at, :] = jnp.concatenate([spot, fill], axis=0).T
        count = jnp.sum(ones, axis=1, keepdims=True)
        windows = jnp.floor((odd + count) * (1.0 / WIN)) + 1.0
        table = jnp.where(lane == b, base - odd, jnp.where(lane == WIN_LANE + b, windows, table))
        base = base + count
    steps = jnp.floor((base + (SLOT - 1)) * (1.0 / SLOT))
    table_out[...] = jnp.where(lane == 2 * WIN_LANE - 1, steps, table).astype(jnp.int32)

    identity = jnp.where(row_ids((LANES, LANES)) == lane_ids((LANES, LANES)), 1.0, 0.0).astype(bf16)
    feature = row_ids((LANES, SEQ))
    two = row_ids((8, SEQ))
    spread = jnp.where(row_ids((8, LANES)) < 2, 1.0, 0.0).astype(bf16)
    lane = lane_ids((1, LANES))
    frequency = jnp.exp(
        (lane % (HD // 2)).astype(f32) * (-2.0 * math.log(10000.0) / HD)
    )
    sign = jnp.where(lane % HD < HD // 2, -1.0, 1.0)
    win = jnp.zeros(win_out.shape, f32)
    win_row, win_lane = row_ids(win_out.shape), lane_ids(win_out.shape)
    for i in range(segs.shape[0]):
        at = slice(i * SEQ, (i + 1) * SEQ)
        seg, var = segs[i : i + 1, :], vars_[i : i + 1, :]
        marks = jnp.where(
            feature < SEG_IDS,
            jnp.where(seg == feature, 1.0, 0.0),
            jnp.where(
                feature < BIAS_END,
                jnp.where(var == feature % VAR_IDS, 1.0, 0.0),
                jnp.where(
                    (feature % HD >= SUM_LANE) & (feature % HD < SUM_LANE + 3), 1.0, 0.0
                ),
            ),
        ).astype(bf16)
        marks_out[at, :] = mm_tn(marks, identity).astype(bf16)
        place_in_time = positions[i : i + 1, :]
        low = lax.bitwise_and(place_in_time, 31)
        halves = jnp.where(
            two == 0, (place_in_time - low).astype(f32), jnp.where(two == 1, low.astype(f32), 0.0)
        ).astype(bf16)
        angles = mm_tn(halves, spread) * frequency
        cos_out[at, :] = jnp.cos(angles)
        sin_out[at, :] = jnp.sin(angles) * sign
        for q in range(NBLK):
            head_id, tail_id = seg[:, q * QB : q * QB + 1], seg[:, (q + 1) * QB - 1 : (q + 1) * QB]
            first = jnp.sum(jnp.where(seg < head_id, 1.0, 0.0), axis=1, keepdims=True)
            last = jnp.sum(jnp.where(seg <= tail_id, 1.0, 0.0), axis=1, keepdims=True)
            first = 16.0 * jnp.floor(first * (1.0 / 16.0))
            keys = jnp.floor((last - first + (QB - 1)) * (1.0 / QB))
            win = jnp.where(
                (win_row == i) & (win_lane == 2 * q),
                first,
                jnp.where((win_row == i) & (win_lane == 2 * q + 1), keys, win),
            )
    win_out[...] = win.astype(jnp.int32)

    shape = (8, LANES)
    head, lanes = row_ids(shape), lane_ids(shape)
    bias = jnp.broadcast_to(small[0:1, 2 * D : 2 * D + 2 * HEADS], (8, 2 * HEADS))
    bias_row, bias_lane = row_ids(bias.shape), lane_ids(bias.shape)
    filled = jnp.where(lanes < SEG_IDS, -FAR, 0.0)
    for kind in range(2):
        own = jnp.sum(
            jnp.where(bias_lane == kind * HEADS + bias_row, bias, 0.0), axis=1, keepdims=True
        )
        for i, piece in enumerate(three_pieces(own)):
            first = SEG_IDS + (3 * kind + i) * VAR_IDS
            filled = jnp.where((lanes >= first) & (lanes < first + VAR_IDS), piece, filled)
    biases_out[...] = jnp.where(head < HEADS, filled, 0.0)


def prepare(place, routes, segs, vars_, positions, small, experts):
    tok = routes.shape[1]
    seqs = segs.shape[0]
    shapes = [
        ((experts, tok), f32), ((tok, LANES), f32), ((experts, LANES), jnp.int32),
        ((-(-seqs // 8) * 8, LANES), jnp.int32), ((tok, LANES), bf16), ((tok, LANES), f32),
        ((tok, LANES), f32), ((8, LANES), f32),
    ]
    return call(
        partial(prepare_kernel, experts=experts),
        8,
        grid_spec=pltpu.PrefetchScalarGridSpec(
            num_scalar_prefetch=1,
            grid=(1,),
            in_specs=resident(5),
            out_specs=resident(len(shapes)),
        ),
        out_shape=[jax.ShapeDtypeStruct(shape, dtype) for shape, dtype in shapes],
        cost_estimate=cost(1e9, 8e6),
        name="prepare",
    )(place, routes, segs, vars_, positions, small)


def row_views(refs, row):
    at = pl.ds(pl.multiple_of(row * SEQ, SEQ), SEQ)
    return [ref.at[at, :] for ref in refs]


ROW_OUTS = 8


def forward_kernel(win, *refs, experts):
    arrays, fixed, refs = refs[:6], refs[6:11], refs[11:]
    rows = arrays[0].shape[0] // SEQ
    scratch = refs[rows * ROW_OUTS :]
    for row in range(rows):
        forward_row(
            row, win, *row_views(arrays, row), *fixed, *refs[row * ROW_OUTS : (row + 1) * ROW_OUTS],
            *scratch, experts=experts,
        )


def forward_row(
    row, win, tokens, cot, cos_ref, sin_ref, marks_ref, place_rows, small, biases,
    in_proj, out_proj, router,
    q_out, k_out, v_out, lse_out, mixed_out, middle_out, rows_out, probs_out,
    keys_aug, values_aug, totals, tops, sums_out, *, experts,
):
    masks = half_masks()
    bias_low = biases[...].astype(bf16)
    gain_one, gain_two = small[0:1, :D], small[0:1, D : 2 * D]
    for p in range(PAIRS):
        values_aug[p, :, LANES:] = jnp.ones((SEQ, LANES), bf16)

    def project(c, carry):
        at = pl.ds(pl.multiple_of(c * CH, CH), CH)
        x = tokens[at, :].astype(f32)
        factor = lax.rsqrt(jnp.mean(x * x, axis=-1, keepdims=True) + norm_epsilon)
        normed = (x * factor * gain_one).astype(bf16)
        projected = mm(normed, in_proj[...])
        cosine, sine = cos_ref[at, :], sin_ref[at, :]
        features = key_features(marks_ref[at, :].astype(f32)).astype(bf16)
        for j in range(2 * PAIRS):
            part = projected[:, j * LANES : (j + 1) * LANES]
            turned = part * cosine + swap_halves(part) * sine
            if j < PAIRS:
                turned = turned.astype(bf16) * jnp.asarray(HD**-0.5, bf16)
                q_out[at, j * LANES : (j + 1) * LANES] = turned
            else:
                p = j - PAIRS
                turned = turned.astype(bf16)
                k_out[at, p * LANES : (p + 1) * LANES] = turned
                keys_aug[p, at, :LANES] = turned
                keys_aug[p, at, LANES:] = features
        for p in range(PAIRS):
            part = projected[:, 2 * D + p * LANES : 2 * D + (p + 1) * LANES].astype(bf16)
            v_out[at, p * LANES : (p + 1) * LANES] = part
            values_aug[p, at, :LANES] = part
        return carry

    lax.fori_loop(0, SEQ // CH, project, 0)

    lane = lane_ids((QB, LANES))

    def attend(quad, carry):
        def step(block, key_start, keys):
            at = pl.ds(pl.multiple_of(block * QB, QB), QB)
            key_at = pl.ds(key_start, keys)
            marks = marks_ref[at, :]
            for p in range(PAIRS):
                cols = slice(p * LANES, (p + 1) * LANES)
                queries = q_out[at, cols]
                stacked = jnp.concatenate(
                    [
                        jnp.concatenate(
                            [queries * masks[i], marks * bias_low[2 * p + i : 2 * p + i + 1, :]], axis=1
                        )
                        for i in range(2)
                    ],
                    axis=0,
                )
                scores = mm_nt(stacked, keys_aug[p, key_at, :])
                top = jnp.max(scores, axis=1, keepdims=True)
                weights = jnp.exp(scores - top).astype(bf16)
                sums = mm(weights, values_aug[p, key_at, :])
                sums_out[at, cols] = jnp.where(lane < HD, sums[:QB, :LANES], sums[QB:, :LANES])
                totals[at, cols] = jnp.where(lane < HD, sums[:QB, LANES:], sums[QB:, LANES:])
                tops[at, cols] = jnp.where(lane < HD, top[:QB], top[QB:])

        in_windows(win, row, 4 * quad, 4, step)
        return carry

    lax.fori_loop(0, NBLK // 4, attend, 0)

    def finish(c, carry):
        at = pl.ds(pl.multiple_of(c * CH, CH), CH)
        for p in range(PAIRS):
            cols = slice(p * LANES, (p + 1) * LANES)
            total = totals[at, cols]
            mixed_out[at, cols] = (sums_out[at, cols] / total).astype(bf16)
            lse_out[at, cols] = own_summand(-(tops[at, cols] + jnp.log(total)))
        middle = tokens[at, :].astype(f32) + mm(mixed_out[at, :], out_proj[...])
        middle_out[at, :] = middle
        factor = lax.rsqrt(jnp.mean(middle * middle, axis=-1, keepdims=True) + norm_epsilon)
        normed = (middle * factor * gain_two).astype(bf16)
        rows_out[at, :D] = normed
        rows_out[at, D : 2 * D] = cot[at, :]
        logits = mm(normed, router[...])
        named = place_rows[at, :] >= 0.0
        top = jnp.max(jnp.where(named, logits, -3.0e38), axis=1, keepdims=True)
        weights = jnp.where(named, jnp.exp(jnp.where(named, logits - top, 0.0)), 0.0)
        probs = weights / jnp.sum(weights, axis=1, keepdims=True)
        probs_out[at, :] = probs
        high, mid, low = three_pieces(probs)
        rows_out[at, 2 * D :] = (
            high + pltpu.roll(mid, experts, 1) + pltpu.roll(low, 2 * experts, 1)
        ).astype(bf16)
        return carry

    lax.fori_loop(0, SEQ // CH, finish, 0)


def forward(win, tokens, cot, cosine, sine, marks, place_rows, small, biases, weights, experts):
    tok = tokens.shape[0]
    shapes = [
        jax.ShapeDtypeStruct((SEQ, width), dtype)
        for width, dtype in [(D, bf16)] * 5 + [(D, f32), (XW, bf16), (LANES, f32)]
    ] * (tok // SEQ)
    return call(
        partial(forward_kernel, experts=experts),
        12,
        grid_spec=pltpu.PrefetchScalarGridSpec(
            num_scalar_prefetch=1,
            grid=(1,),
            in_specs=resident(11),
            out_specs=resident(len(shapes)),
            scratch_shapes=[
                pltpu.VMEM((PAIRS, SEQ, 2 * LANES), bf16),
                pltpu.VMEM((PAIRS, SEQ, 2 * LANES), bf16),
                pltpu.VMEM((SEQ, D), f32),
                pltpu.VMEM((SEQ, D), f32),
                pltpu.VMEM((SEQ, D), f32),
            ],
        ),
        out_shape=shapes,
        cost_estimate=cost(2e10, 2e7),
        name="attention_forward",
    )(win, tokens, cot, cosine, sine, marks, place_rows, small, biases, *weights)


def experts_kernel(table, *refs, group, experts, blocks, chained):
    size = len(group)
    weights_hbm = refs[:size]
    place_lanes, place_rows = refs[size : size + 2]
    seqs = blocks * CH // SEQ
    rows, refs = refs[size + 2 : size + 2 + seqs], refs[size + 2 + seqs :]
    earlier, refs = refs[:chained], refs[chained:]
    part_out, *grads_hbm = refs[: size + 1]
    slots, weights, grads, grad_in, grad_down, total, in_sems, out_sems = refs[size + 1 :]
    ff = grad_down.shape[0]
    cuts = ff // LANES
    arrivals = [
        pltpu.make_async_copy(weights_hbm[g], weights.at[g % 2], in_sems.at[g]) for g in range(size)
    ]
    departures = [
        pltpu.make_async_copy(grads.at[g % 2], grads_hbm[g], out_sems.at[g]) for g in range(size)
    ]
    for copy in arrivals[:2]:
        copy.start()

    def first_slot(block, r):
        return pl.multiple_of(table[r, block], 16)

    for g in range(size):
        slots[g, 0:16, :] = jnp.zeros((16, XW), bf16)

    def gather(seq, inner, carry):
        block = seq * (SEQ // CH) + inner
        at = pl.ds(pl.multiple_of(block * CH, CH), CH)
        source = rows[seq][pl.ds(pl.multiple_of(inner * CH, CH), CH), :]
        slot = row_ids((WIN, CH)).astype(f32)

        def picks(r, first):
            return jnp.where(place_lanes[r : r + 1, at] - first == slot, 1.0, 0.0).astype(bf16)

        moved = mm(jnp.concatenate([picks(r, 0.0) for r in group], axis=0), source).astype(bf16)
        for g, r in enumerate(group):
            start = first_slot(block, r)
            slots[g, pl.ds(start, 16), :] += moved[g * WIN : g * WIN + 16]
            slots[g, pl.ds(start + 16, WIN - 16), :] = moved[g * WIN + 16 : (g + 1) * WIN]

            def more(w, inner, g=g, r=r, start=start):
                slots[g, pl.ds(start + w * WIN, WIN), :] = mm(
                    picks(r, (w * WIN).astype(f32)), source
                ).astype(bf16)
                return inner

            lax.fori_loop(1, table[r, WIN_LANE + block], more, 0)
        return carry

    for seq in range(seqs):
        lax.fori_loop(0, SEQ // CH, partial(gather, seq), 0)

    for g, r in enumerate(group):
        end = first_slot(blocks - 1, r) + table[r, WIN_LANE + blocks - 1] * WIN
        slots[g, pl.ds(end, SLOT), :] = jnp.zeros((SLOT, XW), bf16)
        arrivals[g].wait()
        gate_w = jnp.concatenate([weights[g % 2, z, :D, :] for z in range(cuts)], axis=1)
        up_w = jnp.concatenate([weights[g % 2, z, D : 2 * D, :] for z in range(cuts)], axis=1)
        down_w = jnp.concatenate(
            [
                jnp.concatenate(
                    [weights[g % 2, z, (6 + j) * LANES : (7 + j) * LANES, :] for j in range(3)], axis=1
                )
                for z in range(cuts)
            ],
            axis=0,
        )
        grad_in[...] = jnp.zeros(grad_in.shape, f32)
        grad_down[...] = jnp.zeros(grad_down.shape, f32)

        def step(i, carry, g=g, r=r, gate_w=gate_w, up_w=up_w, down_w=down_w):
            at = pl.ds(pl.multiple_of(i * SLOT, SLOT), SLOT)
            x = slots[g, at, :D]
            cot = slots[g, at, D : 2 * D].astype(f32)
            parts = slots[g, at, 2 * D :].astype(f32)
            prob = (
                parts[:, r : r + 1]
                + parts[:, experts + r : experts + r + 1]
                + parts[:, 2 * experts + r : 2 * experts + r + 1]
            )
            gate_pre = mm(x, gate_w)
            up_pre = mm(x, up_w)
            sigmoid = 1.0 / (1.0 + jnp.exp(-gate_pre))
            silu = gate_pre * sigmoid
            hidden = (silu * up_pre).astype(bf16)
            result = mm(hidden, down_w).astype(bf16).astype(f32)
            grad_result = (prob * cot).astype(bf16)
            grad_hidden = mm_nt(grad_result, down_w)
            grad_gate = (
                grad_hidden * up_pre * sigmoid * (1.0 + gate_pre * (1.0 - sigmoid))
            ).astype(bf16)
            grad_up = (grad_hidden * silu).astype(bf16)
            grad_rows = mm_nt(grad_gate, gate_w) + mm_nt(grad_up, up_w)
            grad_in[:, :ff] += mm_tn(x, grad_gate)
            grad_in[:, ff:] += mm_tn(x, grad_up)
            grad_down[...] += mm_tn(hidden, grad_result)
            score = jnp.sum(cot * result, axis=1, keepdims=True)
            high, mid, _ = three_pieces(jnp.broadcast_to(score, (SLOT, LANES)))
            lane = lane_ids((SLOT, LANES))
            slots[g, at, :D] = (prob * result).astype(bf16)
            slots[g, at, D : 2 * D] = grad_rows.astype(bf16)
            slots[g, at, 2 * D :] = jnp.where(
                lane == r, high, jnp.where(lane == experts + r, mid, 0.0)
            ).astype(bf16)
            return carry

        lax.fori_loop(0, table[r, 2 * WIN_LANE - 1], step, 0)
        if g + 2 < size:
            arrivals[g + 2].start()
        if g >= 2:
            departures[g - 2].wait()
        for z in range(cuts):
            cols = slice(z * LANES, (z + 1) * LANES)
            grads[g % 2, z, :D, :] = grad_in[:, cols].astype(bf16)
            grads[g % 2, z, D : 2 * D, :] = grad_in[:, ff + z * LANES : ff + (z + 1) * LANES].astype(bf16)
            for j in range(3):
                grads[g % 2, z, (6 + j) * LANES : (7 + j) * LANES, :] = grad_down[
                    cols, j * LANES : (j + 1) * LANES
                ].astype(bf16)
        departures[g].start()

    def scatter(block, carry):
        at = pl.ds(pl.multiple_of(block * CH, CH), CH)
        places = place_rows[at, :]
        slot = lane_ids((CH, WIN)).astype(f32)

        def picks(r, first):
            return jnp.where(places[:, r : r + 1] - first == slot, 1.0, 0.0).astype(bf16)

        source = jnp.concatenate(
            [slots[g, pl.ds(first_slot(block, r), WIN), :] for g, r in enumerate(group)], axis=0
        )
        total[...] = mm(jnp.concatenate([picks(r, 0.0) for r in group], axis=1), source)
        for g, r in enumerate(group):

            def more(w, inner, g=g, r=r):
                total[...] += mm(
                    picks(r, (w * WIN).astype(f32)),
                    slots[g, pl.ds(first_slot(block, r) + w * WIN, WIN), :],
                )
                return inner

            lax.fori_loop(1, table[r, WIN_LANE + block], more, 0)
        result = total[...]
        for ref in earlier:
            result = result + ref[at, :].astype(f32)
        part_out[at, :] = result.astype(bf16)
        return carry

    lax.fori_loop(0, blocks, scatter, 0)
    for copy in departures[-2:]:
        copy.wait()


def run_experts(table, weights, rows, place_lanes, place_rows, earlier, group, experts, cap):
    tok = place_rows.shape[0]
    ff = weights[0].shape[0] * LANES
    blocks = tok // CH
    shape = weights[0].shape
    size = len(group)
    there = [pl.BlockSpec(memory_space=pltpu.HBM)] * size
    out = call(
        partial(
            experts_kernel, group=group, experts=experts, blocks=blocks, chained=len(earlier)
        ),
        11 + 5 * size // 2,
        grid_spec=pltpu.PrefetchScalarGridSpec(
            num_scalar_prefetch=1,
            grid=(1,),
            in_specs=there + resident(2 + len(rows) + len(earlier)),
            out_specs=resident(1) + there,
            scratch_shapes=[
                pltpu.VMEM((size, cap + WIN + SLOT, XW), bf16),
                pltpu.VMEM((2, *shape), bf16),
                pltpu.VMEM((2, *shape), bf16),
                pltpu.VMEM((D, 2 * ff), f32),
                pltpu.VMEM((ff, D), f32),
                pltpu.VMEM((CH, XW), f32),
                pltpu.SemaphoreType.DMA((size,)),
                pltpu.SemaphoreType.DMA((size,)),
            ],
        ),
        out_shape=[jax.ShapeDtypeStruct((tok, XW), bf16)] + [jax.ShapeDtypeStruct(shape, bf16)] * size,
        input_output_aliases={3 + size + len(rows): 0} if earlier else {},
        cost_estimate=cost(4e9 * size, 3e6 * size + 8e6),
        name="experts",
    )(table, *weights, place_lanes, place_rows, *rows, *earlier)
    return out[0], out[1:]


SUMS = 5


def backward_kernel(win, place, *refs, row, rows, experts, n_tp, shard):
    arrays, fixed, refs = refs[:13], refs[13:18], refs[18:]
    earlier = refs[: SUMS if row else 0]
    refs = refs[SUMS + 2 if row else 0 :]
    results, refs = refs[:2], refs[2:]
    if row < rows - 1:
        sums, (buffers, scratch) = refs[:SUMS], (refs[SUMS : SUMS + 2], refs[SUMS + 2 : -2])
    else:
        dense_out, buffers, scratch, sums = refs[0], refs[1:3], refs[3 : -SUMS - 2], refs[-SUMS - 2 : -2]
        scratch, flat = scratch[:-1], scratch[-1]
    sems = refs[-2:]
    for i, ref in enumerate(sums):
        ref[...] = earlier[i][...] if row else jnp.zeros(ref.shape, f32)
    copies = [
        pltpu.make_async_copy(buffer, result.at[pl.ds(row * SEQ, SEQ), :], sem)
        for buffer, result, sem in zip(buffers, results, sems)
    ]
    backward_row(
        row, win, place, copies[0], *row_views(arrays[:6], row), *arrays[6:], *fixed, *buffers, *scratch, *sums,
        experts=experts,
    )
    copies[1].start()
    if row == rows - 1:
        backward_flush(place, dense_out, flat, *sums, experts=experts, n_tp=n_tp, shard=shard)
    for copy in copies:
        copy.wait()


def backward_row(
    row, win, place, block_copy,
    part_ref, tokens, cot_ref, marks_ref, cos_ref, sin_ref,
    q_ref, k_ref, v_ref, lse_ref, mixed_ref, middle_ref, probs_ref, small, biases, in_proj, out_proj, router,
    block_out, grad_in_out,
    grad_middle, grad_mixed, inner_ref, keys_aug, values_aug, grad_q, grad_k, grad_v,
    grad_in_proj, grad_out_proj, grad_router, gain_out, bias_out, *, experts,
):
    masks = half_masks()
    bias_low = biases[...].astype(bf16)
    pair_sum = jnp.where(
        (row_ids((2 * LANES, LANES)) % LANES < HD) == (lane_ids((2 * LANES, LANES)) < HD), 1.0, 0.0
    ).astype(bf16)
    gain_one, gain_two = small[0:1, :D], small[0:1, D : 2 * D]
    fold_row, fold_lane = row_ids((LANES, LANES)), lane_ids((LANES, LANES))
    tile = jnp.where(
        (lax.bitwise_xor(fold_row, place[0]) == fold_lane % experts) & (fold_row < experts), 1.0, 0.0
    ).astype(bf16)

    def head(c, carry):
        at = pl.ds(pl.multiple_of(c * CH, CH), CH)
        back = part_ref[at, :].astype(f32)
        middle = middle_ref[at, :]
        block_out[at, :] = (middle + back[:, :D]).astype(bf16)
        scores = back[:, 2 * D :]
        scores = scores + pltpu.roll(scores, LANES - experts, 1)
        probs = probs_ref[at, :]
        inner = jnp.sum(probs * scores, axis=1, keepdims=True)
        grad_logits = (probs * (scores - inner)).astype(bf16)
        grad_normed = mm_nt(grad_logits, router[...]) + back[:, D : 2 * D]
        factor = lax.rsqrt(jnp.mean(middle * middle, axis=-1, keepdims=True) + norm_epsilon)
        normed = (middle * factor * gain_two).astype(bf16)
        grad_router[...] += mm_tn(normed, mm(grad_logits, tile).astype(bf16))
        weighted = grad_normed * gain_two
        gain_out[1:2, :] += jnp.sum(grad_normed * middle * factor, axis=0, keepdims=True)
        cot = cot_ref[at, :].astype(f32)
        grad = (
            cot
            + factor * weighted
            - middle
            * (factor * factor * factor)
            * jnp.mean(weighted * middle, axis=-1, keepdims=True)
        )
        grad_middle[at, :] = grad
        branch = grad.astype(bf16)
        grad_out_proj[...] += mm_tn(mixed_ref[at, :], branch)
        mixed_grad = mm_nt(branch, out_proj[...]).astype(bf16)
        grad_mixed[at, :] = mixed_grad
        features = key_features(marks_ref[at, :].astype(f32)).astype(bf16)
        for p in range(PAIRS):
            cols = slice(p * LANES, (p + 1) * LANES)
            product = mixed_grad[:, cols].astype(f32) * mixed_ref[at, cols].astype(f32)
            high, mid, _ = three_pieces(product)
            inner = mm(jnp.concatenate([high, mid], axis=1).astype(bf16), pair_sum)
            inner_ref[at, cols] = own_summand(-inner)
            keys_aug[p, at, :LANES] = k_ref[at, cols]
            keys_aug[p, at, LANES:] = features
            values_aug[p, at, :LANES] = v_ref[at, cols]
            values_aug[p, at, LANES:] = features
        return carry

    lax.fori_loop(0, SEQ // CH, head, 0)
    block_copy.start()
    grad_k[...] = jnp.zeros(grad_k.shape, f32)
    grad_v[...] = jnp.zeros(grad_v.shape, f32)

    lane = lane_ids((QB, LANES))

    def attend(couple, carry):
        def step(block, key_start, keys):
            at = pl.ds(pl.multiple_of(block * QB, QB), QB)
            marks = marks_ref[at, :]
            key_at = pl.ds(key_start, keys)
            for p in range(PAIRS):
                cols = slice(p * LANES, (p + 1) * LANES)
                queries, logs = q_ref[at, cols], lse_ref[at, cols]
                out_grad, inner = grad_mixed[at, cols], inner_ref[at, cols]
                stacked = jnp.concatenate(
                    [
                        jnp.concatenate(
                            [
                                queries * masks[i],
                                marks * bias_low[2 * p + i : 2 * p + i + 1, :] + logs * masks[i],
                            ],
                            axis=1,
                        )
                        for i in range(2)
                    ],
                    axis=0,
                )
                grads = jnp.concatenate(
                    [
                        jnp.concatenate([out_grad * masks[i], inner * masks[i]], axis=1)
                        for i in range(2)
                    ],
                    axis=0,
                )
                keys_here = keys_aug[p, key_at, :]
                probs = jnp.exp(mm_nt(keys_here, stacked))
                shifted = mm_nt(values_aug[p, key_at, :], grads)
                grad_scores = (probs * shifted).astype(bf16)
                grad_v[key_at, cols] += mm(probs.astype(bf16), grads[:, :LANES])
                grad_k[key_at, cols] += mm(grad_scores, stacked[:, :LANES])
                back = mm_tn(grad_scores, keys_here)
                grad_q[at, cols] = (
                    jnp.where(lane < HD, back[:QB, :LANES], back[QB:, :LANES]) * HD**-0.5
                )
                for i in range(2):
                    bias_out[2 * p + i] += jnp.sum(
                        (marks.astype(f32) * back[i * QB : (i + 1) * QB, LANES:]).reshape(QB // 8, 8, LANES),
                        axis=0,
                    )

        in_windows(win, row, 2 * couple, 2, step)
        return carry

    lax.fori_loop(0, NBLK // 2, attend, 0)

    def tail(c, carry):
        at = pl.ds(pl.multiple_of(c * CH, CH), CH)
        cosine, sine = cos_ref[at, :], sin_ref[at, :]
        pieces = []
        for ref in (grad_q, grad_k):
            for p in range(PAIRS):
                part = ref[at, p * LANES : (p + 1) * LANES]
                pieces.append((part * cosine - swap_halves(part) * sine).astype(bf16))
        pieces.append(grad_v[at, :].astype(bf16))
        grad_projected = jnp.concatenate(pieces, axis=1)
        x = tokens[at, :].astype(f32)
        factor = lax.rsqrt(jnp.mean(x * x, axis=-1, keepdims=True) + norm_epsilon)
        normed = (x * factor * gain_one).astype(bf16)
        grad_in_proj[...] += mm_tn(normed, grad_projected)
        grad_normed = mm_nt(grad_projected, in_proj[...])
        weighted = grad_normed * gain_one
        gain_out[0:1, :] += jnp.sum(grad_normed * x * factor, axis=0, keepdims=True)
        grad_in_out[at, :] = (
            grad_middle[at, :]
            + factor * weighted
            - x * (factor * factor * factor) * jnp.mean(weighted * x, axis=-1, keepdims=True)
        ).astype(bf16)
        return carry

    lax.fori_loop(0, SEQ // CH, tail, 0)


def backward_flush(
    place, dense_out, flat, grad_in_proj, grad_out_proj, grad_router, gain_out, bias_out,
    *, experts, n_tp, shard,
):
    for j in range(9):
        flat[pl.ds(j, D, stride=9), :] = grad_in_proj[:, j * LANES : (j + 1) * LANES]
    for j in range(3):
        flat[pl.ds(9 * D + j, D, stride=3), :] = grad_out_proj[:, j * LANES : (j + 1) * LANES]
    share = LANES // experts
    count = D // share
    lanes = lane_ids((D, LANES))
    grad_router[...] = jnp.where(
        lanes // experts == row_ids((D, LANES)) % share, grad_router[...], 0.0
    )
    merged = grad_router[pl.ds(0, count, stride=share), :]
    for i in range(1, share):
        merged = merged + grad_router[pl.ds(i, count, stride=share), :]
    flat[12 * D : 12 * D + count, :] = merged
    spare = flat.shape[0] - (12 * D + count)
    flat[12 * D + count :, :] = jnp.zeros((spare, LANES), f32)
    n_dev = dense_out.shape[0]
    rows = dense_out.shape[1]
    half = n_dev // 2
    piece_lane = lane_ids((rows, LANES))
    for s in range(n_dev):
        exp_rel = lax.bitwise_xor(s // n_tp, place[0])
        rel = (
            (exp_rel % 2) * half + (exp_rel // 2) * n_tp + lax.bitwise_xor(s % n_tp, place[1])
        )
        start, off = divmod(shard * s, LANES)
        piece = flat[start : start + rows, :]
        if off:
            piece = jnp.where(
                piece_lane < LANES - off,
                pltpu.roll(piece, LANES - off, 1),
                pltpu.roll(flat[start + 1 : start + 1 + rows, :], LANES - off, 1),
            )
        dense_out[rel] = piece.astype(bf16)
    shape = (8, LANES)
    bias_rows, bias_lanes = row_ids(shape), lane_ids(shape)
    sums = jnp.concatenate(
        [jnp.sum(bias_out[h], axis=0, keepdims=True) for h in range(HEADS)]
        + [jnp.zeros((8 - HEADS, LANES), f32)],
        axis=0,
    )
    extra = jnp.zeros((1, LANES), f32)
    for kind in range(2):
        first_lane = SEG_IDS + 3 * kind * VAR_IDS
        own = jnp.sum(
            jnp.where((bias_lanes >= first_lane) & (bias_lanes < first_lane + VAR_IDS), sums, 0.0),
            axis=1,
            keepdims=True,
        )
        extra = extra + jnp.sum(
            jnp.where((bias_lanes == bias_rows + kind * HEADS) & (bias_rows < HEADS), own, 0.0),
            axis=0,
            keepdims=True,
        )
    spare_rows = jnp.concatenate(
        [gain_out[i : i + 1, j * LANES : (j + 1) * LANES] for i in range(2) for j in range(3)]
        + [extra, jnp.zeros((1, LANES), f32)],
        axis=0,
    ).astype(bf16)
    for s in range(n_dev):
        dense_out[s, rows - 8 :, :] = spare_rows


def backward(win, place, row, earlier, arrays, small, biases, weights, sizes):
    experts, n_exp, n_tp, shard, shard_rows = sizes
    tok = arrays[0].shape[0]
    rows = tok // SEQ
    last = row == rows - 1
    sums = [(D, 3 * D), (D, D), (D, LANES), (8, D), (HEADS, 8, LANES)]
    flat_rows = shard * n_exp * n_tp // LANES + shard_rows + 8
    there = [pl.BlockSpec(memory_space=pltpu.HBM)] * 2
    results = [jax.ShapeDtypeStruct((tok, D), bf16)] * 2
    tail_scratch = [pltpu.VMEM((flat_rows, LANES), f32)] + [pltpu.VMEM(shape, f32) for shape in sums]
    return call(
        partial(backward_kernel, row=row, rows=rows, experts=experts, n_tp=n_tp, shard=shard),
        24 if last else 18,
        grid_spec=pltpu.PrefetchScalarGridSpec(
            num_scalar_prefetch=2,
            grid=(1,),
            in_specs=resident(18) + (resident(SUMS) + there if row else []),
            out_specs=there + resident(1 if last else SUMS),
            scratch_shapes=[
                pltpu.VMEM((SEQ, D), bf16),
                pltpu.VMEM((SEQ, D), bf16),
                pltpu.VMEM((SEQ, D), f32),
                pltpu.VMEM((SEQ, D), bf16),
                pltpu.VMEM((SEQ, D), bf16),
                pltpu.VMEM((PAIRS, SEQ, 2 * LANES), bf16),
                pltpu.VMEM((PAIRS, SEQ, 2 * LANES), bf16),
                pltpu.VMEM((SEQ, D), f32),
                pltpu.VMEM((SEQ, D), f32),
                pltpu.VMEM((SEQ, D), f32),
                *(tail_scratch if last else []),
                pltpu.SemaphoreType.DMA(()),
                pltpu.SemaphoreType.DMA(()),
            ],
        ),
        out_shape=results
        + (
            [jax.ShapeDtypeStruct((n_exp * n_tp, shard_rows, LANES), bf16)]
            if last
            else [jax.ShapeDtypeStruct(shape, f32) for shape in sums]
        ),
        input_output_aliases={20 + SUMS: 0, 21 + SUMS: 1} if row else {},
        cost_estimate=cost(2e10, 2e7),
        name="attention_backward",
    )(win, place, *arrays, small, biases, *weights, *earlier)


def swap(values, axis, mask):
    size = lax.axis_size(axis)
    return lax.ppermute(values, axis, [(i, i ^ mask) for i in range(size)])


def add_up(parts):
    parts = [part.astype(f32) for part in parts]
    while len(parts) > 1:
        parts = [sum(parts[i + 1 : i + 2], parts[i]) for i in range(0, len(parts), 2)]
    return parts[0]


def adamw_update(old_state, grad_value, rate, decay, step_value):
    moment_one = moment_rate * old_state[1] + (1.0 - moment_rate) * grad_value
    moment_two = moment_rate * old_state[2] + (1.0 - moment_rate) * grad_value * grad_value
    correction = 1.0 - jnp.power(moment_rate, step_value)
    master = old_state[0] - rate * (
        moment_one / correction / (jnp.sqrt(moment_two / correction) + adam_epsilon)
        + decay * old_state[0]
    )
    average = average_rate * old_state[3] + (1.0 - average_rate) * master
    return jnp.stack([master, moment_one, moment_two, average])


def local(
    tokens, cotangent, routes, segments, variates, positions, step_count,
    dense_state, gate_up_state, down_state, small_state,
):
    tok, seqs = tokens.shape[0], segments.shape[0]
    n_exp, n_tp = lax.axis_size("exp"), lax.axis_size("tp")
    experts = n_exp * gate_up_state.shape[1]
    cap = 2 * tok * TOP // experts
    my_exp, my_tp = lax.axis_index("exp"), lax.axis_index("tp")
    place = jnp.stack([my_exp, my_tp]).astype(jnp.int32)
    shard = dense_state.shape[1]
    shard_rows = -(-(-(-shard // LANES) + 8) // 16) * 16

    def in_line(values):
        return [values] + [swap(values, "tp", j) for j in range(1, n_tp)]

    def in_plane(values):
        return [values] + [swap(values, "exp", m) for m in range(2, n_exp, 2)]

    own = jnp.pad(dense_state[0].astype(bf16), (0, shard_rows * LANES - shard))
    line = jnp.concatenate(in_line(own.reshape(1, shard_rows, LANES)), axis=0)
    routes_later, _ = lax.optimization_barrier((routes.T, line))
    prepared = prepare(place, routes_later, segments, variates, positions, small_state, experts)
    here = jnp.concatenate(in_plane(line), axis=0)

    gate_up = gate_up_state[0, 0].astype(bf16)
    down = down_state[0, 0].astype(bf16)
    slice_ff = gate_up.shape[2]
    ff = slice_ff * n_tp
    cuts = ff // LANES

    def pack(gate_up, down):
        return jnp.stack(
            [
                jnp.concatenate(
                    [gate_up[0, :, at : at + LANES], gate_up[1, :, at : at + LANES]]
                    + [down[at : at + LANES, i : i + LANES] for i in range(0, D, LANES)],
                    axis=0,
                )
                for at in range(0, gate_up.shape[2], LANES)
            ]
        )

    def unpack(packed):
        count = packed.shape[0]
        gate, up = packed[:, :D], packed[:, D : 2 * D]
        return (
            jnp.stack([jnp.concatenate([m[i] for i in range(count)], axis=1) for m in (gate, up)]),
            jnp.concatenate(
                [packed[:, 2 * D + i : 2 * D + i + LANES] for i in range(0, D, LANES)], axis=2
            ).reshape(count * LANES, D),
        )

    if slice_ff % LANES == 0:
        packed = jnp.concatenate(in_line(pack(gate_up, down)), axis=0)
    else:
        packed = pack(
            jnp.concatenate(in_line(gate_up), axis=2), jnp.concatenate(in_line(down), axis=0)
        )
    here, packed, prepared = lax.optimization_barrier((here, packed, prepared))
    place_lanes, place_rows, table, win, marks, cosine, sine, biases = prepared
    there = swap(here, "exp", 1)
    weights = unpack_dense(place, here, there, shard, experts, n_tp)
    if n_exp == 8:
        expert_weights = {0: packed, 2: swap(packed, "exp", 2), 4: swap(packed, "exp", 4)}
    else:
        expert_weights = {2 * i: values for i, values in enumerate(in_plane(packed))}
    expert_weights[1] = swap(packed, "exp", 1)
    saved = forward(
        win, tokens, cotangent, cosine, sine, marks, place_rows, small_state, biases, weights, experts
    )
    saved = [saved[i : i + ROW_OUTS] for i in range(0, len(saved), ROW_OUTS)]
    routed = [outs[6] for outs in saved]
    if n_exp == 8:
        groups = [(0, 1), (6, 7), (2, 3, 4, 5)]
        one, other, _ = lax.optimization_barrier((expert_weights[2], expert_weights[4], saved[-1][7]))
        expert_weights[6] = jnp.concatenate(
            [swap(one[: cuts // 2], "exp", 4), swap(other[cuts // 2 :], "exp", 2)], axis=0
        )
    else:
        groups = [(0, 1)] + [tuple(range(i, min(i + 4, n_exp))) for i in range(2, n_exp, 4)]
    chain, halves, mine = [], {}, {}
    for group in groups:
        part, grads = run_experts(
            table, [expert_weights[r] for r in group], routed, place_lanes, place_rows, chain, group,
            experts, cap,
        )
        if not chain:
            for g in groups[1:]:
                for m in g[::2]:
                    values, _ = lax.optimization_barrier((expert_weights[m], part))
                    expert_weights[m + 1] = swap(values, "exp", 1)
        if group == groups[-1]:
            part, grads, mine[far] = lax.optimization_barrier((part, grads, mine[far]))
        for i in range(0, len(group), 2):
            halves[group[i]] = add_up([grads[i], swap(grads[i + 1], "exp", 1)]).astype(bf16)
        if chain and group != groups[-1] and not mine:
            far = group[0]
            mine = {far: swap(halves[far], "exp", far)}
            part, _ = lax.optimization_barrier((part, halves[far]))
        chain = [part]
    mine[0] = halves[0]
    for m in range(2, n_exp, 2):
        if m not in mine:
            mine[m] = swap(halves[m], "exp", m)

    arrays = (part, tokens, cotangent, marks, cosine, sine)
    sizes = (experts, n_exp, n_tp, shard, shard_rows)
    earlier = []
    for row in range(seqs):
        if row == seqs - 1:
            mine = add_up([mine[m] for m in range(0, n_exp, 2)]).astype(bf16)
            earlier, mine = lax.optimization_barrier((earlier, mine))
        block_out, grad_in, *rest = backward(
            win, place, row, earlier, (*arrays, *saved[row][:6], saved[row][7]), small_state, biases, weights, sizes
        )
        earlier = [*rest, block_out, grad_in]
    dense_grad = rest[0]

    if slice_ff % LANES == 0:
        mine = mine.reshape(n_tp, slice_ff // LANES, 3 * D, LANES)
        arrived = [[mine[0]] + [swap(mine[j], "tp", j) for j in range(1, n_tp)]]
    else:
        mine_in, mine_down = unpack(mine)
        mine_in = mine_in.reshape(2, D, n_tp, slice_ff)
        mine_down = mine_down.reshape(n_tp, slice_ff, D)
        arrived = [
            [mine_in[:, :, 0]] + [swap(mine_in[:, :, j], "tp", j) for j in range(1, n_tp)],
            [mine_down[0]] + [swap(mine_down[j], "tp", j) for j in range(1, n_tp)],
        ]

    dense_grad, arrived = lax.optimization_barrier((dense_grad, arrived))

    dense_grad = dense_grad.reshape(2, n_exp // 2, n_tp, shard_rows, LANES)
    dense_half = add_up([dense_grad[0], swap(dense_grad[1], "exp", 1)]).astype(bf16)
    dense_line = add_up(
        [dense_half[0]] + [swap(dense_half[m // 2], "exp", m) for m in range(2, n_exp, 2)]
    ).astype(bf16)
    dense_parts = [dense_line[0]] + [swap(dense_line[j], "tp", j) for j in range(1, n_tp)]
    dense_mine = add_up(dense_parts)
    small_grad = dense_mine[shard_rows - 8 :].reshape(-1)[: small_state.shape[1]]
    dense_mine = dense_mine[: shard_rows - 8].reshape(-1)[:shard]
    if slice_ff % LANES == 0:
        grad_gate_up, grad_down = unpack(add_up(arrived[0]))
    else:
        grad_gate_up, grad_down = add_up(arrived[0]), add_up(arrived[1])
    grad_gate_up, grad_down = grad_gate_up[None], grad_down[None]

    step_value = step_count[0].astype(f32)
    dense_new = adamw_update(dense_state, dense_mine, rate_dense, weight_decay, step_value)
    gate_up_new = adamw_update(gate_up_state, grad_gate_up, rate_expert, weight_decay, step_value)
    down_new = adamw_update(down_state, grad_down, rate_expert, weight_decay, step_value)
    small_new = adamw_update(small_state, small_grad, rate_small, 0.0, step_value)
    return (
        block_out,
        grad_in,
        dense_new,
        dense_new[0].astype(bf16),
        gate_up_new,
        gate_up_new[0].astype(bf16),
        down_new,
        down_new[0].astype(bf16),
        small_new,
    )


def solution(mesh):
    in_specs = (
        P(("exp", "tp"), None),
        P(("exp", "tp"), None),
        P(("exp", "tp"), None),
        P(("exp", "tp"), None),
        P(("exp", "tp"), None),
        P(("exp", "tp"), None),
        P(),
        P(None, ("exp", "tp")),
        P(None, "exp", None, None, "tp"),
        P(None, "exp", "tp", None),
        P(),
    )
    out_specs = (
        P(("exp", "tp"), None),
        P(("exp", "tp"), None),
        P(None, ("exp", "tp")),
        P(("exp", "tp")),
        P(None, "exp", None, None, "tp"),
        P("exp", None, None, "tp"),
        P(None, "exp", "tp", None),
        P("exp", "tp", None),
        P(),
    )
    return jax.shard_map(local, mesh=mesh, in_specs=in_specs, out_specs=out_specs, check_vma=False)
```

```python
from functools import partial
import math

import jax
import jax.numpy as jnp
from jax import lax
from jax.experimental import pallas as pl
from jax.experimental.pallas import tpu as pltpu
from jax.sharding import PartitionSpec as P

D = 384
HEADS = 6
HD = 64
PAIRS = HEADS // 2
TOP = 2
SEQ = 1024
LANES = 128
QB = 128
CH = 256
NBLK = SEQ // QB
WIN = 128
SLOT = 256
XW = 2 * D + LANES
SEG_IDS = 8
VAR_IDS = 4
BIAS_END = SEG_IDS + 6 * VAR_IDS
SUM_LANE = 36
WIN_LANE = 64
FAR = 2.0**100

norm_epsilon = 1e-06
moment_rate = 0.5
average_rate = 0.9
adam_epsilon = 1e-08
weight_decay = 0.1
rate_dense = 0.05
rate_expert = 0.04
rate_small = 0.2

bf16 = jnp.bfloat16
f32 = jnp.float32


def mm(left, right):
    return lax.dot_general(left, right, (((1,), (0,)), ((), ())), preferred_element_type=f32)


def mm_nt(left, right):
    return lax.dot_general(left, right, (((1,), (1,)), ((), ())), preferred_element_type=f32)


def mm_tn(left, right):
    return lax.dot_general(left, right, (((0,), (0,)), ((), ())), preferred_element_type=f32)


def lane_ids(shape):
    return lax.broadcasted_iota(jnp.int32, shape, len(shape) - 1)


def row_ids(shape):
    return lax.broadcasted_iota(jnp.int32, shape, 0)


def three_pieces(value):
    high = value.astype(bf16)
    rest = value - high.astype(f32)
    middle = rest.astype(bf16)
    low = (rest - middle.astype(f32)).astype(bf16)
    return high.astype(f32), middle.astype(f32), low.astype(f32)


def own_summand(value):
    high, middle, low = three_pieces(value)
    lane = lane_ids(value.shape) % HD
    return jnp.where(
        lane == SUM_LANE,
        high,
        jnp.where(lane == SUM_LANE + 1, middle, jnp.where(lane == SUM_LANE + 2, low, 0.0)),
    ).astype(bf16)


def half_masks():
    lane = lane_ids((1, LANES))
    return [jnp.where(mask, 1.0, 0.0).astype(bf16) for mask in (lane < HD, lane >= HD)]


def swap_halves(values):
    lane = lane_ids(values.shape)
    return jnp.where(
        lane % HD < HD // 2,
        pltpu.roll(values, LANES - HD // 2, 1),
        pltpu.roll(values, HD // 2, 1),
    )


def call(kernel, mib, **kwargs):
    return pl.pallas_call(
        kernel,
        compiler_params=pltpu.CompilerParams(
            vmem_limit_bytes=mib * 1024 * 1024, dimension_semantics=("arbitrary",)
        ),
        **kwargs,
    )


def whole(shape):
    return pl.BlockSpec(shape, lambda *_: (0,) * len(shape))


def resident(count):
    return [pl.BlockSpec(memory_space=pltpu.VMEM)] * count


def cost(flops, moved):
    return pl.CostEstimate(flops=int(flops), transcendentals=0, bytes_accessed=int(moved))


def unpack_kernel(place, here, there, in_out, out_out, router_out, flat, spread, *, shard, experts, n_tp):
    rows = here.shape[1]
    n_dev = 2 * here.shape[0]
    flat[...] = jnp.zeros(flat.shape, f32)
    lane = lane_ids((rows, LANES))
    odd = place[0] % 2 == 1
    for s in range(n_dev):
        exp = s // n_tp
        rel = lax.bitwise_xor(exp // 2, place[0] // 2) * n_tp + lax.bitwise_xor(s % n_tp, place[1])
        start, off = divmod(shard * s, LANES)
        one, other = here[rel].astype(f32), there[rel].astype(f32)
        piece = jnp.where(odd, other, one) if exp % 2 == 0 else jnp.where(odd, one, other)
        if off:
            piece = pltpu.roll(piece, off, 1)
            flat[start : start + rows] += jnp.where(lane >= off, piece, 0.0)
            flat[start + 1 : start + 1 + rows] += jnp.where(lane < off, piece, 0.0)
        else:
            flat[start : start + rows] += piece
    for j in range(9):
        in_out[:, j * LANES : (j + 1) * LANES] = flat[pl.ds(j, D, stride=9), :].astype(bf16)
    for j in range(3):
        out_out[:, j * LANES : (j + 1) * LANES] = flat[pl.ds(9 * D + j, D, stride=3), :].astype(bf16)
    share = LANES // experts
    count = D // share
    for i in range(share):
        spread[pl.ds(i, count, stride=share), :] = flat[12 * D : 12 * D + count, :]
    lanes = lane_ids((D, LANES))
    kept = jnp.where(lanes // experts == row_ids((D, LANES)) % share, spread[...], 0.0).astype(bf16)
    fold_lane = lane_ids((LANES, LANES))
    fold = (row_ids((LANES, LANES)) % experts == lax.bitwise_xor(fold_lane, place[0])) & (
        fold_lane < experts
    )
    router_out[...] = mm(kept, jnp.where(fold, 1.0, 0.0).astype(bf16)).astype(bf16)


def unpack_dense(place, here, there, shard, experts, n_tp):
    total = shard * 2 * here.shape[0] // LANES
    flat_rows = total + here.shape[1] + 8
    return call(
        partial(unpack_kernel, shard=shard, experts=experts, n_tp=n_tp),
        6,
        grid_spec=pltpu.PrefetchScalarGridSpec(
            num_scalar_prefetch=1,
            grid=(1,),
            in_specs=resident(2),
            out_specs=resident(3),
            scratch_shapes=[pltpu.VMEM((flat_rows, LANES), f32), pltpu.VMEM((D, LANES), f32)],
        ),
        out_shape=[
            jax.ShapeDtypeStruct((D, 3 * D), bf16),
            jax.ShapeDtypeStruct((D, D), bf16),
            jax.ShapeDtypeStruct((D, LANES), bf16),
        ],
        cost_estimate=cost(1e8, 4e6),
        name="unpack_dense",
    )(place, here, there)


def key_features(marks):
    lane = lane_ids(marks.shape)
    flip = (lane < SEG_IDS) | ((lane >= SEG_IDS + 3 * VAR_IDS) & (lane < BIAS_END))
    return jnp.where(flip, 1.0 - marks, marks)


def in_windows(win, row, first, count, step):
    need = win[row, 2 * first + 1]
    for i in range(1, count):
        need = jnp.maximum(need, win[row, 2 * (first + i) + 1])

    def run(keys):
        for i in range(count):
            low = win[row, 2 * (first + i)]
            step(first + i, pl.multiple_of(jnp.minimum(low, SEQ - keys), 16), keys)

    def looped(keys):
        def one(i, carry):
            low = win[row, 2 * (first + i)]
            step(first + i, pl.multiple_of(jnp.minimum(low, SEQ - keys), 16), keys)
            return carry

        lax.fori_loop(0, count, one, 0)

    fewest = 2 if count == 2 else 3
    for blocks in range(fewest, 5):
        fits = need <= blocks if blocks == fewest else need == blocks
        pl.when(fits)(partial(run, blocks * QB))
    pl.when((need > 4) & (need <= 6))(partial(looped, 6 * QB))
    pl.when(need > 6)(partial(looped, SEQ))


def prepare_kernel(
    place, routes, segs, vars_, positions, small,
    lanes_out, rows_out, table_out, win_out, marks_out, cos_out, sin_out, biases_out, *, experts,
):
    tok = routes.shape[1]
    blocks = tok // CH
    above = jnp.where(row_ids((CH, CH)) < lane_ids((CH, CH)), 1.0, 0.0).astype(bf16)
    base = jnp.zeros((experts, 1), f32)
    lane = lane_ids((experts, LANES))
    table = jnp.zeros((experts, LANES), f32)
    rel = lax.bitwise_xor(row_ids((experts, CH)), place[0])
    fill = jnp.full((LANES - experts, CH), -1.0, f32)
    for b in range(blocks):
        at = slice(b * CH, (b + 1) * CH)
        named = (routes[0:1, at] == rel) | (routes[1:2, at] == rel)
        ones = jnp.where(named, 1.0, 0.0)
        rank = mm(ones.astype(bf16), above)
        odd = base - 16.0 * jnp.floor(base * (1.0 / 16.0))
        spot = jnp.where(named, rank + odd, -1.0)
        lanes_out[:, at] = spot
        rows_out[at, :] = jnp.concatenate([spot, fill], axis=0).T
        count = jnp.sum(ones, axis=1, keepdims=True)
        windows = jnp.floor((odd + count) * (1.0 / WIN)) + 1.0
        table = jnp.where(lane == b, base - odd, jnp.where(lane == WIN_LANE + b, windows, table))
        base = base + count
    steps = jnp.floor((base + (SLOT // 2 - 1)) * (1.0 / SLOT))
    rest = jnp.where(base > steps * SLOT, 1.0, 0.0)
    table = jnp.where(lane == 2 * WIN_LANE - 1, steps, table)
    table_out[...] = jnp.where(lane == 2 * WIN_LANE - 2, rest, table).astype(jnp.int32)

    identity = jnp.where(row_ids((LANES, LANES)) == lane_ids((LANES, LANES)), 1.0, 0.0).astype(bf16)
    feature = row_ids((LANES, SEQ))
    two = row_ids((8, SEQ))
    spread = jnp.where(row_ids((8, LANES)) < 2, 1.0, 0.0).astype(bf16)
    lane = lane_ids((1, LANES))
    frequency = jnp.exp(
        (lane % (HD // 2)).astype(f32) * (-2.0 * math.log(10000.0) / HD)
    )
    sign = jnp.where(lane % HD < HD // 2, -1.0, 1.0)
    win = jnp.zeros(win_out.shape, f32)
    win_row, win_lane = row_ids(win_out.shape), lane_ids(win_out.shape)
    for i in range(segs.shape[0]):
        at = slice(i * SEQ, (i + 1) * SEQ)
        seg, var = segs[i : i + 1, :], vars_[i : i + 1, :]
        marks = jnp.where(
            feature < SEG_IDS,
            jnp.where(seg == feature, 1.0, 0.0),
            jnp.where(
                feature < BIAS_END,
                jnp.where(var == feature % VAR_IDS, 1.0, 0.0),
                jnp.where(
                    (feature % HD >= SUM_LANE) & (feature % HD < SUM_LANE + 3), 1.0, 0.0
                ),
            ),
        ).astype(bf16)
        marks_out[at, :] = mm_tn(marks, identity).astype(bf16)
        place_in_time = positions[i : i + 1, :]
        low = lax.bitwise_and(place_in_time, 31)
        halves = jnp.where(
            two == 0, (place_in_time - low).astype(f32), jnp.where(two == 1, low.astype(f32), 0.0)
        ).astype(bf16)
        angles = mm_tn(halves, spread) * frequency
        cos_out[at, :] = jnp.cos(angles)
        sin_out[at, :] = jnp.sin(angles) * sign
        for q in range(NBLK):
            head_id, tail_id = seg[:, q * QB : q * QB + 1], seg[:, (q + 1) * QB - 1 : (q + 1) * QB]
            first = jnp.sum(jnp.where(seg < head_id, 1.0, 0.0), axis=1, keepdims=True)
            last = jnp.sum(jnp.where(seg <= tail_id, 1.0, 0.0), axis=1, keepdims=True)
            first = 16.0 * jnp.floor(first * (1.0 / 16.0))
            keys = jnp.floor((last - first + (QB - 1)) * (1.0 / QB))
            win = jnp.where(
                (win_row == i) & (win_lane == 2 * q),
                first,
                jnp.where((win_row == i) & (win_lane == 2 * q + 1), keys, win),
            )
    win_out[...] = win.astype(jnp.int32)

    shape = (8, LANES)
    head, lanes = row_ids(shape), lane_ids(shape)
    bias = jnp.broadcast_to(small[0:1, 2 * D : 2 * D + 2 * HEADS], (8, 2 * HEADS))
    bias_row, bias_lane = row_ids(bias.shape), lane_ids(bias.shape)
    filled = jnp.where(lanes < SEG_IDS, -FAR, 0.0)
    for kind in range(2):
        own = jnp.sum(
            jnp.where(bias_lane == kind * HEADS + bias_row, bias, 0.0), axis=1, keepdims=True
        )
        for i, piece in enumerate(three_pieces(own)):
            first = SEG_IDS + (3 * kind + i) * VAR_IDS
            filled = jnp.where((lanes >= first) & (lanes < first + VAR_IDS), piece, filled)
    biases_out[...] = jnp.where(head < HEADS, filled, 0.0)


def prepare(place, routes, segs, vars_, positions, small, experts):
    tok = routes.shape[1]
    seqs = segs.shape[0]
    shapes = [
        ((experts, tok), f32), ((tok, LANES), f32), ((experts, LANES), jnp.int32),
        ((-(-seqs // 8) * 8, LANES), jnp.int32), ((tok, LANES), bf16), ((tok, LANES), f32),
        ((tok, LANES), f32), ((8, LANES), f32),
    ]
    return call(
        partial(prepare_kernel, experts=experts),
        8,
        grid_spec=pltpu.PrefetchScalarGridSpec(
            num_scalar_prefetch=1,
            grid=(1,),
            in_specs=resident(5),
            out_specs=resident(len(shapes)),
        ),
        out_shape=[jax.ShapeDtypeStruct(shape, dtype) for shape, dtype in shapes],
        cost_estimate=cost(1e9, 8e6),
        name="prepare",
    )(place, routes, segs, vars_, positions, small)


def row_views(refs, row):
    at = pl.ds(pl.multiple_of(row * SEQ, SEQ), SEQ)
    return [ref.at[at, :] for ref in refs]


ROW_OUTS = 8


def forward_kernel(win, *refs, experts):
    arrays, fixed, refs = refs[:6], refs[6:11], refs[11:]
    rows = arrays[0].shape[0] // SEQ
    scratch = refs[rows * ROW_OUTS :]
    for row in range(rows):
        forward_row(
            row, win, *row_views(arrays, row), *fixed, *refs[row * ROW_OUTS : (row + 1) * ROW_OUTS],
            *scratch, experts=experts,
        )


def forward_row(
    row, win, tokens, cot, cos_ref, sin_ref, marks_ref, place_rows, small, biases,
    in_proj, out_proj, router,
    q_out, k_out, v_out, lse_out, mixed_out, middle_out, rows_out, probs_out,
    keys_aug, values_aug, totals, tops, sums_out, *, experts,
):
    masks = half_masks()
    bias_low = biases[...].astype(bf16)
    gain_one, gain_two = small[0:1, :D], small[0:1, D : 2 * D]
    for p in range(PAIRS):
        values_aug[p, :, LANES:] = jnp.ones((SEQ, LANES), bf16)

    def project(c, carry):
        at = pl.ds(pl.multiple_of(c * CH, CH), CH)
        x = tokens[at, :].astype(f32)
        factor = lax.rsqrt(jnp.mean(x * x, axis=-1, keepdims=True) + norm_epsilon)
        normed = (x * factor * gain_one).astype(bf16)
        projected = mm(normed, in_proj[...])
        cosine, sine = cos_ref[at, :], sin_ref[at, :]
        features = key_features(marks_ref[at, :].astype(f32)).astype(bf16)
        for j in range(2 * PAIRS):
            part = projected[:, j * LANES : (j + 1) * LANES]
            turned = part * cosine + swap_halves(part) * sine
            if j < PAIRS:
                turned = turned.astype(bf16) * jnp.asarray(HD**-0.5, bf16)
                q_out[at, j * LANES : (j + 1) * LANES] = turned
            else:
                p = j - PAIRS
                turned = turned.astype(bf16)
                k_out[at, p * LANES : (p + 1) * LANES] = turned
                keys_aug[p, at, :LANES] = turned
                keys_aug[p, at, LANES:] = features
        for p in range(PAIRS):
            part = projected[:, 2 * D + p * LANES : 2 * D + (p + 1) * LANES].astype(bf16)
            v_out[at, p * LANES : (p + 1) * LANES] = part
            values_aug[p, at, :LANES] = part
        return carry

    lax.fori_loop(0, SEQ // CH, project, 0, unroll=4)

    lane = lane_ids((QB, LANES))

    def attend(quad, carry):
        def step(block, key_start, keys):
            at = pl.ds(pl.multiple_of(block * QB, QB), QB)
            key_at = pl.ds(key_start, keys)
            marks = marks_ref[at, :]
            for p in range(PAIRS):
                cols = slice(p * LANES, (p + 1) * LANES)
                queries = q_out[at, cols]
                stacked = jnp.concatenate(
                    [
                        jnp.concatenate(
                            [queries * masks[i], marks * bias_low[2 * p + i : 2 * p + i + 1, :]], axis=1
                        )
                        for i in range(2)
                    ],
                    axis=0,
                )
                scores = mm_nt(stacked, keys_aug[p, key_at, :])
                top = jnp.max(scores, axis=1, keepdims=True)
                weights = jnp.exp(scores - top).astype(bf16)
                sums = mm(weights, values_aug[p, key_at, :])
                sums_out[at, cols] = jnp.where(lane < HD, sums[:QB, :LANES], sums[QB:, :LANES])
                totals[at, cols] = jnp.where(lane < HD, sums[:QB, LANES:], sums[QB:, LANES:])
                tops[at, cols] = jnp.where(lane < HD, top[:QB], top[QB:])

        in_windows(win, row, 4 * quad, 4, step)
        return carry

    lax.fori_loop(0, NBLK // 4, attend, 0)

    def finish(c, carry):
        at = pl.ds(pl.multiple_of(c * CH, CH), CH)
        for p in range(PAIRS):
            cols = slice(p * LANES, (p + 1) * LANES)
            total = totals[at, cols]
            mixed_out[at, cols] = (sums_out[at, cols] / total).astype(bf16)
            lse_out[at, cols] = own_summand(-(tops[at, cols] + jnp.log(total)))
        middle = tokens[at, :].astype(f32) + mm(mixed_out[at, :], out_proj[...])
        middle_out[at, :] = middle
        factor = lax.rsqrt(jnp.mean(middle * middle, axis=-1, keepdims=True) + norm_epsilon)
        normed = (middle * factor * gain_two).astype(bf16)
        rows_out[at, :D] = normed
        rows_out[at, D : 2 * D] = cot[at, :]
        logits = mm(normed, router[...])
        named = place_rows[at, :] >= 0.0
        top = jnp.max(jnp.where(named, logits, -3.0e38), axis=1, keepdims=True)
        weights = jnp.where(named, jnp.exp(jnp.where(named, logits - top, 0.0)), 0.0)
        probs = weights / jnp.sum(weights, axis=1, keepdims=True)
        probs_out[at, :] = probs
        high, mid, low = three_pieces(probs)
        rows_out[at, 2 * D :] = (
            high + pltpu.roll(mid, experts, 1) + pltpu.roll(low, 2 * experts, 1)
        ).astype(bf16)
        return carry

    lax.fori_loop(0, SEQ // CH, finish, 0, unroll=4)


def forward(win, tokens, cot, cosine, sine, marks, place_rows, small, biases, weights, experts):
    tok = tokens.shape[0]
    shapes = [
        jax.ShapeDtypeStruct((SEQ, width), dtype)
        for width, dtype in [(D, bf16)] * 5 + [(D, f32), (XW, bf16), (LANES, f32)]
    ] * (tok // SEQ)
    return call(
        partial(forward_kernel, experts=experts),
        12,
        grid_spec=pltpu.PrefetchScalarGridSpec(
            num_scalar_prefetch=1,
            grid=(1,),
            in_specs=resident(11),
            out_specs=resident(len(shapes)),
            scratch_shapes=[
                pltpu.VMEM((PAIRS, SEQ, 2 * LANES), bf16),
                pltpu.VMEM((PAIRS, SEQ, 2 * LANES), bf16),
                pltpu.VMEM((SEQ, D), f32),
                pltpu.VMEM((SEQ, D), f32),
                pltpu.VMEM((SEQ, D), f32),
            ],
        ),
        out_shape=shapes,
        cost_estimate=cost(2e10, 2e7),
        name="attention_forward",
    )(win, tokens, cot, cosine, sine, marks, place_rows, small, biases, *weights)


def experts_kernel(table, *refs, group, experts, blocks, chained):
    size = len(group)
    weights_hbm = refs[:size]
    place_lanes, place_rows = refs[size : size + 2]
    seqs = blocks * CH // SEQ
    rows, refs = refs[size + 2 : size + 2 + seqs], refs[size + 2 + seqs :]
    earlier, refs = refs[:chained], refs[chained:]
    part_out, *grads_hbm = refs[: size + 1]
    slots, weights, grads, grad_in, grad_down, total, in_sems, out_sems = refs[size + 1 :]
    ff = grad_down.shape[0]
    cuts = ff // LANES
    arrivals = [
        pltpu.make_async_copy(weights_hbm[g], weights.at[g % 2], in_sems.at[g]) for g in range(size)
    ]
    departures = [
        pltpu.make_async_copy(grads.at[g % 2], grads_hbm[g], out_sems.at[g]) for g in range(size)
    ]
    for copy in arrivals[:2]:
        copy.start()

    def first_slot(block, r):
        return pl.multiple_of(table[r, block], 16)

    for g in range(size):
        slots[g, 0:16, :] = jnp.zeros((16, XW), bf16)

    def gather(seq, inner, carry):
        block = seq * (SEQ // CH) + inner
        at = pl.ds(pl.multiple_of(block * CH, CH), CH)
        source = rows[seq][pl.ds(pl.multiple_of(inner * CH, CH), CH), :]
        slot = row_ids((WIN, CH)).astype(f32)

        def picks(r, first):
            return jnp.where(place_lanes[r : r + 1, at] - first == slot, 1.0, 0.0).astype(bf16)

        moved = mm(jnp.concatenate([picks(r, 0.0) for r in group], axis=0), source).astype(bf16)
        for g, r in enumerate(group):
            start = first_slot(block, r)
            slots[g, pl.ds(start, 16), :] += moved[g * WIN : g * WIN + 16]
            slots[g, pl.ds(start + 16, WIN - 16), :] = moved[g * WIN + 16 : (g + 1) * WIN]

            def more(w, inner, g=g, r=r, start=start):
                slots[g, pl.ds(start + w * WIN, WIN), :] = mm(
                    picks(r, (w * WIN).astype(f32)), source
                ).astype(bf16)
                return inner

            lax.fori_loop(1, table[r, WIN_LANE + block], more, 0)
        return carry

    for seq in range(seqs):
        lax.fori_loop(0, SEQ // CH, partial(gather, seq), 0)

    for g, r in enumerate(group):
        end = first_slot(blocks - 1, r) + table[r, WIN_LANE + blocks - 1] * WIN
        slots[g, pl.ds(end, SLOT), :] = jnp.zeros((SLOT, XW), bf16)
        arrivals[g].wait()
        gate_w = jnp.concatenate([weights[g % 2, z, :D, :] for z in range(cuts)], axis=1)
        up_w = jnp.concatenate([weights[g % 2, z, D : 2 * D, :] for z in range(cuts)], axis=1)
        down_w = jnp.concatenate(
            [
                jnp.concatenate(
                    [weights[g % 2, z, (6 + j) * LANES : (7 + j) * LANES, :] for j in range(3)], axis=1
                )
                for z in range(cuts)
            ],
            axis=0,
        )
        grad_in[...] = jnp.zeros(grad_in.shape, f32)
        grad_down[...] = jnp.zeros(grad_down.shape, f32)

        def step(i, carry, size=SLOT, g=g, r=r, gate_w=gate_w, up_w=up_w, down_w=down_w):
            at = pl.ds(pl.multiple_of(i * SLOT, SLOT), size)
            x = slots[g, at, :D]
            cot = slots[g, at, D : 2 * D].astype(f32)
            parts = slots[g, at, 2 * D :].astype(f32)
            prob = (
                parts[:, r : r + 1]
                + parts[:, experts + r : experts + r + 1]
                + parts[:, 2 * experts + r : 2 * experts + r + 1]
            )
            gate_pre = mm(x, gate_w)
            up_pre = mm(x, up_w)
            sigmoid = 1.0 / (1.0 + jnp.exp(-gate_pre))
            silu = gate_pre * sigmoid
            hidden = (silu * up_pre).astype(bf16)
            result = mm(hidden, down_w).astype(bf16).astype(f32)
            grad_result = (prob * cot).astype(bf16)
            grad_hidden = mm_nt(grad_result, down_w)
            grad_gate = (
                grad_hidden * up_pre * sigmoid * (1.0 + gate_pre * (1.0 - sigmoid))
            ).astype(bf16)
            grad_up = (grad_hidden * silu).astype(bf16)
            grad_rows = mm_nt(grad_gate, gate_w) + mm_nt(grad_up, up_w)
            grad_in[:, :ff] += mm_tn(x, grad_gate)
            grad_in[:, ff:] += mm_tn(x, grad_up)
            grad_down[...] += mm_tn(hidden, grad_result)
            score = jnp.sum(cot * result, axis=1, keepdims=True)
            high, mid, _ = three_pieces(jnp.broadcast_to(score, (size, LANES)))
            lane = lane_ids((size, LANES))
            slots[g, at, :D] = (prob * result).astype(bf16)
            slots[g, at, D : 2 * D] = grad_rows.astype(bf16)
            slots[g, at, 2 * D :] = jnp.where(
                lane == r, high, jnp.where(lane == experts + r, mid, 0.0)
            ).astype(bf16)
            return carry

        steps = table[r, 2 * WIN_LANE - 1]
        lax.fori_loop(0, steps, step, 0)
        pl.when(table[r, 2 * WIN_LANE - 2] > 0)(partial(step, steps, None, SLOT // 2))
        if g + 2 < size:
            arrivals[g + 2].start()
        if g >= 2:
            departures[g - 2].wait()
        for z in range(cuts):
            cols = slice(z * LANES, (z + 1) * LANES)
            grads[g % 2, z, :D, :] = grad_in[:, cols].astype(bf16)
            grads[g % 2, z, D : 2 * D, :] = grad_in[:, ff + z * LANES : ff + (z + 1) * LANES].astype(bf16)
            for j in range(3):
                grads[g % 2, z, (6 + j) * LANES : (7 + j) * LANES, :] = grad_down[
                    cols, j * LANES : (j + 1) * LANES
                ].astype(bf16)
        departures[g].start()

    def scatter(block, carry):
        at = pl.ds(pl.multiple_of(block * CH, CH), CH)
        places = place_rows[at, :]
        slot = lane_ids((CH, WIN)).astype(f32)

        def picks(r, first):
            return jnp.where(places[:, r : r + 1] - first == slot, 1.0, 0.0).astype(bf16)

        source = jnp.concatenate(
            [slots[g, pl.ds(first_slot(block, r), WIN), :] for g, r in enumerate(group)], axis=0
        )
        total[...] = mm(jnp.concatenate([picks(r, 0.0) for r in group], axis=1), source)
        for g, r in enumerate(group):

            def more(w, inner, g=g, r=r):
                total[...] += mm(
                    picks(r, (w * WIN).astype(f32)),
                    slots[g, pl.ds(first_slot(block, r) + w * WIN, WIN), :],
                )
                return inner

            lax.fori_loop(1, table[r, WIN_LANE + block], more, 0)
        result = total[...]
        for ref in earlier:
            result = result + ref[at, :].astype(f32)
        part_out[at, :] = result.astype(bf16)
        return carry

    lax.fori_loop(0, blocks, scatter, 0)
    for copy in departures[-2:]:
        copy.wait()


def run_experts(table, weights, rows, place_lanes, place_rows, earlier, group, experts, cap):
    tok = place_rows.shape[0]
    ff = weights[0].shape[0] * LANES
    blocks = tok // CH
    shape = weights[0].shape
    size = len(group)
    there = [pl.BlockSpec(memory_space=pltpu.HBM)] * size
    out = call(
        partial(
            experts_kernel, group=group, experts=experts, blocks=blocks, chained=len(earlier)
        ),
        11 + 5 * size // 2,
        grid_spec=pltpu.PrefetchScalarGridSpec(
            num_scalar_prefetch=1,
            grid=(1,),
            in_specs=there + resident(2 + len(rows) + len(earlier)),
            out_specs=resident(1) + there,
            scratch_shapes=[
                pltpu.VMEM((size, cap + WIN + SLOT, XW), bf16),
                pltpu.VMEM((2, *shape), bf16),
                pltpu.VMEM((2, *shape), bf16),
                pltpu.VMEM((D, 2 * ff), f32),
                pltpu.VMEM((ff, D), f32),
                pltpu.VMEM((CH, XW), f32),
                pltpu.SemaphoreType.DMA((size,)),
                pltpu.SemaphoreType.DMA((size,)),
            ],
        ),
        out_shape=[jax.ShapeDtypeStruct((tok, XW), bf16)] + [jax.ShapeDtypeStruct(shape, bf16)] * size,
        input_output_aliases={3 + size + len(rows): 0} if earlier else {},
        cost_estimate=cost(4e9 * size, 3e6 * size + 8e6),
        name="experts",
    )(table, *weights, place_lanes, place_rows, *rows, *earlier)
    return out[0], out[1:]


SUMS = 5


def backward_kernel(win, place, *refs, row, rows, experts, n_tp, shard):
    arrays, fixed, refs = refs[:13], refs[13:18], refs[18:]
    earlier = refs[: SUMS if row else 0]
    refs = refs[SUMS + 2 if row else 0 :]
    results, refs = refs[:2], refs[2:]
    if row < rows - 1:
        sums, (buffers, scratch) = refs[:SUMS], (refs[SUMS : SUMS + 2], refs[SUMS + 2 : -2])
    else:
        dense_out, buffers, scratch, sums = refs[0], refs[1:3], refs[3 : -SUMS - 2], refs[-SUMS - 2 : -2]
        scratch, flat = scratch[:-1], scratch[-1]
    sems = refs[-2:]
    for i, ref in enumerate(sums):
        ref[...] = earlier[i][...] if row else jnp.zeros(ref.shape, f32)
    copies = [
        pltpu.make_async_copy(buffer, result.at[pl.ds(row * SEQ, SEQ), :], sem)
        for buffer, result, sem in zip(buffers, results, sems)
    ]
    backward_row(
        row, win, place, copies[0], *row_views(arrays[:6], row), *arrays[6:], *fixed, *buffers, *scratch, *sums,
        experts=experts,
    )
    copies[1].start()
    if row == rows - 1:
        backward_flush(place, dense_out, flat, *sums, experts=experts, n_tp=n_tp, shard=shard)
    for copy in copies:
        copy.wait()


def backward_row(
    row, win, place, block_copy,
    part_ref, tokens, cot_ref, marks_ref, cos_ref, sin_ref,
    q_ref, k_ref, v_ref, lse_ref, mixed_ref, middle_ref, probs_ref, small, biases, in_proj, out_proj, router,
    block_out, grad_in_out,
    grad_middle, grad_mixed, inner_ref, keys_aug, values_aug, grad_q, grad_k, grad_v,
    grad_in_proj, grad_out_proj, grad_router, gain_out, bias_out, *, experts,
):
    masks = half_masks()
    bias_low = biases[...].astype(bf16)
    pair_sum = jnp.where(
        (row_ids((2 * LANES, LANES)) % LANES < HD) == (lane_ids((2 * LANES, LANES)) < HD), 1.0, 0.0
    ).astype(bf16)
    gain_one, gain_two = small[0:1, :D], small[0:1, D : 2 * D]
    fold_row, fold_lane = row_ids((LANES, LANES)), lane_ids((LANES, LANES))
    tile = jnp.where(
        (lax.bitwise_xor(fold_row, place[0]) == fold_lane % experts) & (fold_row < experts), 1.0, 0.0
    ).astype(bf16)

    def head(c, carry):
        at = pl.ds(pl.multiple_of(c * CH, CH), CH)
        back = part_ref[at, :].astype(f32)
        middle = middle_ref[at, :]
        block_out[at, :] = (middle + back[:, :D]).astype(bf16)
        scores = back[:, 2 * D :]
        scores = scores + pltpu.roll(scores, LANES - experts, 1)
        probs = probs_ref[at, :]
        inner = jnp.sum(probs * scores, axis=1, keepdims=True)
        grad_logits = (probs * (scores - inner)).astype(bf16)
        grad_normed = mm_nt(grad_logits, router[...]) + back[:, D : 2 * D]
        factor = lax.rsqrt(jnp.mean(middle * middle, axis=-1, keepdims=True) + norm_epsilon)
        normed = (middle * factor * gain_two).astype(bf16)
        grad_router[...] += mm_tn(normed, mm(grad_logits, tile).astype(bf16))
        weighted = grad_normed * gain_two
        gain_out[1:2, :] += jnp.sum(grad_normed * middle * factor, axis=0, keepdims=True)
        cot = cot_ref[at, :].astype(f32)
        grad = (
            cot
            + factor * weighted
            - middle
            * (factor * factor * factor)
            * jnp.mean(weighted * middle, axis=-1, keepdims=True)
        )
        grad_middle[at, :] = grad
        branch = grad.astype(bf16)
        grad_out_proj[...] += mm_tn(mixed_ref[at, :], branch)
        mixed_grad = mm_nt(branch, out_proj[...]).astype(bf16)
        grad_mixed[at, :] = mixed_grad
        features = key_features(marks_ref[at, :].astype(f32)).astype(bf16)
        for p in range(PAIRS):
            cols = slice(p * LANES, (p + 1) * LANES)
            product = mixed_grad[:, cols].astype(f32) * mixed_ref[at, cols].astype(f32)
            high, mid, _ = three_pieces(product)
            inner = mm(jnp.concatenate([high, mid], axis=1).astype(bf16), pair_sum)
            inner_ref[at, cols] = own_summand(-inner)
            keys_aug[p, at, :LANES] = k_ref[at, cols]
            keys_aug[p, at, LANES:] = features
            values_aug[p, at, :LANES] = v_ref[at, cols]
            values_aug[p, at, LANES:] = features
        return carry

    lax.fori_loop(0, SEQ // CH, head, 0, unroll=4)
    block_copy.start()
    grad_k[...] = jnp.zeros(grad_k.shape, f32)
    grad_v[...] = jnp.zeros(grad_v.shape, f32)

    lane = lane_ids((QB, LANES))

    def attend(couple, carry):
        def step(block, key_start, keys):
            at = pl.ds(pl.multiple_of(block * QB, QB), QB)
            marks = marks_ref[at, :]
            key_at = pl.ds(key_start, keys)
            for p in range(PAIRS):
                cols = slice(p * LANES, (p + 1) * LANES)
                queries, logs = q_ref[at, cols], lse_ref[at, cols]
                out_grad, inner = grad_mixed[at, cols], inner_ref[at, cols]
                stacked = jnp.concatenate(
                    [
                        jnp.concatenate(
                            [
                                queries * masks[i],
                                marks * bias_low[2 * p + i : 2 * p + i + 1, :] + logs * masks[i],
                            ],
                            axis=1,
                        )
                        for i in range(2)
                    ],
                    axis=0,
                )
                grads = jnp.concatenate(
                    [
                        jnp.concatenate([out_grad * masks[i], inner * masks[i]], axis=1)
                        for i in range(2)
                    ],
                    axis=0,
                )
                keys_here = keys_aug[p, key_at, :]
                probs = jnp.exp(mm_nt(keys_here, stacked))
                shifted = mm_nt(values_aug[p, key_at, :], grads)
                grad_scores = (probs * shifted).astype(bf16)
                grad_v[key_at, cols] += mm(probs.astype(bf16), grads[:, :LANES])
                grad_k[key_at, cols] += mm(grad_scores, stacked[:, :LANES])
                back = mm_tn(grad_scores, keys_here)
                grad_q[at, cols] = (
                    jnp.where(lane < HD, back[:QB, :LANES], back[QB:, :LANES]) * HD**-0.5
                )
                for i in range(2):
                    bias_out[2 * p + i] += jnp.sum(
                        (marks.astype(f32) * back[i * QB : (i + 1) * QB, LANES:]).reshape(QB // 8, 8, LANES),
                        axis=0,
                    )

        in_windows(win, row, 2 * couple, 2, step)
        return carry

    lax.fori_loop(0, NBLK // 2, attend, 0)

    def tail(c, carry):
        at = pl.ds(pl.multiple_of(c * CH, CH), CH)
        cosine, sine = cos_ref[at, :], sin_ref[at, :]
        pieces = []
        for ref in (grad_q, grad_k):
            for p in range(PAIRS):
                part = ref[at, p * LANES : (p + 1) * LANES]
                pieces.append((part * cosine - swap_halves(part) * sine).astype(bf16))
        pieces.append(grad_v[at, :].astype(bf16))
        grad_projected = jnp.concatenate(pieces, axis=1)
        x = tokens[at, :].astype(f32)
        factor = lax.rsqrt(jnp.mean(x * x, axis=-1, keepdims=True) + norm_epsilon)
        normed = (x * factor * gain_one).astype(bf16)
        grad_in_proj[...] += mm_tn(normed, grad_projected)
        grad_normed = mm_nt(grad_projected, in_proj[...])
        weighted = grad_normed * gain_one
        gain_out[0:1, :] += jnp.sum(grad_normed * x * factor, axis=0, keepdims=True)
        grad_in_out[at, :] = (
            grad_middle[at, :]
            + factor * weighted
            - x * (factor * factor * factor) * jnp.mean(weighted * x, axis=-1, keepdims=True)
        ).astype(bf16)
        return carry

    lax.fori_loop(0, SEQ // CH, tail, 0, unroll=4)


def backward_flush(
    place, dense_out, flat, grad_in_proj, grad_out_proj, grad_router, gain_out, bias_out,
    *, experts, n_tp, shard,
):
    for j in range(9):
        flat[pl.ds(j, D, stride=9), :] = grad_in_proj[:, j * LANES : (j + 1) * LANES]
    for j in range(3):
        flat[pl.ds(9 * D + j, D, stride=3), :] = grad_out_proj[:, j * LANES : (j + 1) * LANES]
    share = LANES // experts
    count = D // share
    lanes = lane_ids((D, LANES))
    grad_router[...] = jnp.where(
        lanes // experts == row_ids((D, LANES)) % share, grad_router[...], 0.0
    )
    merged = grad_router[pl.ds(0, count, stride=share), :]
    for i in range(1, share):
        merged = merged + grad_router[pl.ds(i, count, stride=share), :]
    flat[12 * D : 12 * D + count, :] = merged
    spare = flat.shape[0] - (12 * D + count)
    flat[12 * D + count :, :] = jnp.zeros((spare, LANES), f32)
    n_dev = dense_out.shape[0]
    rows = dense_out.shape[1]
    half = n_dev // 2
    piece_lane = lane_ids((rows, LANES))
    for s in range(n_dev):
        exp_rel = lax.bitwise_xor(s // n_tp, place[0])
        rel = (
            (exp_rel % 2) * half + (exp_rel // 2) * n_tp + lax.bitwise_xor(s % n_tp, place[1])
        )
        start, off = divmod(shard * s, LANES)
        piece = flat[start : start + rows, :]
        if off:
            piece = jnp.where(
                piece_lane < LANES - off,
                pltpu.roll(piece, LANES - off, 1),
                pltpu.roll(flat[start + 1 : start + 1 + rows, :], LANES - off, 1),
            )
        dense_out[rel] = piece.astype(bf16)
    shape = (8, LANES)
    bias_rows, bias_lanes = row_ids(shape), lane_ids(shape)
    sums = jnp.concatenate(
        [jnp.sum(bias_out[h], axis=0, keepdims=True) for h in range(HEADS)]
        + [jnp.zeros((8 - HEADS, LANES), f32)],
        axis=0,
    )
    extra = jnp.zeros((1, LANES), f32)
    for kind in range(2):
        first_lane = SEG_IDS + 3 * kind * VAR_IDS
        own = jnp.sum(
            jnp.where((bias_lanes >= first_lane) & (bias_lanes < first_lane + VAR_IDS), sums, 0.0),
            axis=1,
            keepdims=True,
        )
        extra = extra + jnp.sum(
            jnp.where((bias_lanes == bias_rows + kind * HEADS) & (bias_rows < HEADS), own, 0.0),
            axis=0,
            keepdims=True,
        )
    spare_rows = jnp.concatenate(
        [gain_out[i : i + 1, j * LANES : (j + 1) * LANES] for i in range(2) for j in range(3)]
        + [extra, jnp.zeros((1, LANES), f32)],
        axis=0,
    ).astype(bf16)
    for s in range(n_dev):
        dense_out[s, rows - 8 :, :] = spare_rows


def backward(win, place, row, earlier, arrays, small, biases, weights, sizes):
    experts, n_exp, n_tp, shard, shard_rows = sizes
    tok = arrays[0].shape[0]
    rows = tok // SEQ
    last = row == rows - 1
    sums = [(D, 3 * D), (D, D), (D, LANES), (8, D), (HEADS, 8, LANES)]
    flat_rows = shard * n_exp * n_tp // LANES + shard_rows + 8
    there = [pl.BlockSpec(memory_space=pltpu.HBM)] * 2
    results = [jax.ShapeDtypeStruct((tok, D), bf16)] * 2
    tail_scratch = [pltpu.VMEM((flat_rows, LANES), f32)] + [pltpu.VMEM(shape, f32) for shape in sums]
    return call(
        partial(backward_kernel, row=row, rows=rows, experts=experts, n_tp=n_tp, shard=shard),
        24 if last else 18,
        grid_spec=pltpu.PrefetchScalarGridSpec(
            num_scalar_prefetch=2,
            grid=(1,),
            in_specs=resident(18) + (resident(SUMS) + there if row else []),
            out_specs=there + resident(1 if last else SUMS),
            scratch_shapes=[
                pltpu.VMEM((SEQ, D), bf16),
                pltpu.VMEM((SEQ, D), bf16),
                pltpu.VMEM((SEQ, D), f32),
                pltpu.VMEM((SEQ, D), bf16),
                pltpu.VMEM((SEQ, D), bf16),
                pltpu.VMEM((PAIRS, SEQ, 2 * LANES), bf16),
                pltpu.VMEM((PAIRS, SEQ, 2 * LANES), bf16),
                pltpu.VMEM((SEQ, D), f32),
                pltpu.VMEM((SEQ, D), f32),
                pltpu.VMEM((SEQ, D), f32),
                *(tail_scratch if last else []),
                pltpu.SemaphoreType.DMA(()),
                pltpu.SemaphoreType.DMA(()),
            ],
        ),
        out_shape=results
        + (
            [jax.ShapeDtypeStruct((n_exp * n_tp, shard_rows, LANES), bf16)]
            if last
            else [jax.ShapeDtypeStruct(shape, f32) for shape in sums]
        ),
        input_output_aliases={20 + SUMS: 0, 21 + SUMS: 1} if row else {},
        cost_estimate=cost(2e10, 2e7),
        name="attention_backward",
    )(win, place, *arrays, small, biases, *weights, *earlier)


def swap(values, axis, mask):
    size = lax.axis_size(axis)
    return lax.ppermute(values, axis, [(i, i ^ mask) for i in range(size)])


def add_up(parts):
    parts = [part.astype(f32) for part in parts]
    while len(parts) > 1:
        parts = [sum(parts[i + 1 : i + 2], parts[i]) for i in range(0, len(parts), 2)]
    return parts[0]


def adamw_update(old_state, grad_value, rate, decay, step_value):
    moment_one = moment_rate * old_state[1] + (1.0 - moment_rate) * grad_value
    moment_two = moment_rate * old_state[2] + (1.0 - moment_rate) * grad_value * grad_value
    correction = 1.0 - jnp.power(moment_rate, step_value)
    master = old_state[0] - rate * (
        moment_one / correction / (jnp.sqrt(moment_two / correction) + adam_epsilon)
        + decay * old_state[0]
    )
    average = average_rate * old_state[3] + (1.0 - average_rate) * master
    return jnp.stack([master, moment_one, moment_two, average])


def local(
    tokens, cotangent, routes, segments, variates, positions, step_count,
    dense_state, gate_up_state, down_state, small_state,
):
    tok, seqs = tokens.shape[0], segments.shape[0]
    n_exp, n_tp = lax.axis_size("exp"), lax.axis_size("tp")
    experts = n_exp * gate_up_state.shape[1]
    cap = 2 * tok * TOP // experts
    my_exp, my_tp = lax.axis_index("exp"), lax.axis_index("tp")
    place = jnp.stack([my_exp, my_tp]).astype(jnp.int32)
    shard = dense_state.shape[1]
    shard_rows = -(-(-(-shard // LANES) + 8) // 16) * 16

    def in_line(values):
        return [values] + [swap(values, "tp", j) for j in range(1, n_tp)]

    def in_plane(values):
        return [values] + [swap(values, "exp", m) for m in range(2, n_exp, 2)]

    own = jnp.pad(dense_state[0].astype(bf16), (0, shard_rows * LANES - shard))
    line = jnp.concatenate(in_line(own.reshape(1, shard_rows, LANES)), axis=0)
    routes_later, _ = lax.optimization_barrier((routes.T, line))
    prepared = prepare(place, routes_later, segments, variates, positions, small_state, experts)
    here = jnp.concatenate(in_plane(line), axis=0)

    gate_up = gate_up_state[0, 0].astype(bf16)
    down = down_state[0, 0].astype(bf16)
    slice_ff = gate_up.shape[2]
    ff = slice_ff * n_tp
    cuts = ff // LANES

    def pack(gate_up, down):
        return jnp.stack(
            [
                jnp.concatenate(
                    [gate_up[0, :, at : at + LANES], gate_up[1, :, at : at + LANES]]
                    + [down[at : at + LANES, i : i + LANES] for i in range(0, D, LANES)],
                    axis=0,
                )
                for at in range(0, gate_up.shape[2], LANES)
            ]
        )

    def unpack(packed):
        count = packed.shape[0]
        gate, up = packed[:, :D], packed[:, D : 2 * D]
        return (
            jnp.stack([jnp.concatenate([m[i] for i in range(count)], axis=1) for m in (gate, up)]),
            jnp.concatenate(
                [packed[:, 2 * D + i : 2 * D + i + LANES] for i in range(0, D, LANES)], axis=2
            ).reshape(count * LANES, D),
        )

    if slice_ff % LANES == 0:
        packed = jnp.concatenate(in_line(pack(gate_up, down)), axis=0)
    else:
        packed = pack(
            jnp.concatenate(in_line(gate_up), axis=2), jnp.concatenate(in_line(down), axis=0)
        )
    here, packed, prepared = lax.optimization_barrier((here, packed, prepared))
    place_lanes, place_rows, table, win, marks, cosine, sine, biases = prepared
    there = swap(here, "exp", 1)
    weights = unpack_dense(place, here, there, shard, experts, n_tp)
    if n_exp == 8:
        expert_weights = {0: packed, 2: swap(packed, "exp", 2), 4: swap(packed, "exp", 4)}
    else:
        expert_weights = {2 * i: values for i, values in enumerate(in_plane(packed))}
    expert_weights[1] = swap(packed, "exp", 1)
    saved = forward(
        win, tokens, cotangent, cosine, sine, marks, place_rows, small_state, biases, weights, experts
    )
    saved = [saved[i : i + ROW_OUTS] for i in range(0, len(saved), ROW_OUTS)]
    routed = [outs[6] for outs in saved]
    if n_exp == 8:
        groups = [(0, 1), (6, 7), (2, 3, 4, 5)]
        one, other, _ = lax.optimization_barrier((expert_weights[2], expert_weights[4], saved[-1][7]))
        expert_weights[6] = jnp.concatenate(
            [swap(one[: cuts // 2], "exp", 4), swap(other[cuts // 2 :], "exp", 2)], axis=0
        )
    else:
        groups = [(0, 1)] + [tuple(range(i, min(i + 4, n_exp))) for i in range(2, n_exp, 4)]
    chain, halves, mine = [], {}, {}
    for group in groups:
        part, grads = run_experts(
            table, [expert_weights[r] for r in group], routed, place_lanes, place_rows, chain, group,
            experts, cap,
        )
        if not chain:
            for g in groups[1:]:
                for m in g[::2]:
                    values, _ = lax.optimization_barrier((expert_weights[m], part))
                    expert_weights[m + 1] = swap(values, "exp", 1)
        if group == groups[-1]:
            part, grads, mine[far] = lax.optimization_barrier((part, grads, mine[far]))
        for i in range(0, len(group), 2):
            halves[group[i]] = add_up([grads[i], swap(grads[i + 1], "exp", 1)]).astype(bf16)
        if chain and group != groups[-1] and not mine:
            far = group[0]
            mine = {far: swap(halves[far], "exp", far)}
            part, _ = lax.optimization_barrier((part, halves[far]))
        chain = [part]
    mine[0] = halves[0]
    for m in range(2, n_exp, 2):
        if m not in mine:
            mine[m] = swap(halves[m], "exp", m)

    arrays = (part, tokens, cotangent, marks, cosine, sine)
    sizes = (experts, n_exp, n_tp, shard, shard_rows)
    earlier = []
    for row in range(seqs):
        if row == seqs - 1:
            mine = add_up([mine[m] for m in range(0, n_exp, 2)]).astype(bf16)
            earlier, mine = lax.optimization_barrier((earlier, mine))
        block_out, grad_in, *rest = backward(
            win, place, row, earlier, (*arrays, *saved[row][:6], saved[row][7]), small_state, biases, weights, sizes
        )
        earlier = [*rest, block_out, grad_in]
    dense_grad = rest[0]

    if slice_ff % LANES == 0:
        mine = mine.reshape(n_tp, slice_ff // LANES, 3 * D, LANES)
        arrived = [[mine[0]] + [swap(mine[j], "tp", j) for j in range(1, n_tp)]]
    else:
        mine_in, mine_down = unpack(mine)
        mine_in = mine_in.reshape(2, D, n_tp, slice_ff)
        mine_down = mine_down.reshape(n_tp, slice_ff, D)
        arrived = [
            [mine_in[:, :, 0]] + [swap(mine_in[:, :, j], "tp", j) for j in range(1, n_tp)],
            [mine_down[0]] + [swap(mine_down[j], "tp", j) for j in range(1, n_tp)],
        ]

    dense_grad, arrived = lax.optimization_barrier((dense_grad, arrived))

    dense_grad = dense_grad.reshape(2, n_exp // 2, n_tp, shard_rows, LANES)
    dense_half = add_up([dense_grad[0], swap(dense_grad[1], "exp", 1)]).astype(bf16)
    dense_line = add_up(
        [dense_half[0]] + [swap(dense_half[m // 2], "exp", m) for m in range(2, n_exp, 2)]
    ).astype(bf16)
    dense_parts = [dense_line[0]] + [swap(dense_line[j], "tp", j) for j in range(1, n_tp)]
    dense_mine = add_up(dense_parts)
    small_grad = dense_mine[shard_rows - 8 :].reshape(-1)[: small_state.shape[1]]
    dense_mine = dense_mine[: shard_rows - 8].reshape(-1)[:shard]
    if slice_ff % LANES == 0:
        grad_gate_up, grad_down = unpack(add_up(arrived[0]))
    else:
        grad_gate_up, grad_down = add_up(arrived[0]), add_up(arrived[1])
    grad_gate_up, grad_down = grad_gate_up[None], grad_down[None]

    step_value = step_count[0].astype(f32)
    dense_old, _ = lax.optimization_barrier((dense_state, dense_grad))
    dense_new = adamw_update(dense_old, dense_mine, rate_dense, weight_decay, step_value)
    gate_up_new = adamw_update(gate_up_state, grad_gate_up, rate_expert, weight_decay, step_value)
    down_new = adamw_update(down_state, grad_down, rate_expert, weight_decay, step_value)
    small_new = adamw_update(small_state, small_grad, rate_small, 0.0, step_value)
    return (
        block_out,
        grad_in,
        dense_new,
        dense_new[0].astype(bf16),
        gate_up_new,
        gate_up_new[0].astype(bf16),
        down_new,
        down_new[0].astype(bf16),
        small_new,
    )


def solution(mesh):
    in_specs = (
        P(("exp", "tp"), None),
        P(("exp", "tp"), None),
        P(("exp", "tp"), None),
        P(("exp", "tp"), None),
        P(("exp", "tp"), None),
        P(("exp", "tp"), None),
        P(),
        P(None, ("exp", "tp")),
        P(None, "exp", None, None, "tp"),
        P(None, "exp", "tp", None),
        P(),
    )
    out_specs = (
        P(("exp", "tp"), None),
        P(("exp", "tp"), None),
        P(None, ("exp", "tp")),
        P(("exp", "tp")),
        P(None, "exp", None, None, "tp"),
        P("exp", None, None, "tp"),
        P(None, "exp", "tp", None),
        P("exp", "tp", None),
        P(),
    )
    return jax.shard_map(local, mesh=mesh, in_specs=in_specs, out_specs=out_specs, check_vma=False)
```

```python
from functools import partial
import math

import jax
import jax.numpy as jnp
from jax import lax
from jax.experimental import pallas as pl
from jax.experimental.pallas import tpu as pltpu
from jax.sharding import PartitionSpec as P

D = 384
HEADS = 6
HD = 64
PAIRS = HEADS // 2
TOP = 2
SEQ = 1024
LANES = 128
QB = 128
CH = 256
RC = 512
NBLK = SEQ // QB
WIN = 128
SLOT = 256
XW = 2 * D + LANES
SEG_IDS = 8
VAR_IDS = 4
BIAS_END = SEG_IDS + 6 * VAR_IDS
SUM_LANE = 36
WIN_LANE = 64
FAR = 2.0**100

norm_epsilon = 1e-06
moment_rate = 0.5
average_rate = 0.9
adam_epsilon = 1e-08
weight_decay = 0.1
rate_dense = 0.05
rate_expert = 0.04
rate_small = 0.2

bf16 = jnp.bfloat16
f32 = jnp.float32


def mm(left, right):
    return lax.dot_general(left, right, (((1,), (0,)), ((), ())), preferred_element_type=f32)


def mm_nt(left, right):
    return lax.dot_general(left, right, (((1,), (1,)), ((), ())), preferred_element_type=f32)


def mm_tn(left, right):
    return lax.dot_general(left, right, (((0,), (0,)), ((), ())), preferred_element_type=f32)


def lane_ids(shape):
    return lax.broadcasted_iota(jnp.int32, shape, len(shape) - 1)


def row_ids(shape):
    return lax.broadcasted_iota(jnp.int32, shape, 0)


def three_pieces(value):
    high = value.astype(bf16)
    rest = value - high.astype(f32)
    middle = rest.astype(bf16)
    low = (rest - middle.astype(f32)).astype(bf16)
    return high.astype(f32), middle.astype(f32), low.astype(f32)


def own_summand(value):
    high, middle, low = three_pieces(value)
    lane = lane_ids(value.shape) % HD
    return jnp.where(
        lane == SUM_LANE,
        high,
        jnp.where(lane == SUM_LANE + 1, middle, jnp.where(lane == SUM_LANE + 2, low, 0.0)),
    ).astype(bf16)


def half_masks():
    lane = lane_ids((1, LANES))
    return [jnp.where(mask, 1.0, 0.0).astype(bf16) for mask in (lane < HD, lane >= HD)]


def swap_halves(values):
    lane = lane_ids(values.shape)
    return jnp.where(
        lane % HD < HD // 2,
        pltpu.roll(values, LANES - HD // 2, 1),
        pltpu.roll(values, HD // 2, 1),
    )


def call(kernel, mib, **kwargs):
    return pl.pallas_call(
        kernel,
        compiler_params=pltpu.CompilerParams(
            vmem_limit_bytes=mib * 1024 * 1024, dimension_semantics=("arbitrary",)
        ),
        **kwargs,
    )


def whole(shape):
    return pl.BlockSpec(shape, lambda *_: (0,) * len(shape))


def resident(count):
    return [pl.BlockSpec(memory_space=pltpu.VMEM)] * count


def cost(flops, moved):
    return pl.CostEstimate(flops=int(flops), transcendentals=0, bytes_accessed=int(moved))


def unpack_kernel(place, here, there, in_out, out_out, router_out, flat, spread, *, shard, experts, n_tp):
    rows = here.shape[1]
    n_dev = 2 * here.shape[0]
    flat[...] = jnp.zeros(flat.shape, f32)
    lane = lane_ids((rows, LANES))
    odd = place[0] % 2 == 1
    for s in range(n_dev):
        exp = s // n_tp
        rel = lax.bitwise_xor(exp // 2, place[0] // 2) * n_tp + lax.bitwise_xor(s % n_tp, place[1])
        start, off = divmod(shard * s, LANES)
        one, other = here[rel].astype(f32), there[rel].astype(f32)
        piece = jnp.where(odd, other, one) if exp % 2 == 0 else jnp.where(odd, one, other)
        if off:
            piece = pltpu.roll(piece, off, 1)
            flat[start : start + rows] += jnp.where(lane >= off, piece, 0.0)
            flat[start + 1 : start + 1 + rows] += jnp.where(lane < off, piece, 0.0)
        else:
            flat[start : start + rows] += piece
    for j in range(9):
        in_out[:, j * LANES : (j + 1) * LANES] = flat[pl.ds(j, D, stride=9), :].astype(bf16)
    for j in range(3):
        out_out[:, j * LANES : (j + 1) * LANES] = flat[pl.ds(9 * D + j, D, stride=3), :].astype(bf16)
    share = LANES // experts
    count = D // share
    for i in range(share):
        spread[pl.ds(i, count, stride=share), :] = flat[12 * D : 12 * D + count, :]
    lanes = lane_ids((D, LANES))
    kept = jnp.where(lanes // experts == row_ids((D, LANES)) % share, spread[...], 0.0).astype(bf16)
    fold_lane = lane_ids((LANES, LANES))
    fold = (row_ids((LANES, LANES)) % experts == lax.bitwise_xor(fold_lane, place[0])) & (
        fold_lane < experts
    )
    router_out[...] = mm(kept, jnp.where(fold, 1.0, 0.0).astype(bf16)).astype(bf16)


def unpack_dense(place, here, there, shard, experts, n_tp):
    total = shard * 2 * here.shape[0] // LANES
    flat_rows = total + here.shape[1] + 8
    return call(
        partial(unpack_kernel, shard=shard, experts=experts, n_tp=n_tp),
        6,
        grid_spec=pltpu.PrefetchScalarGridSpec(
            num_scalar_prefetch=1,
            grid=(1,),
            in_specs=resident(2),
            out_specs=resident(3),
            scratch_shapes=[pltpu.VMEM((flat_rows, LANES), f32), pltpu.VMEM((D, LANES), f32)],
        ),
        out_shape=[
            jax.ShapeDtypeStruct((D, 3 * D), bf16),
            jax.ShapeDtypeStruct((D, D), bf16),
            jax.ShapeDtypeStruct((D, LANES), bf16),
        ],
        cost_estimate=cost(1e8, 4e6),
        name="unpack_dense",
    )(place, here, there)


def key_features(marks):
    lane = lane_ids(marks.shape)
    flip = (lane < SEG_IDS) | ((lane >= SEG_IDS + 3 * VAR_IDS) & (lane < BIAS_END))
    return jnp.where(flip, 1.0 - marks, marks)


def in_windows(win, row, first, count, step):
    need = win[row, 2 * first + 1]
    for i in range(1, count):
        need = jnp.maximum(need, win[row, 2 * (first + i) + 1])

    def run(keys):
        for i in range(count):
            low = win[row, 2 * (first + i)]
            step(first + i, pl.multiple_of(jnp.minimum(low, SEQ - keys), 16), keys)

    def looped(keys):
        def one(i, carry):
            low = win[row, 2 * (first + i)]
            step(first + i, pl.multiple_of(jnp.minimum(low, SEQ - keys), 16), keys)
            return carry

        lax.fori_loop(0, count, one, 0)

    fewest = 2 if count == 2 else 3
    for blocks in range(fewest, 5):
        fits = need <= blocks if blocks == fewest else need == blocks
        pl.when(fits)(partial(run, blocks * QB))
    pl.when((need > 4) & (need <= 6))(partial(looped, 6 * QB))
    pl.when(need > 6)(partial(looped, SEQ))


def prepare_kernel(
    place, routes, segs, vars_, positions, small,
    lanes_out, rows_out, table_out, win_out, marks_out, cos_out, sin_out, biases_out, *, experts,
):
    tok = routes.shape[1]
    blocks = tok // CH
    above = jnp.where(row_ids((CH, CH)) < lane_ids((CH, CH)), 1.0, 0.0).astype(bf16)
    base = jnp.zeros((experts, 1), f32)
    lane = lane_ids((experts, LANES))
    table = jnp.zeros((experts, LANES), f32)
    rel = lax.bitwise_xor(row_ids((experts, CH)), place[0])
    fill = jnp.full((LANES - experts, CH), -1.0, f32)
    for b in range(blocks):
        at = slice(b * CH, (b + 1) * CH)
        named = (routes[0:1, at] == rel) | (routes[1:2, at] == rel)
        ones = jnp.where(named, 1.0, 0.0)
        rank = mm(ones.astype(bf16), above)
        odd = base - 16.0 * jnp.floor(base * (1.0 / 16.0))
        spot = jnp.where(named, rank + odd, -1.0)
        lanes_out[:, at] = spot
        rows_out[at, :] = jnp.concatenate([spot, fill], axis=0).T
        count = jnp.sum(ones, axis=1, keepdims=True)
        windows = jnp.floor((odd + count) * (1.0 / WIN)) + 1.0
        table = jnp.where(lane == b, base - odd, jnp.where(lane == WIN_LANE + b, windows, table))
        base = base + count
    steps = jnp.floor((base + (SLOT // 2 - 1)) * (1.0 / SLOT))
    rest = jnp.where(base > steps * SLOT, 1.0, 0.0)
    table = jnp.where(lane == 2 * WIN_LANE - 1, steps, table)
    table_out[...] = jnp.where(lane == 2 * WIN_LANE - 2, rest, table).astype(jnp.int32)

    identity = jnp.where(row_ids((LANES, LANES)) == lane_ids((LANES, LANES)), 1.0, 0.0).astype(bf16)
    feature = row_ids((LANES, SEQ))
    two = row_ids((8, SEQ))
    spread = jnp.where(row_ids((8, LANES)) < 2, 1.0, 0.0).astype(bf16)
    lane = lane_ids((1, LANES))
    frequency = jnp.exp(
        (lane % (HD // 2)).astype(f32) * (-2.0 * math.log(10000.0) / HD)
    )
    sign = jnp.where(lane % HD < HD // 2, -1.0, 1.0)
    win = jnp.zeros(win_out.shape, f32)
    win_row, win_lane = row_ids(win_out.shape), lane_ids(win_out.shape)
    for i in range(segs.shape[0]):
        at = slice(i * SEQ, (i + 1) * SEQ)
        seg, var = segs[i : i + 1, :], vars_[i : i + 1, :]
        marks = jnp.where(
            feature < SEG_IDS,
            jnp.where(seg == feature, 1.0, 0.0),
            jnp.where(
                feature < BIAS_END,
                jnp.where(var == feature % VAR_IDS, 1.0, 0.0),
                jnp.where(
                    (feature % HD >= SUM_LANE) & (feature % HD < SUM_LANE + 3), 1.0, 0.0
                ),
            ),
        ).astype(bf16)
        marks_out[at, :] = mm_tn(marks, identity).astype(bf16)
        place_in_time = positions[i : i + 1, :]
        low = lax.bitwise_and(place_in_time, 31)
        halves = jnp.where(
            two == 0, (place_in_time - low).astype(f32), jnp.where(two == 1, low.astype(f32), 0.0)
        ).astype(bf16)
        angles = mm_tn(halves, spread) * frequency
        cos_out[at, :] = jnp.cos(angles)
        sin_out[at, :] = jnp.sin(angles) * sign
        for q in range(NBLK):
            head_id, tail_id = seg[:, q * QB : q * QB + 1], seg[:, (q + 1) * QB - 1 : (q + 1) * QB]
            first = jnp.sum(jnp.where(seg < head_id, 1.0, 0.0), axis=1, keepdims=True)
            last = jnp.sum(jnp.where(seg <= tail_id, 1.0, 0.0), axis=1, keepdims=True)
            first = 16.0 * jnp.floor(first * (1.0 / 16.0))
            keys = jnp.floor((last - first + (QB - 1)) * (1.0 / QB))
            win = jnp.where(
                (win_row == i) & (win_lane == 2 * q),
                first,
                jnp.where((win_row == i) & (win_lane == 2 * q + 1), keys, win),
            )
    win_out[...] = win.astype(jnp.int32)

    shape = (8, LANES)
    head, lanes = row_ids(shape), lane_ids(shape)
    bias = jnp.broadcast_to(small[0:1, 2 * D : 2 * D + 2 * HEADS], (8, 2 * HEADS))
    bias_row, bias_lane = row_ids(bias.shape), lane_ids(bias.shape)
    filled = jnp.where(lanes < SEG_IDS, -FAR, 0.0)
    for kind in range(2):
        own = jnp.sum(
            jnp.where(bias_lane == kind * HEADS + bias_row, bias, 0.0), axis=1, keepdims=True
        )
        for i, piece in enumerate(three_pieces(own)):
            first = SEG_IDS + (3 * kind + i) * VAR_IDS
            filled = jnp.where((lanes >= first) & (lanes < first + VAR_IDS), piece, filled)
    biases_out[...] = jnp.where(head < HEADS, filled, 0.0)


def prepare(place, routes, segs, vars_, positions, small, experts):
    tok = routes.shape[1]
    seqs = segs.shape[0]
    shapes = [
        ((experts, tok), f32), ((tok, LANES), f32), ((experts, LANES), jnp.int32),
        ((-(-seqs // 8) * 8, LANES), jnp.int32), ((tok, LANES), bf16), ((tok, LANES), f32),
        ((tok, LANES), f32), ((8, LANES), f32),
    ]
    return call(
        partial(prepare_kernel, experts=experts),
        8,
        grid_spec=pltpu.PrefetchScalarGridSpec(
            num_scalar_prefetch=1,
            grid=(1,),
            in_specs=resident(5),
            out_specs=resident(len(shapes)),
        ),
        out_shape=[jax.ShapeDtypeStruct(shape, dtype) for shape, dtype in shapes],
        cost_estimate=cost(1e9, 8e6),
        name="prepare",
    )(place, routes, segs, vars_, positions, small)


def row_views(refs, row):
    at = pl.ds(pl.multiple_of(row * SEQ, SEQ), SEQ)
    return [ref.at[at, :] for ref in refs]


ROW_OUTS = 8


def forward_kernel(win, *refs, experts):
    arrays, fixed, refs = refs[:6], refs[6:11], refs[11:]
    rows = arrays[0].shape[0] // SEQ
    scratch = refs[rows * ROW_OUTS :]
    for row in range(rows):
        forward_row(
            row, win, *row_views(arrays, row), *fixed, *refs[row * ROW_OUTS : (row + 1) * ROW_OUTS],
            *scratch, experts=experts,
        )


def forward_row(
    row, win, tokens, cot, cos_ref, sin_ref, marks_ref, place_rows, small, biases,
    in_proj, out_proj, router,
    q_out, k_out, v_out, lse_out, mixed_out, middle_out, rows_out, probs_out,
    keys_aug, values_aug, totals, tops, sums_out, *, experts,
):
    masks = half_masks()
    bias_low = biases[...].astype(bf16)
    gain_one, gain_two = small[0:1, :D], small[0:1, D : 2 * D]
    for p in range(PAIRS):
        values_aug[p, :, LANES:] = jnp.ones((SEQ, LANES), bf16)

    def project(c, carry):
        at = pl.ds(pl.multiple_of(c * RC, RC), RC)
        x = tokens[at, :].astype(f32)
        factor = lax.rsqrt(jnp.mean(x * x, axis=-1, keepdims=True) + norm_epsilon)
        normed = (x * factor * gain_one).astype(bf16)
        projected = mm(normed, in_proj[...])
        cosine, sine = cos_ref[at, :], sin_ref[at, :]
        features = key_features(marks_ref[at, :].astype(f32)).astype(bf16)
        for j in range(2 * PAIRS):
            part = projected[:, j * LANES : (j + 1) * LANES]
            turned = part * cosine + swap_halves(part) * sine
            if j < PAIRS:
                turned = turned.astype(bf16) * jnp.asarray(HD**-0.5, bf16)
                q_out[at, j * LANES : (j + 1) * LANES] = turned
            else:
                p = j - PAIRS
                turned = turned.astype(bf16)
                k_out[at, p * LANES : (p + 1) * LANES] = turned
                keys_aug[p, at, :LANES] = turned
                keys_aug[p, at, LANES:] = features
        for p in range(PAIRS):
            part = projected[:, 2 * D + p * LANES : 2 * D + (p + 1) * LANES].astype(bf16)
            v_out[at, p * LANES : (p + 1) * LANES] = part
            values_aug[p, at, :LANES] = part
        return carry

    lax.fori_loop(0, SEQ // RC, project, 0, unroll=2)

    lane = lane_ids((QB, LANES))

    def attend(quad, carry):
        def step(block, key_start, keys):
            at = pl.ds(pl.multiple_of(block * QB, QB), QB)
            key_at = pl.ds(key_start, keys)
            marks = marks_ref[at, :]
            for p in range(PAIRS):
                cols = slice(p * LANES, (p + 1) * LANES)
                queries = q_out[at, cols]
                stacked = jnp.concatenate(
                    [
                        jnp.concatenate(
                            [queries * masks[i], marks * bias_low[2 * p + i : 2 * p + i + 1, :]], axis=1
                        )
                        for i in range(2)
                    ],
                    axis=0,
                )
                scores = mm_nt(stacked, keys_aug[p, key_at, :])
                top = jnp.max(scores, axis=1, keepdims=True)
                weights = jnp.exp(scores - top).astype(bf16)
                sums = mm(weights, values_aug[p, key_at, :])
                sums_out[at, cols] = jnp.where(lane < HD, sums[:QB, :LANES], sums[QB:, :LANES])
                totals[at, cols] = jnp.where(lane < HD, sums[:QB, LANES:], sums[QB:, LANES:])
                tops[at, cols] = jnp.where(lane < HD, top[:QB], top[QB:])

        in_windows(win, row, 4 * quad, 4, step)
        return carry

    lax.fori_loop(0, NBLK // 4, attend, 0)

    def finish(c, carry):
        at = pl.ds(pl.multiple_of(c * RC, RC), RC)
        for p in range(PAIRS):
            cols = slice(p * LANES, (p + 1) * LANES)
            total = totals[at, cols]
            mixed_out[at, cols] = (sums_out[at, cols] / total).astype(bf16)
            lse_out[at, cols] = own_summand(-(tops[at, cols] + jnp.log(total)))
        middle = tokens[at, :].astype(f32) + mm(mixed_out[at, :], out_proj[...])
        middle_out[at, :] = middle
        factor = lax.rsqrt(jnp.mean(middle * middle, axis=-1, keepdims=True) + norm_epsilon)
        normed = (middle * factor * gain_two).astype(bf16)
        rows_out[at, :D] = normed
        rows_out[at, D : 2 * D] = cot[at, :]
        logits = mm(normed, router[...])
        named = place_rows[at, :] >= 0.0
        top = jnp.max(jnp.where(named, logits, -3.0e38), axis=1, keepdims=True)
        weights = jnp.where(named, jnp.exp(jnp.where(named, logits - top, 0.0)), 0.0)
        probs = weights / jnp.sum(weights, axis=1, keepdims=True)
        probs_out[at, :] = probs
        high, mid, low = three_pieces(probs)
        rows_out[at, 2 * D :] = (
            high + pltpu.roll(mid, experts, 1) + pltpu.roll(low, 2 * experts, 1)
        ).astype(bf16)
        return carry

    lax.fori_loop(0, SEQ // RC, finish, 0, unroll=2)


def forward(win, tokens, cot, cosine, sine, marks, place_rows, small, biases, weights, experts):
    tok = tokens.shape[0]
    shapes = [
        jax.ShapeDtypeStruct((SEQ, width), dtype)
        for width, dtype in [(D, bf16)] * 5 + [(D, f32), (XW, bf16), (LANES, f32)]
    ] * (tok // SEQ)
    return call(
        partial(forward_kernel, experts=experts),
        12,
        grid_spec=pltpu.PrefetchScalarGridSpec(
            num_scalar_prefetch=1,
            grid=(1,),
            in_specs=resident(11),
            out_specs=resident(len(shapes)),
            scratch_shapes=[
                pltpu.VMEM((PAIRS, SEQ, 2 * LANES), bf16),
                pltpu.VMEM((PAIRS, SEQ, 2 * LANES), bf16),
                pltpu.VMEM((SEQ, D), f32),
                pltpu.VMEM((SEQ, D), f32),
                pltpu.VMEM((SEQ, D), f32),
            ],
        ),
        out_shape=shapes,
        cost_estimate=cost(2e10, 2e7),
        name="attention_forward",
    )(win, tokens, cot, cosine, sine, marks, place_rows, small, biases, *weights)


def experts_kernel(table, *refs, group, experts, blocks, chained):
    size = len(group)
    weights_hbm = refs[:size]
    place_lanes, place_rows = refs[size : size + 2]
    seqs = blocks * CH // SEQ
    rows, refs = refs[size + 2 : size + 2 + seqs], refs[size + 2 + seqs :]
    earlier, refs = refs[:chained], refs[chained:]
    part_out, *grads_hbm = refs[: size + 1]
    slots, weights, grads, grad_in, grad_down, total, in_sems, out_sems = refs[size + 1 :]
    ff = grad_down.shape[0]
    cuts = ff // LANES
    arrivals = [
        pltpu.make_async_copy(weights_hbm[g], weights.at[g % 2], in_sems.at[g]) for g in range(size)
    ]
    departures = [
        pltpu.make_async_copy(grads.at[g % 2], grads_hbm[g], out_sems.at[g]) for g in range(size)
    ]
    for copy in arrivals[:2]:
        copy.start()

    def first_slot(block, r):
        return pl.multiple_of(table[r, block], 16)

    for g in range(size):
        slots[g, 0:16, :] = jnp.zeros((16, XW), bf16)

    def gather(seq, inner, carry):
        block = seq * (SEQ // CH) + inner
        at = pl.ds(pl.multiple_of(block * CH, CH), CH)
        source = rows[seq][pl.ds(pl.multiple_of(inner * CH, CH), CH), :]
        slot = row_ids((WIN, CH)).astype(f32)

        def picks(r, first):
            return jnp.where(place_lanes[r : r + 1, at] - first == slot, 1.0, 0.0).astype(bf16)

        moved = mm(jnp.concatenate([picks(r, 0.0) for r in group], axis=0), source).astype(bf16)
        for g, r in enumerate(group):
            start = first_slot(block, r)
            slots[g, pl.ds(start, 16), :] += moved[g * WIN : g * WIN + 16]
            slots[g, pl.ds(start + 16, WIN - 16), :] = moved[g * WIN + 16 : (g + 1) * WIN]

            def more(w, inner, g=g, r=r, start=start):
                slots[g, pl.ds(start + w * WIN, WIN), :] = mm(
                    picks(r, (w * WIN).astype(f32)), source
                ).astype(bf16)
                return inner

            lax.fori_loop(1, table[r, WIN_LANE + block], more, 0)
        return carry

    for seq in range(seqs):
        lax.fori_loop(0, SEQ // CH, partial(gather, seq), 0, unroll=2)

    for g, r in enumerate(group):
        end = first_slot(blocks - 1, r) + table[r, WIN_LANE + blocks - 1] * WIN
        slots[g, pl.ds(end, SLOT), :] = jnp.zeros((SLOT, XW), bf16)
        arrivals[g].wait()
        gate_w = jnp.concatenate([weights[g % 2, z, :D, :] for z in range(cuts)], axis=1)
        up_w = jnp.concatenate([weights[g % 2, z, D : 2 * D, :] for z in range(cuts)], axis=1)
        down_w = jnp.concatenate(
            [
                jnp.concatenate(
                    [weights[g % 2, z, (6 + j) * LANES : (7 + j) * LANES, :] for j in range(3)], axis=1
                )
                for z in range(cuts)
            ],
            axis=0,
        )
        grad_in[...] = jnp.zeros(grad_in.shape, f32)
        grad_down[...] = jnp.zeros(grad_down.shape, f32)

        def step(i, carry, size=SLOT, g=g, r=r, gate_w=gate_w, up_w=up_w, down_w=down_w):
            at = pl.ds(pl.multiple_of(i * SLOT, SLOT), size)
            x = slots[g, at, :D]
            cot = slots[g, at, D : 2 * D].astype(f32)
            parts = slots[g, at, 2 * D :].astype(f32)
            prob = (
                parts[:, r : r + 1]
                + parts[:, experts + r : experts + r + 1]
                + parts[:, 2 * experts + r : 2 * experts + r + 1]
            )
            gate_pre = mm(x, gate_w)
            up_pre = mm(x, up_w)
            sigmoid = 1.0 / (1.0 + jnp.exp(-gate_pre))
            silu = gate_pre * sigmoid
            hidden = (silu * up_pre).astype(bf16)
            result = mm(hidden, down_w).astype(bf16).astype(f32)
            grad_result = (prob * cot).astype(bf16)
            grad_hidden = mm_nt(grad_result, down_w)
            grad_gate = (
                grad_hidden * up_pre * sigmoid * (1.0 + gate_pre * (1.0 - sigmoid))
            ).astype(bf16)
            grad_up = (grad_hidden * silu).astype(bf16)
            grad_rows = mm_nt(grad_gate, gate_w) + mm_nt(grad_up, up_w)
            grad_in[:, :ff] += mm_tn(x, grad_gate)
            grad_in[:, ff:] += mm_tn(x, grad_up)
            grad_down[...] += mm_tn(hidden, grad_result)
            score = jnp.sum(cot * result, axis=1, keepdims=True)
            high, mid, _ = three_pieces(jnp.broadcast_to(score, (size, LANES)))
            lane = lane_ids((size, LANES))
            slots[g, at, :D] = (prob * result).astype(bf16)
            slots[g, at, D : 2 * D] = grad_rows.astype(bf16)
            slots[g, at, 2 * D :] = jnp.where(
                lane == r, high, jnp.where(lane == experts + r, mid, 0.0)
            ).astype(bf16)
            return carry

        steps = table[r, 2 * WIN_LANE - 1]
        lax.fori_loop(0, steps, step, 0)
        pl.when(table[r, 2 * WIN_LANE - 2] > 0)(partial(step, steps, None, SLOT // 2))
        if g + 2 < size:
            arrivals[g + 2].start()
        if g >= 2:
            departures[g - 2].wait()
        for z in range(cuts):
            cols = slice(z * LANES, (z + 1) * LANES)
            grads[g % 2, z, :D, :] = grad_in[:, cols].astype(bf16)
            grads[g % 2, z, D : 2 * D, :] = grad_in[:, ff + z * LANES : ff + (z + 1) * LANES].astype(bf16)
            for j in range(3):
                grads[g % 2, z, (6 + j) * LANES : (7 + j) * LANES, :] = grad_down[
                    cols, j * LANES : (j + 1) * LANES
                ].astype(bf16)
        departures[g].start()

    def scatter(block, carry):
        at = pl.ds(pl.multiple_of(block * CH, CH), CH)
        places = place_rows[at, :]
        slot = lane_ids((CH, WIN)).astype(f32)

        def picks(r, first):
            return jnp.where(places[:, r : r + 1] - first == slot, 1.0, 0.0).astype(bf16)

        source = jnp.concatenate(
            [slots[g, pl.ds(first_slot(block, r), WIN), :] for g, r in enumerate(group)], axis=0
        )
        total[...] = mm(jnp.concatenate([picks(r, 0.0) for r in group], axis=1), source)
        for g, r in enumerate(group):

            def more(w, inner, g=g, r=r):
                total[...] += mm(
                    picks(r, (w * WIN).astype(f32)),
                    slots[g, pl.ds(first_slot(block, r) + w * WIN, WIN), :],
                )
                return inner

            lax.fori_loop(1, table[r, WIN_LANE + block], more, 0)
        result = total[...]
        for ref in earlier:
            result = result + ref[at, :].astype(f32)
        part_out[at, :] = result.astype(bf16)
        return carry

    lax.fori_loop(0, blocks, scatter, 0, unroll=2)
    for copy in departures[-2:]:
        copy.wait()


def run_experts(table, weights, rows, place_lanes, place_rows, earlier, group, experts, cap):
    tok = place_rows.shape[0]
    ff = weights[0].shape[0] * LANES
    blocks = tok // CH
    shape = weights[0].shape
    size = len(group)
    there = [pl.BlockSpec(memory_space=pltpu.HBM)] * size
    out = call(
        partial(
            experts_kernel, group=group, experts=experts, blocks=blocks, chained=len(earlier)
        ),
        11 + 5 * size // 2,
        grid_spec=pltpu.PrefetchScalarGridSpec(
            num_scalar_prefetch=1,
            grid=(1,),
            in_specs=there + resident(2 + len(rows) + len(earlier)),
            out_specs=resident(1) + there,
            scratch_shapes=[
                pltpu.VMEM((size, cap + WIN + SLOT, XW), bf16),
                pltpu.VMEM((2, *shape), bf16),
                pltpu.VMEM((2, *shape), bf16),
                pltpu.VMEM((D, 2 * ff), f32),
                pltpu.VMEM((ff, D), f32),
                pltpu.VMEM((CH, XW), f32),
                pltpu.SemaphoreType.DMA((size,)),
                pltpu.SemaphoreType.DMA((size,)),
            ],
        ),
        out_shape=[jax.ShapeDtypeStruct((tok, XW), bf16)] + [jax.ShapeDtypeStruct(shape, bf16)] * size,
        input_output_aliases={3 + size + len(rows): 0} if earlier else {},
        cost_estimate=cost(4e9 * size, 3e6 * size + 8e6),
        name="experts",
    )(table, *weights, place_lanes, place_rows, *rows, *earlier)
    return out[0], out[1:]


SUMS = 5


def backward_kernel(win, place, *refs, row, rows, experts, n_tp, shard):
    arrays, fixed, refs = refs[:13], refs[13:18], refs[18:]
    earlier = refs[: SUMS if row else 0]
    refs = refs[SUMS + 2 if row else 0 :]
    results, refs = refs[:2], refs[2:]
    if row < rows - 1:
        sums, (buffers, scratch) = refs[:SUMS], (refs[SUMS : SUMS + 2], refs[SUMS + 2 : -2])
    else:
        dense_out, buffers, scratch, sums = refs[0], refs[1:3], refs[3 : -SUMS - 2], refs[-SUMS - 2 : -2]
        scratch, flat = scratch[:-1], scratch[-1]
    sems = refs[-2:]
    for i, ref in enumerate(sums):
        ref[...] = earlier[i][...] if row else jnp.zeros(ref.shape, f32)
    copies = [
        pltpu.make_async_copy(buffer, result.at[pl.ds(row * SEQ, SEQ), :], sem)
        for buffer, result, sem in zip(buffers, results, sems)
    ]
    backward_row(
        row, win, place, copies[0], *row_views(arrays[:6], row), *arrays[6:], *fixed, *buffers, *scratch, *sums,
        experts=experts,
    )
    copies[1].start()
    if row == rows - 1:
        backward_flush(place, dense_out, flat, *sums, experts=experts, n_tp=n_tp, shard=shard)
    for copy in copies:
        copy.wait()


def backward_row(
    row, win, place, block_copy,
    part_ref, tokens, cot_ref, marks_ref, cos_ref, sin_ref,
    q_ref, k_ref, v_ref, lse_ref, mixed_ref, middle_ref, probs_ref, small, biases, in_proj, out_proj, router,
    block_out, grad_in_out,
    grad_middle, grad_mixed, inner_ref, keys_aug, values_aug, grad_q, grad_k, grad_v,
    grad_in_proj, grad_out_proj, grad_router, gain_out, bias_out, *, experts,
):
    masks = half_masks()
    bias_low = biases[...].astype(bf16)
    pair_sum = jnp.where(
        (row_ids((2 * LANES, LANES)) % LANES < HD) == (lane_ids((2 * LANES, LANES)) < HD), 1.0, 0.0
    ).astype(bf16)
    gain_one, gain_two = small[0:1, :D], small[0:1, D : 2 * D]
    fold_row, fold_lane = row_ids((LANES, LANES)), lane_ids((LANES, LANES))
    tile = jnp.where(
        (lax.bitwise_xor(fold_row, place[0]) == fold_lane % experts) & (fold_row < experts), 1.0, 0.0
    ).astype(bf16)

    def head(c, carry):
        at = pl.ds(pl.multiple_of(c * RC, RC), RC)
        back = part_ref[at, :].astype(f32)
        middle = middle_ref[at, :]
        block_out[at, :] = (middle + back[:, :D]).astype(bf16)
        scores = back[:, 2 * D :]
        scores = scores + pltpu.roll(scores, LANES - experts, 1)
        probs = probs_ref[at, :]
        inner = jnp.sum(probs * scores, axis=1, keepdims=True)
        grad_logits = (probs * (scores - inner)).astype(bf16)
        grad_normed = mm_nt(grad_logits, router[...]) + back[:, D : 2 * D]
        factor = lax.rsqrt(jnp.mean(middle * middle, axis=-1, keepdims=True) + norm_epsilon)
        normed = (middle * factor * gain_two).astype(bf16)
        grad_router[...] += mm_tn(normed, mm(grad_logits, tile).astype(bf16))
        weighted = grad_normed * gain_two
        gain_out[1:2, :] += jnp.sum(grad_normed * middle * factor, axis=0, keepdims=True)
        cot = cot_ref[at, :].astype(f32)
        grad = (
            cot
            + factor * weighted
            - middle
            * (factor * factor * factor)
            * jnp.mean(weighted * middle, axis=-1, keepdims=True)
        )
        grad_middle[at, :] = grad
        branch = grad.astype(bf16)
        grad_out_proj[...] += mm_tn(mixed_ref[at, :], branch)
        mixed_grad = mm_nt(branch, out_proj[...]).astype(bf16)
        grad_mixed[at, :] = mixed_grad
        features = key_features(marks_ref[at, :].astype(f32)).astype(bf16)
        for p in range(PAIRS):
            cols = slice(p * LANES, (p + 1) * LANES)
            product = mixed_grad[:, cols].astype(f32) * mixed_ref[at, cols].astype(f32)
            high, mid, _ = three_pieces(product)
            inner = mm(jnp.concatenate([high, mid], axis=1).astype(bf16), pair_sum)
            inner_ref[at, cols] = own_summand(-inner)
            keys_aug[p, at, :LANES] = k_ref[at, cols]
            keys_aug[p, at, LANES:] = features
            values_aug[p, at, :LANES] = v_ref[at, cols]
            values_aug[p, at, LANES:] = features
        return carry

    lax.fori_loop(0, SEQ // RC, head, 0, unroll=2)
    block_copy.start()
    grad_k[...] = jnp.zeros(grad_k.shape, f32)
    grad_v[...] = jnp.zeros(grad_v.shape, f32)

    lane = lane_ids((QB, LANES))

    def attend(couple, carry):
        def step(block, key_start, keys):
            at = pl.ds(pl.multiple_of(block * QB, QB), QB)
            marks = marks_ref[at, :]
            key_at = pl.ds(key_start, keys)
            for p in range(PAIRS):
                cols = slice(p * LANES, (p + 1) * LANES)
                queries, logs = q_ref[at, cols], lse_ref[at, cols]
                out_grad, inner = grad_mixed[at, cols], inner_ref[at, cols]
                stacked = jnp.concatenate(
                    [
                        jnp.concatenate(
                            [
                                queries * masks[i],
                                marks * bias_low[2 * p + i : 2 * p + i + 1, :] + logs * masks[i],
                            ],
                            axis=1,
                        )
                        for i in range(2)
                    ],
                    axis=0,
                )
                grads = jnp.concatenate(
                    [
                        jnp.concatenate([out_grad * masks[i], inner * masks[i]], axis=1)
                        for i in range(2)
                    ],
                    axis=0,
                )
                keys_here = keys_aug[p, key_at, :]
                probs = jnp.exp(mm_nt(keys_here, stacked))
                shifted = mm_nt(values_aug[p, key_at, :], grads)
                grad_scores = (probs * shifted).astype(bf16)
                grad_v[key_at, cols] += mm(probs.astype(bf16), grads[:, :LANES])
                grad_k[key_at, cols] += mm(grad_scores, stacked[:, :LANES])
                back = mm_tn(grad_scores, keys_here)
                grad_q[at, cols] = (
                    jnp.where(lane < HD, back[:QB, :LANES], back[QB:, :LANES]) * HD**-0.5
                )
                for i in range(2):
                    bias_out[2 * p + i] += jnp.sum(
                        (marks.astype(f32) * back[i * QB : (i + 1) * QB, LANES:]).reshape(QB // 8, 8, LANES),
                        axis=0,
                    )

        in_windows(win, row, 2 * couple, 2, step)
        return carry

    lax.fori_loop(0, NBLK // 2, attend, 0)

    def tail(c, carry):
        at = pl.ds(pl.multiple_of(c * RC, RC), RC)
        cosine, sine = cos_ref[at, :], sin_ref[at, :]
        pieces = []
        for ref in (grad_q, grad_k):
            for p in range(PAIRS):
                part = ref[at, p * LANES : (p + 1) * LANES]
                pieces.append((part * cosine - swap_halves(part) * sine).astype(bf16))
        pieces.append(grad_v[at, :].astype(bf16))
        grad_projected = jnp.concatenate(pieces, axis=1)
        x = tokens[at, :].astype(f32)
        factor = lax.rsqrt(jnp.mean(x * x, axis=-1, keepdims=True) + norm_epsilon)
        normed = (x * factor * gain_one).astype(bf16)
        grad_in_proj[...] += mm_tn(normed, grad_projected)
        grad_normed = mm_nt(grad_projected, in_proj[...])
        weighted = grad_normed * gain_one
        gain_out[0:1, :] += jnp.sum(grad_normed * x * factor, axis=0, keepdims=True)
        grad_in_out[at, :] = (
            grad_middle[at, :]
            + factor * weighted
            - x * (factor * factor * factor) * jnp.mean(weighted * x, axis=-1, keepdims=True)
        ).astype(bf16)
        return carry

    lax.fori_loop(0, SEQ // RC, tail, 0, unroll=2)


def backward_flush(
    place, dense_out, flat, grad_in_proj, grad_out_proj, grad_router, gain_out, bias_out,
    *, experts, n_tp, shard,
):
    for j in range(9):
        flat[pl.ds(j, D, stride=9), :] = grad_in_proj[:, j * LANES : (j + 1) * LANES]
    for j in range(3):
        flat[pl.ds(9 * D + j, D, stride=3), :] = grad_out_proj[:, j * LANES : (j + 1) * LANES]
    share = LANES // experts
    count = D // share
    lanes = lane_ids((D, LANES))
    grad_router[...] = jnp.where(
        lanes // experts == row_ids((D, LANES)) % share, grad_router[...], 0.0
    )
    merged = grad_router[pl.ds(0, count, stride=share), :]
    for i in range(1, share):
        merged = merged + grad_router[pl.ds(i, count, stride=share), :]
    flat[12 * D : 12 * D + count, :] = merged
    spare = flat.shape[0] - (12 * D + count)
    flat[12 * D + count :, :] = jnp.zeros((spare, LANES), f32)
    n_dev = dense_out.shape[0]
    rows = dense_out.shape[1]
    half = n_dev // 2
    piece_lane = lane_ids((rows, LANES))
    for s in range(n_dev):
        exp_rel = lax.bitwise_xor(s // n_tp, place[0])
        rel = (
            (exp_rel % 2) * half + (exp_rel // 2) * n_tp + lax.bitwise_xor(s % n_tp, place[1])
        )
        start, off = divmod(shard * s, LANES)
        piece = flat[start : start + rows, :]
        if off:
            piece = jnp.where(
                piece_lane < LANES - off,
                pltpu.roll(piece, LANES - off, 1),
                pltpu.roll(flat[start + 1 : start + 1 + rows, :], LANES - off, 1),
            )
        dense_out[rel] = piece.astype(bf16)
    shape = (8, LANES)
    bias_rows, bias_lanes = row_ids(shape), lane_ids(shape)
    sums = jnp.concatenate(
        [jnp.sum(bias_out[h], axis=0, keepdims=True) for h in range(HEADS)]
        + [jnp.zeros((8 - HEADS, LANES), f32)],
        axis=0,
    )
    extra = jnp.zeros((1, LANES), f32)
    for kind in range(2):
        first_lane = SEG_IDS + 3 * kind * VAR_IDS
        own = jnp.sum(
            jnp.where((bias_lanes >= first_lane) & (bias_lanes < first_lane + VAR_IDS), sums, 0.0),
            axis=1,
            keepdims=True,
        )
        extra = extra + jnp.sum(
            jnp.where((bias_lanes == bias_rows + kind * HEADS) & (bias_rows < HEADS), own, 0.0),
            axis=0,
            keepdims=True,
        )
    spare_rows = jnp.concatenate(
        [gain_out[i : i + 1, j * LANES : (j + 1) * LANES] for i in range(2) for j in range(3)]
        + [extra, jnp.zeros((1, LANES), f32)],
        axis=0,
    ).astype(bf16)
    for s in range(n_dev):
        dense_out[s, rows - 8 :, :] = spare_rows


def backward(win, place, row, earlier, arrays, small, biases, weights, sizes):
    experts, n_exp, n_tp, shard, shard_rows = sizes
    tok = arrays[0].shape[0]
    rows = tok // SEQ
    last = row == rows - 1
    sums = [(D, 3 * D), (D, D), (D, LANES), (8, D), (HEADS, 8, LANES)]
    flat_rows = shard * n_exp * n_tp // LANES + shard_rows + 8
    there = [pl.BlockSpec(memory_space=pltpu.HBM)] * 2
    results = [jax.ShapeDtypeStruct((tok, D), bf16)] * 2
    tail_scratch = [pltpu.VMEM((flat_rows, LANES), f32)] + [pltpu.VMEM(shape, f32) for shape in sums]
    return call(
        partial(backward_kernel, row=row, rows=rows, experts=experts, n_tp=n_tp, shard=shard),
        26 if last else 20,
        grid_spec=pltpu.PrefetchScalarGridSpec(
            num_scalar_prefetch=2,
            grid=(1,),
            in_specs=resident(18) + (resident(SUMS) + there if row else []),
            out_specs=there + resident(1 if last else SUMS),
            scratch_shapes=[
                pltpu.VMEM((SEQ, D), bf16),
                pltpu.VMEM((SEQ, D), bf16),
                pltpu.VMEM((SEQ, D), f32),
                pltpu.VMEM((SEQ, D), bf16),
                pltpu.VMEM((SEQ, D), bf16),
                pltpu.VMEM((PAIRS, SEQ, 2 * LANES), bf16),
                pltpu.VMEM((PAIRS, SEQ, 2 * LANES), bf16),
                pltpu.VMEM((SEQ, D), f32),
                pltpu.VMEM((SEQ, D), f32),
                pltpu.VMEM((SEQ, D), f32),
                *(tail_scratch if last else []),
                pltpu.SemaphoreType.DMA(()),
                pltpu.SemaphoreType.DMA(()),
            ],
        ),
        out_shape=results
        + (
            [jax.ShapeDtypeStruct((n_exp * n_tp, shard_rows, LANES), bf16)]
            if last
            else [jax.ShapeDtypeStruct(shape, f32) for shape in sums]
        ),
        input_output_aliases={20 + SUMS: 0, 21 + SUMS: 1} if row else {},
        cost_estimate=cost(2e10, 2e7),
        name="attention_backward",
    )(win, place, *arrays, small, biases, *weights, *earlier)


def swap(values, axis, mask):
    size = lax.axis_size(axis)
    return lax.ppermute(values, axis, [(i, i ^ mask) for i in range(size)])


def add_up(parts):
    parts = [part.astype(f32) for part in parts]
    while len(parts) > 1:
        parts = [sum(parts[i + 1 : i + 2], parts[i]) for i in range(0, len(parts), 2)]
    return parts[0]


def adamw_update(old_state, grad_value, rate, decay, step_value):
    moment_one = moment_rate * old_state[1] + (1.0 - moment_rate) * grad_value
    moment_two = moment_rate * old_state[2] + (1.0 - moment_rate) * grad_value * grad_value
    correction = 1.0 - jnp.power(moment_rate, step_value)
    master = old_state[0] - rate * (
        moment_one / correction / (jnp.sqrt(moment_two / correction) + adam_epsilon)
        + decay * old_state[0]
    )
    average = average_rate * old_state[3] + (1.0 - average_rate) * master
    return jnp.stack([master, moment_one, moment_two, average])


def local(
    tokens, cotangent, routes, segments, variates, positions, step_count,
    dense_state, gate_up_state, down_state, small_state,
):
    tok, seqs = tokens.shape[0], segments.shape[0]
    n_exp, n_tp = lax.axis_size("exp"), lax.axis_size("tp")
    experts = n_exp * gate_up_state.shape[1]
    cap = 2 * tok * TOP // experts
    my_exp, my_tp = lax.axis_index("exp"), lax.axis_index("tp")
    place = jnp.stack([my_exp, my_tp]).astype(jnp.int32)
    shard = dense_state.shape[1]
    shard_rows = -(-(-(-shard // LANES) + 8) // 16) * 16

    def in_line(values):
        return [values] + [swap(values, "tp", j) for j in range(1, n_tp)]

    def in_plane(values):
        return [values] + [swap(values, "exp", m) for m in range(2, n_exp, 2)]

    own = jnp.pad(dense_state[0].astype(bf16), (0, shard_rows * LANES - shard))
    line = jnp.concatenate(in_line(own.reshape(1, shard_rows, LANES)), axis=0)
    routes_later, _ = lax.optimization_barrier((routes.T, line))
    prepared = prepare(place, routes_later, segments, variates, positions, small_state, experts)
    here = jnp.concatenate(in_plane(line), axis=0)

    gate_up = gate_up_state[0, 0].astype(bf16)
    down = down_state[0, 0].astype(bf16)
    slice_ff = gate_up.shape[2]
    ff = slice_ff * n_tp
    cuts = ff // LANES

    def pack(gate_up, down):
        return jnp.stack(
            [
                jnp.concatenate(
                    [gate_up[0, :, at : at + LANES], gate_up[1, :, at : at + LANES]]
                    + [down[at : at + LANES, i : i + LANES] for i in range(0, D, LANES)],
                    axis=0,
                )
                for at in range(0, gate_up.shape[2], LANES)
            ]
        )

    def unpack(packed):
        count = packed.shape[0]
        gate, up = packed[:, :D], packed[:, D : 2 * D]
        return (
            jnp.stack([jnp.concatenate([m[i] for i in range(count)], axis=1) for m in (gate, up)]),
            jnp.concatenate(
                [packed[:, 2 * D + i : 2 * D + i + LANES] for i in range(0, D, LANES)], axis=2
            ).reshape(count * LANES, D),
        )

    if slice_ff % LANES == 0:
        packed = jnp.concatenate(in_line(pack(gate_up, down)), axis=0)
    else:
        packed = pack(
            jnp.concatenate(in_line(gate_up), axis=2), jnp.concatenate(in_line(down), axis=0)
        )
    here, packed, prepared = lax.optimization_barrier((here, packed, prepared))
    place_lanes, place_rows, table, win, marks, cosine, sine, biases = prepared
    there = swap(here, "exp", 1)
    weights = unpack_dense(place, here, there, shard, experts, n_tp)
    if n_exp == 8:
        expert_weights = {0: packed, 2: swap(packed, "exp", 2), 4: swap(packed, "exp", 4)}
    else:
        expert_weights = {2 * i: values for i, values in enumerate(in_plane(packed))}
    expert_weights[1] = swap(packed, "exp", 1)
    saved = forward(
        win, tokens, cotangent, cosine, sine, marks, place_rows, small_state, biases, weights, experts
    )
    saved = [saved[i : i + ROW_OUTS] for i in range(0, len(saved), ROW_OUTS)]
    routed = [outs[6] for outs in saved]
    if n_exp == 8:
        groups = [(0, 1), (6, 7), (2, 3, 4, 5)]
        one, other, _ = lax.optimization_barrier((expert_weights[2], expert_weights[4], saved[-1][7]))
        expert_weights[6] = jnp.concatenate(
            [swap(one[: cuts // 2], "exp", 4), swap(other[cuts // 2 :], "exp", 2)], axis=0
        )
    else:
        groups = [(0, 1)] + [tuple(range(i, min(i + 4, n_exp))) for i in range(2, n_exp, 4)]
    chain, halves, mine = [], {}, {}
    for group in groups:
        part, grads = run_experts(
            table, [expert_weights[r] for r in group], routed, place_lanes, place_rows, chain, group,
            experts, cap,
        )
        if not chain:
            for g in groups[1:]:
                for m in g[::2]:
                    values, _ = lax.optimization_barrier((expert_weights[m], part))
                    expert_weights[m + 1] = swap(values, "exp", 1)
        if group == groups[-1]:
            part, grads, mine[far] = lax.optimization_barrier((part, grads, mine[far]))
        for i in range(0, len(group), 2):
            halves[group[i]] = add_up([grads[i], swap(grads[i + 1], "exp", 1)]).astype(bf16)
        if chain and group != groups[-1] and not mine:
            far = group[0]
            mine = {far: swap(halves[far], "exp", far)}
            part, _ = lax.optimization_barrier((part, halves[far]))
        chain = [part]
    mine[0] = halves[0]
    for m in range(2, n_exp, 2):
        if m not in mine:
            mine[m] = swap(halves[m], "exp", m)

    arrays = (part, tokens, cotangent, marks, cosine, sine)
    sizes = (experts, n_exp, n_tp, shard, shard_rows)
    earlier = []
    for row in range(seqs):
        if row == seqs - 1:
            mine = add_up([mine[m] for m in range(0, n_exp, 2)]).astype(bf16)
            earlier, mine = lax.optimization_barrier((earlier, mine))
        block_out, grad_in, *rest = backward(
            win, place, row, earlier, (*arrays, *saved[row][:6], saved[row][7]), small_state, biases, weights, sizes
        )
        earlier = [*rest, block_out, grad_in]
    dense_grad = rest[0]

    if slice_ff % LANES == 0:
        mine = mine.reshape(n_tp, slice_ff // LANES, 3 * D, LANES)
        arrived = [[mine[0]] + [swap(mine[j], "tp", j) for j in range(1, n_tp)]]
    else:
        mine_in, mine_down = unpack(mine)
        mine_in = mine_in.reshape(2, D, n_tp, slice_ff)
        mine_down = mine_down.reshape(n_tp, slice_ff, D)
        arrived = [
            [mine_in[:, :, 0]] + [swap(mine_in[:, :, j], "tp", j) for j in range(1, n_tp)],
            [mine_down[0]] + [swap(mine_down[j], "tp", j) for j in range(1, n_tp)],
        ]

    dense_grad, arrived = lax.optimization_barrier((dense_grad, arrived))

    dense_grad = dense_grad.reshape(2, n_exp // 2, n_tp, shard_rows, LANES)
    dense_half = add_up([dense_grad[0], swap(dense_grad[1], "exp", 1)]).astype(bf16)
    dense_line = add_up(
        [dense_half[0]] + [swap(dense_half[m // 2], "exp", m) for m in range(2, n_exp, 2)]
    ).astype(bf16)
    dense_parts = [dense_line[0]] + [swap(dense_line[j], "tp", j) for j in range(1, n_tp)]
    dense_mine = add_up(dense_parts)
    small_grad = dense_mine[shard_rows - 8 :].reshape(-1)[: small_state.shape[1]]
    dense_mine = dense_mine[: shard_rows - 8].reshape(-1)[:shard]
    if slice_ff % LANES == 0:
        grad_gate_up, grad_down = unpack(add_up(arrived[0]))
    else:
        grad_gate_up, grad_down = add_up(arrived[0]), add_up(arrived[1])
    grad_gate_up, grad_down = grad_gate_up[None], grad_down[None]

    step_value = step_count[0].astype(f32)
    dense_old, _ = lax.optimization_barrier((dense_state, dense_grad))
    dense_new = adamw_update(dense_old, dense_mine, rate_dense, weight_decay, step_value)
    gate_up_new = adamw_update(gate_up_state, grad_gate_up, rate_expert, weight_decay, step_value)
    down_new = adamw_update(down_state, grad_down, rate_expert, weight_decay, step_value)
    small_new = adamw_update(small_state, small_grad, rate_small, 0.0, step_value)
    return (
        block_out,
        grad_in,
        dense_new,
        dense_new[0].astype(bf16),
        gate_up_new,
        gate_up_new[0].astype(bf16),
        down_new,
        down_new[0].astype(bf16),
        small_new,
    )


def solution(mesh):
    in_specs = (
        P(("exp", "tp"), None),
        P(("exp", "tp"), None),
        P(("exp", "tp"), None),
        P(("exp", "tp"), None),
        P(("exp", "tp"), None),
        P(("exp", "tp"), None),
        P(),
        P(None, ("exp", "tp")),
        P(None, "exp", None, None, "tp"),
        P(None, "exp", "tp", None),
        P(),
    )
    out_specs = (
        P(("exp", "tp"), None),
        P(("exp", "tp"), None),
        P(None, ("exp", "tp")),
        P(("exp", "tp")),
        P(None, "exp", None, None, "tp"),
        P("exp", None, None, "tp"),
        P(None, "exp", "tp", None),
        P("exp", "tp", None),
        P(),
    )
    return jax.shard_map(local, mesh=mesh, in_specs=in_specs, out_specs=out_specs, check_vma=False)
```

```python
from functools import partial
import math

import jax
import jax.numpy as jnp
from jax import lax
from jax.experimental import pallas as pl
from jax.experimental.pallas import tpu as pltpu
from jax.sharding import PartitionSpec as P

D = 384
HEADS = 6
HD = 64
PAIRS = HEADS // 2
TOP = 2
SEQ = 1024
LANES = 128
QB = 128
CH = 256
RC = 512
NBLK = SEQ // QB
WIN = 128
SLOT = 256
XW = 2 * D + LANES
SEG_IDS = 8
VAR_IDS = 4
BIAS_END = SEG_IDS + 6 * VAR_IDS
SUM_LANE = 36
WIN_LANE = 64
FAR = 2.0**100

norm_epsilon = 1e-06
moment_rate = 0.5
average_rate = 0.9
adam_epsilon = 1e-08
weight_decay = 0.1
rate_dense = 0.05
rate_expert = 0.04
rate_small = 0.2

bf16 = jnp.bfloat16
f32 = jnp.float32


def mm(left, right):
    return lax.dot_general(left, right, (((1,), (0,)), ((), ())), preferred_element_type=f32)


def mm_nt(left, right):
    return lax.dot_general(left, right, (((1,), (1,)), ((), ())), preferred_element_type=f32)


def mm_tn(left, right):
    return lax.dot_general(left, right, (((0,), (0,)), ((), ())), preferred_element_type=f32)


def lane_ids(shape):
    return lax.broadcasted_iota(jnp.int32, shape, len(shape) - 1)


def row_ids(shape):
    return lax.broadcasted_iota(jnp.int32, shape, 0)


def three_pieces(value):
    high = value.astype(bf16)
    rest = value - high.astype(f32)
    middle = rest.astype(bf16)
    low = (rest - middle.astype(f32)).astype(bf16)
    return high.astype(f32), middle.astype(f32), low.astype(f32)


def own_summand(value):
    high, middle, low = three_pieces(value)
    lane = lane_ids(value.shape) % HD
    return jnp.where(
        lane == SUM_LANE,
        high,
        jnp.where(lane == SUM_LANE + 1, middle, jnp.where(lane == SUM_LANE + 2, low, 0.0)),
    ).astype(bf16)


def half_masks():
    lane = lane_ids((1, LANES))
    return [jnp.where(mask, 1.0, 0.0).astype(bf16) for mask in (lane < HD, lane >= HD)]


def swap_halves(values):
    lane = lane_ids(values.shape)
    return jnp.where(
        lane % HD < HD // 2,
        pltpu.roll(values, LANES - HD // 2, 1),
        pltpu.roll(values, HD // 2, 1),
    )


def call(kernel, mib, **kwargs):
    return pl.pallas_call(
        kernel,
        compiler_params=pltpu.CompilerParams(
            vmem_limit_bytes=mib * 1024 * 1024, dimension_semantics=("arbitrary",)
        ),
        **kwargs,
    )


def whole(shape):
    return pl.BlockSpec(shape, lambda *_: (0,) * len(shape))


def resident(count):
    return [pl.BlockSpec(memory_space=pltpu.VMEM)] * count


def cost(flops, moved):
    return pl.CostEstimate(flops=int(flops), transcendentals=0, bytes_accessed=int(moved))


def unpack_kernel(place, here, there, in_out, out_out, router_out, flat, spread, *, shard, experts, n_tp):
    rows = here.shape[1]
    n_dev = 2 * here.shape[0]
    flat[...] = jnp.zeros(flat.shape, f32)
    lane = lane_ids((rows, LANES))
    odd = place[0] % 2 == 1
    for s in range(n_dev):
        exp = s // n_tp
        rel = lax.bitwise_xor(exp // 2, place[0] // 2) * n_tp + lax.bitwise_xor(s % n_tp, place[1])
        start, off = divmod(shard * s, LANES)
        one, other = here[rel].astype(f32), there[rel].astype(f32)
        piece = jnp.where(odd, other, one) if exp % 2 == 0 else jnp.where(odd, one, other)
        if off:
            piece = pltpu.roll(piece, off, 1)
            flat[start : start + rows] += jnp.where(lane >= off, piece, 0.0)
            flat[start + 1 : start + 1 + rows] += jnp.where(lane < off, piece, 0.0)
        else:
            flat[start : start + rows] += piece
    for j in range(9):
        in_out[:, j * LANES : (j + 1) * LANES] = flat[pl.ds(j, D, stride=9), :].astype(bf16)
    for j in range(3):
        out_out[:, j * LANES : (j + 1) * LANES] = flat[pl.ds(9 * D + j, D, stride=3), :].astype(bf16)
    share = LANES // experts
    count = D // share
    for i in range(share):
        spread[pl.ds(i, count, stride=share), :] = flat[12 * D : 12 * D + count, :]
    lanes = lane_ids((D, LANES))
    kept = jnp.where(lanes // experts == row_ids((D, LANES)) % share, spread[...], 0.0).astype(bf16)
    fold_lane = lane_ids((LANES, LANES))
    fold = (row_ids((LANES, LANES)) % experts == lax.bitwise_xor(fold_lane, place[0])) & (
        fold_lane < experts
    )
    router_out[...] = mm(kept, jnp.where(fold, 1.0, 0.0).astype(bf16)).astype(bf16)


def unpack_dense(place, here, there, shard, experts, n_tp):
    total = shard * 2 * here.shape[0] // LANES
    flat_rows = total + here.shape[1] + 8
    return call(
        partial(unpack_kernel, shard=shard, experts=experts, n_tp=n_tp),
        6,
        grid_spec=pltpu.PrefetchScalarGridSpec(
            num_scalar_prefetch=1,
            grid=(1,),
            in_specs=resident(2),
            out_specs=resident(3),
            scratch_shapes=[pltpu.VMEM((flat_rows, LANES), f32), pltpu.VMEM((D, LANES), f32)],
        ),
        out_shape=[
            jax.ShapeDtypeStruct((D, 3 * D), bf16),
            jax.ShapeDtypeStruct((D, D), bf16),
            jax.ShapeDtypeStruct((D, LANES), bf16),
        ],
        cost_estimate=cost(1e8, 4e6),
        name="unpack_dense",
    )(place, here, there)


def key_features(marks):
    lane = lane_ids(marks.shape)
    flip = (lane < SEG_IDS) | ((lane >= SEG_IDS + 3 * VAR_IDS) & (lane < BIAS_END))
    return jnp.where(flip, 1.0 - marks, marks)


def in_windows(win, row, first, count, step):
    need = win[row, 2 * first + 1]
    for i in range(1, count):
        need = jnp.maximum(need, win[row, 2 * (first + i) + 1])

    def run(keys):
        for i in range(count):
            low = win[row, 2 * (first + i)]
            step(first + i, pl.multiple_of(jnp.minimum(low, SEQ - keys), 16), keys)

    def looped(keys):
        def one(i, carry):
            low = win[row, 2 * (first + i)]
            step(first + i, pl.multiple_of(jnp.minimum(low, SEQ - keys), 16), keys)
            return carry

        lax.fori_loop(0, count, one, 0)

    fewest = 2 if count == 2 else 3
    for blocks in range(fewest, 5):
        fits = need <= blocks if blocks == fewest else need == blocks
        pl.when(fits)(partial(run, blocks * QB))
    pl.when((need > 4) & (need <= 6))(partial(looped, 6 * QB))
    pl.when(need > 6)(partial(looped, SEQ))


def prepare_kernel(
    place, routes, segs, vars_, positions, small,
    lanes_out, rows_out, table_out, win_out, marks_out, cos_out, sin_out, biases_out, *, experts,
):
    tok = routes.shape[1]
    blocks = tok // CH
    above = jnp.where(row_ids((CH, CH)) < lane_ids((CH, CH)), 1.0, 0.0).astype(bf16)
    base = jnp.zeros((experts, 1), f32)
    lane = lane_ids((experts, LANES))
    table = jnp.zeros((experts, LANES), f32)
    rel = lax.bitwise_xor(row_ids((experts, CH)), place[0])
    fill = jnp.full((LANES - experts, CH), -1.0, f32)
    for b in range(blocks):
        at = slice(b * CH, (b + 1) * CH)
        named = (routes[0:1, at] == rel) | (routes[1:2, at] == rel)
        ones = jnp.where(named, 1.0, 0.0)
        rank = mm(ones.astype(bf16), above)
        odd = base - 16.0 * jnp.floor(base * (1.0 / 16.0))
        spot = jnp.where(named, rank + odd, -1.0)
        lanes_out[:, at] = spot
        rows_out[at, :] = jnp.concatenate([spot, fill], axis=0).T
        count = jnp.sum(ones, axis=1, keepdims=True)
        windows = jnp.floor((odd + count) * (1.0 / WIN)) + 1.0
        table = jnp.where(lane == b, base - odd, jnp.where(lane == WIN_LANE + b, windows, table))
        base = base + count
    steps = jnp.floor((base + (SLOT // 2 - 1)) * (1.0 / SLOT))
    rest = jnp.where(base > steps * SLOT, 1.0, 0.0)
    table = jnp.where(lane == 2 * WIN_LANE - 1, steps, table)
    table_out[...] = jnp.where(lane == 2 * WIN_LANE - 2, rest, table).astype(jnp.int32)

    identity = jnp.where(row_ids((LANES, LANES)) == lane_ids((LANES, LANES)), 1.0, 0.0).astype(bf16)
    feature = row_ids((LANES, SEQ))
    two = row_ids((8, SEQ))
    spread = jnp.where(row_ids((8, LANES)) < 2, 1.0, 0.0).astype(bf16)
    lane = lane_ids((1, LANES))
    frequency = jnp.exp(
        (lane % (HD // 2)).astype(f32) * (-2.0 * math.log(10000.0) / HD)
    )
    sign = jnp.where(lane % HD < HD // 2, -1.0, 1.0)
    win = jnp.zeros(win_out.shape, f32)
    win_row, win_lane = row_ids(win_out.shape), lane_ids(win_out.shape)
    for i in range(segs.shape[0]):
        at = slice(i * SEQ, (i + 1) * SEQ)
        seg, var = segs[i : i + 1, :], vars_[i : i + 1, :]
        marks = jnp.where(
            feature < SEG_IDS,
            jnp.where(seg == feature, 1.0, 0.0),
            jnp.where(
                feature < BIAS_END,
                jnp.where(var == feature % VAR_IDS, 1.0, 0.0),
                jnp.where(
                    (feature % HD >= SUM_LANE) & (feature % HD < SUM_LANE + 3), 1.0, 0.0
                ),
            ),
        ).astype(bf16)
        marks_out[at, :] = mm_tn(marks, identity).astype(bf16)
        place_in_time = positions[i : i + 1, :]
        low = lax.bitwise_and(place_in_time, 31)
        halves = jnp.where(
            two == 0, (place_in_time - low).astype(f32), jnp.where(two == 1, low.astype(f32), 0.0)
        ).astype(bf16)
        angles = mm_tn(halves, spread) * frequency
        cos_out[at, :] = jnp.cos(angles)
        sin_out[at, :] = jnp.sin(angles) * sign
        for q in range(NBLK):
            head_id, tail_id = seg[:, q * QB : q * QB + 1], seg[:, (q + 1) * QB - 1 : (q + 1) * QB]
            first = jnp.sum(jnp.where(seg < head_id, 1.0, 0.0), axis=1, keepdims=True)
            last = jnp.sum(jnp.where(seg <= tail_id, 1.0, 0.0), axis=1, keepdims=True)
            first = 16.0 * jnp.floor(first * (1.0 / 16.0))
            keys = jnp.floor((last - first + (QB - 1)) * (1.0 / QB))
            win = jnp.where(
                (win_row == i) & (win_lane == 2 * q),
                first,
                jnp.where((win_row == i) & (win_lane == 2 * q + 1), keys, win),
            )
    win_out[...] = win.astype(jnp.int32)

    shape = (8, LANES)
    head, lanes = row_ids(shape), lane_ids(shape)
    bias = jnp.broadcast_to(small[0:1, 2 * D : 2 * D + 2 * HEADS], (8, 2 * HEADS))
    bias_row, bias_lane = row_ids(bias.shape), lane_ids(bias.shape)
    filled = jnp.where(lanes < SEG_IDS, -FAR, 0.0)
    for kind in range(2):
        own = jnp.sum(
            jnp.where(bias_lane == kind * HEADS + bias_row, bias, 0.0), axis=1, keepdims=True
        )
        for i, piece in enumerate(three_pieces(own)):
            first = SEG_IDS + (3 * kind + i) * VAR_IDS
            filled = jnp.where((lanes >= first) & (lanes < first + VAR_IDS), piece, filled)
    biases_out[...] = jnp.where(head < HEADS, filled, 0.0)


def prepare(place, routes, segs, vars_, positions, small, experts):
    tok = routes.shape[1]
    seqs = segs.shape[0]
    shapes = [
        ((experts, tok), f32), ((tok, LANES), f32), ((experts, LANES), jnp.int32),
        ((-(-seqs // 8) * 8, LANES), jnp.int32), ((tok, LANES), bf16), ((tok, LANES), f32),
        ((tok, LANES), f32), ((8, LANES), f32),
    ]
    return call(
        partial(prepare_kernel, experts=experts),
        8,
        grid_spec=pltpu.PrefetchScalarGridSpec(
            num_scalar_prefetch=1,
            grid=(1,),
            in_specs=resident(5),
            out_specs=resident(len(shapes)),
        ),
        out_shape=[jax.ShapeDtypeStruct(shape, dtype) for shape, dtype in shapes],
        cost_estimate=cost(1e9, 8e6),
        name="prepare",
    )(place, routes, segs, vars_, positions, small)


def row_views(refs, row):
    at = pl.ds(pl.multiple_of(row * SEQ, SEQ), SEQ)
    return [ref.at[at, :] for ref in refs]


ROW_OUTS = 8


def forward_kernel(win, *refs, experts):
    arrays, fixed, refs = refs[:6], refs[6:11], refs[11:]
    rows = arrays[0].shape[0] // SEQ
    scratch = refs[rows * ROW_OUTS :]
    for row in range(rows):
        forward_row(
            row, win, *row_views(arrays, row), *fixed, *refs[row * ROW_OUTS : (row + 1) * ROW_OUTS],
            *scratch, experts=experts,
        )


def forward_row(
    row, win, tokens, cot, cos_ref, sin_ref, marks_ref, place_rows, small, biases,
    in_proj, out_proj, router,
    q_out, k_out, v_out, lse_out, mixed_out, middle_out, rows_out, probs_out,
    keys_aug, values_aug, totals, tops, sums_out, *, experts,
):
    masks = half_masks()
    bias_low = biases[...].astype(bf16)
    gain_one, gain_two = small[0:1, :D], small[0:1, D : 2 * D]
    for p in range(PAIRS):
        values_aug[p, :, LANES:] = jnp.ones((SEQ, LANES), bf16)

    def project(c, carry):
        at = pl.ds(pl.multiple_of(c * RC, RC), RC)
        x = tokens[at, :].astype(f32)
        factor = lax.rsqrt(jnp.mean(x * x, axis=-1, keepdims=True) + norm_epsilon)
        normed = (x * factor * gain_one).astype(bf16)
        projected = mm(normed, in_proj[...])
        cosine, sine = cos_ref[at, :], sin_ref[at, :]
        features = key_features(marks_ref[at, :].astype(f32)).astype(bf16)
        for j in range(2 * PAIRS):
            part = projected[:, j * LANES : (j + 1) * LANES]
            turned = part * cosine + swap_halves(part) * sine
            if j < PAIRS:
                turned = turned.astype(bf16) * jnp.asarray(HD**-0.5, bf16)
                q_out[at, j * LANES : (j + 1) * LANES] = turned
            else:
                p = j - PAIRS
                turned = turned.astype(bf16)
                k_out[at, p * LANES : (p + 1) * LANES] = turned
                keys_aug[p, at, :LANES] = turned
                keys_aug[p, at, LANES:] = features
        for p in range(PAIRS):
            part = projected[:, 2 * D + p * LANES : 2 * D + (p + 1) * LANES].astype(bf16)
            v_out[at, p * LANES : (p + 1) * LANES] = part
            values_aug[p, at, :LANES] = part
        return carry

    lax.fori_loop(0, SEQ // RC, project, 0, unroll=2)

    lane = lane_ids((QB, LANES))

    def attend(quad, carry):
        def step(block, key_start, keys):
            at = pl.ds(pl.multiple_of(block * QB, QB), QB)
            key_at = pl.ds(key_start, keys)
            marks = marks_ref[at, :]
            for p in range(PAIRS):
                cols = slice(p * LANES, (p + 1) * LANES)
                queries = q_out[at, cols]
                stacked = jnp.concatenate(
                    [
                        jnp.concatenate(
                            [queries * masks[i], marks * bias_low[2 * p + i : 2 * p + i + 1, :]], axis=1
                        )
                        for i in range(2)
                    ],
                    axis=0,
                )
                scores = mm_nt(stacked, keys_aug[p, key_at, :])
                top = jnp.max(scores, axis=1, keepdims=True)
                weights = jnp.exp(scores - top).astype(bf16)
                sums = mm(weights, values_aug[p, key_at, :])
                sums_out[at, cols] = jnp.where(lane < HD, sums[:QB, :LANES], sums[QB:, :LANES])
                totals[at, cols] = jnp.where(lane < HD, sums[:QB, LANES:], sums[QB:, LANES:])
                tops[at, cols] = jnp.where(lane < HD, top[:QB], top[QB:])

        in_windows(win, row, 4 * quad, 4, step)
        return carry

    lax.fori_loop(0, NBLK // 4, attend, 0)

    def finish(c, carry):
        at = pl.ds(pl.multiple_of(c * RC, RC), RC)
        for p in range(PAIRS):
            cols = slice(p * LANES, (p + 1) * LANES)
            total = totals[at, cols]
            mixed_out[at, cols] = (sums_out[at, cols] / total).astype(bf16)
            lse_out[at, cols] = own_summand(-(tops[at, cols] + jnp.log(total)))
        middle = tokens[at, :].astype(f32) + mm(mixed_out[at, :], out_proj[...])
        middle_out[at, :] = middle
        factor = lax.rsqrt(jnp.mean(middle * middle, axis=-1, keepdims=True) + norm_epsilon)
        normed = (middle * factor * gain_two).astype(bf16)
        rows_out[at, :D] = normed
        rows_out[at, D : 2 * D] = cot[at, :]
        logits = mm(normed, router[...])
        named = place_rows[at, :] >= 0.0
        top = jnp.max(jnp.where(named, logits, -3.0e38), axis=1, keepdims=True)
        weights = jnp.where(named, jnp.exp(jnp.where(named, logits - top, 0.0)), 0.0)
        probs = weights / jnp.sum(weights, axis=1, keepdims=True)
        probs_out[at, :] = probs
        high, mid, low = three_pieces(probs)
        rows_out[at, 2 * D :] = (
            high + pltpu.roll(mid, experts, 1) + pltpu.roll(low, 2 * experts, 1)
        ).astype(bf16)
        return carry

    lax.fori_loop(0, SEQ // RC, finish, 0, unroll=2)


def forward(win, tokens, cot, cosine, sine, marks, place_rows, small, biases, weights, experts):
    tok = tokens.shape[0]
    shapes = [
        jax.ShapeDtypeStruct((SEQ, width), dtype)
        for width, dtype in [(D, bf16)] * 5 + [(D, f32), (XW, bf16), (LANES, f32)]
    ] * (tok // SEQ)
    return call(
        partial(forward_kernel, experts=experts),
        12,
        grid_spec=pltpu.PrefetchScalarGridSpec(
            num_scalar_prefetch=1,
            grid=(1,),
            in_specs=resident(11),
            out_specs=resident(len(shapes)),
            scratch_shapes=[
                pltpu.VMEM((PAIRS, SEQ, 2 * LANES), bf16),
                pltpu.VMEM((PAIRS, SEQ, 2 * LANES), bf16),
                pltpu.VMEM((SEQ, D), f32),
                pltpu.VMEM((SEQ, D), f32),
                pltpu.VMEM((SEQ, D), f32),
            ],
        ),
        out_shape=shapes,
        cost_estimate=cost(2e10, 2e7),
        name="attention_forward",
    )(win, tokens, cot, cosine, sine, marks, place_rows, small, biases, *weights)


def experts_kernel(table, *refs, group, experts, blocks, chained):
    size = len(group)
    weights_hbm = refs[:size]
    place_lanes, place_rows = refs[size : size + 2]
    seqs = blocks * CH // SEQ
    rows, refs = refs[size + 2 : size + 2 + seqs], refs[size + 2 + seqs :]
    earlier, refs = refs[:chained], refs[chained:]
    part_out, *grads_hbm = refs[: size + 1]
    slots, weights, grads, grad_in, grad_down, total, in_sems, out_sems = refs[size + 1 :]
    ff = grad_down.shape[0]
    cuts = ff // LANES
    arrivals = [
        pltpu.make_async_copy(weights_hbm[g], weights.at[g % 2], in_sems.at[g]) for g in range(size)
    ]
    departures = [
        pltpu.make_async_copy(grads.at[g % 2], grads_hbm[g], out_sems.at[g]) for g in range(size)
    ]
    for copy in arrivals[:2]:
        copy.start()

    def first_slot(block, r):
        return pl.multiple_of(table[r, block], 16)

    for g in range(size):
        slots[g, 0:16, :] = jnp.zeros((16, XW), bf16)

    def gather(seq, inner, carry):
        block = seq * (SEQ // CH) + inner
        at = pl.ds(pl.multiple_of(block * CH, CH), CH)
        source = rows[seq][pl.ds(pl.multiple_of(inner * CH, CH), CH), :]
        slot = row_ids((WIN, CH)).astype(f32)

        def picks(r, first):
            return jnp.where(place_lanes[r : r + 1, at] - first == slot, 1.0, 0.0).astype(bf16)

        moved = mm(jnp.concatenate([picks(r, 0.0) for r in group], axis=0), source).astype(bf16)
        for g, r in enumerate(group):
            start = first_slot(block, r)
            slots[g, pl.ds(start, 16), :] += moved[g * WIN : g * WIN + 16]
            slots[g, pl.ds(start + 16, WIN - 16), :] = moved[g * WIN + 16 : (g + 1) * WIN]

            def more(w, inner, g=g, r=r, start=start):
                slots[g, pl.ds(start + w * WIN, WIN), :] = mm(
                    picks(r, (w * WIN).astype(f32)), source
                ).astype(bf16)
                return inner

            lax.fori_loop(1, table[r, WIN_LANE + block], more, 0)
        return carry

    for seq in range(seqs):
        lax.fori_loop(0, SEQ // CH, partial(gather, seq), 0, unroll=2)

    for g, r in enumerate(group):
        end = first_slot(blocks - 1, r) + table[r, WIN_LANE + blocks - 1] * WIN
        slots[g, pl.ds(end, SLOT), :] = jnp.zeros((SLOT, XW), bf16)
        arrivals[g].wait()
        gate_w = jnp.concatenate([weights[g % 2, z, :D, :] for z in range(cuts)], axis=1)
        up_w = jnp.concatenate([weights[g % 2, z, D : 2 * D, :] for z in range(cuts)], axis=1)
        down_w = jnp.concatenate(
            [
                jnp.concatenate(
                    [weights[g % 2, z, (6 + j) * LANES : (7 + j) * LANES, :] for j in range(3)], axis=1
                )
                for z in range(cuts)
            ],
            axis=0,
        )
        grad_in[...] = jnp.zeros(grad_in.shape, f32)
        grad_down[...] = jnp.zeros(grad_down.shape, f32)

        def step(i, carry, size=SLOT, g=g, r=r, gate_w=gate_w, up_w=up_w, down_w=down_w):
            at = pl.ds(pl.multiple_of(i * SLOT, SLOT), size)
            x = slots[g, at, :D]
            cot = slots[g, at, D : 2 * D].astype(f32)
            parts = slots[g, at, 2 * D :].astype(f32)
            prob = (
                parts[:, r : r + 1]
                + parts[:, experts + r : experts + r + 1]
                + parts[:, 2 * experts + r : 2 * experts + r + 1]
            )
            gate_pre = mm(x, gate_w)
            up_pre = mm(x, up_w)
            sigmoid = 1.0 / (1.0 + jnp.exp(-gate_pre))
            silu = gate_pre * sigmoid
            hidden = (silu * up_pre).astype(bf16)
            result = mm(hidden, down_w).astype(bf16).astype(f32)
            grad_result = (prob * cot).astype(bf16)
            grad_hidden = mm_nt(grad_result, down_w)
            grad_gate = (
                grad_hidden * up_pre * sigmoid * (1.0 + gate_pre * (1.0 - sigmoid))
            ).astype(bf16)
            grad_up = (grad_hidden * silu).astype(bf16)
            grad_rows = mm_nt(grad_gate, gate_w) + mm_nt(grad_up, up_w)
            grad_in[:, :ff] += mm_tn(x, grad_gate)
            grad_in[:, ff:] += mm_tn(x, grad_up)
            grad_down[...] += mm_tn(hidden, grad_result)
            score = jnp.sum(cot * result, axis=1, keepdims=True)
            high, mid, _ = three_pieces(jnp.broadcast_to(score, (size, LANES)))
            lane = lane_ids((size, LANES))
            slots[g, at, :D] = (prob * result).astype(bf16)
            slots[g, at, D : 2 * D] = grad_rows.astype(bf16)
            slots[g, at, 2 * D :] = jnp.where(
                lane == r, high, jnp.where(lane == experts + r, mid, 0.0)
            ).astype(bf16)
            return carry

        steps = table[r, 2 * WIN_LANE - 1]
        lax.fori_loop(0, steps, step, 0)
        pl.when(table[r, 2 * WIN_LANE - 2] > 0)(partial(step, steps, None, SLOT // 2))
        if g + 2 < size:
            arrivals[g + 2].start()
        if g >= 2:
            departures[g - 2].wait()
        for z in range(cuts):
            cols = slice(z * LANES, (z + 1) * LANES)
            grads[g % 2, z, :D, :] = grad_in[:, cols].astype(bf16)
            grads[g % 2, z, D : 2 * D, :] = grad_in[:, ff + z * LANES : ff + (z + 1) * LANES].astype(bf16)
            for j in range(3):
                grads[g % 2, z, (6 + j) * LANES : (7 + j) * LANES, :] = grad_down[
                    cols, j * LANES : (j + 1) * LANES
                ].astype(bf16)
        departures[g].start()

    def scatter(block, carry):
        at = pl.ds(pl.multiple_of(block * CH, CH), CH)
        places = place_rows[at, :]
        slot = lane_ids((CH, WIN)).astype(f32)

        def picks(r, first):
            return jnp.where(places[:, r : r + 1] - first == slot, 1.0, 0.0).astype(bf16)

        source = jnp.concatenate(
            [slots[g, pl.ds(first_slot(block, r), WIN), :] for g, r in enumerate(group)], axis=0
        )
        total[...] = mm(jnp.concatenate([picks(r, 0.0) for r in group], axis=1), source)
        for g, r in enumerate(group):

            def more(w, inner, g=g, r=r):
                total[...] += mm(
                    picks(r, (w * WIN).astype(f32)),
                    slots[g, pl.ds(first_slot(block, r) + w * WIN, WIN), :],
                )
                return inner

            lax.fori_loop(1, table[r, WIN_LANE + block], more, 0)
        result = total[...]
        for ref in earlier:
            result = result + ref[at, :].astype(f32)
        part_out[at, :] = result.astype(bf16)
        return carry

    lax.fori_loop(0, blocks, scatter, 0, unroll=2)
    for copy in departures[-2:]:
        copy.wait()


def run_experts(table, weights, rows, place_lanes, place_rows, earlier, group, experts, cap):
    tok = place_rows.shape[0]
    ff = weights[0].shape[0] * LANES
    blocks = tok // CH
    shape = weights[0].shape
    size = len(group)
    there = [pl.BlockSpec(memory_space=pltpu.HBM)] * size
    out = call(
        partial(
            experts_kernel, group=group, experts=experts, blocks=blocks, chained=len(earlier)
        ),
        11 + 5 * size // 2,
        grid_spec=pltpu.PrefetchScalarGridSpec(
            num_scalar_prefetch=1,
            grid=(1,),
            in_specs=there + resident(2 + len(rows) + len(earlier)),
            out_specs=resident(1) + there,
            scratch_shapes=[
                pltpu.VMEM((size, cap + WIN + SLOT, XW), bf16),
                pltpu.VMEM((2, *shape), bf16),
                pltpu.VMEM((2, *shape), bf16),
                pltpu.VMEM((D, 2 * ff), f32),
                pltpu.VMEM((ff, D), f32),
                pltpu.VMEM((CH, XW), f32),
                pltpu.SemaphoreType.DMA((size,)),
                pltpu.SemaphoreType.DMA((size,)),
            ],
        ),
        out_shape=[jax.ShapeDtypeStruct((tok, XW), bf16)] + [jax.ShapeDtypeStruct(shape, bf16)] * size,
        input_output_aliases={3 + size + len(rows): 0} if earlier else {},
        cost_estimate=cost(4e9 * size, 3e6 * size + 8e6),
        name="experts",
    )(table, *weights, place_lanes, place_rows, *rows, *earlier)
    return out[0], out[1:]


SUMS = 5


def backward_kernel(win, place, *refs, row, rows, experts, n_tp, shard):
    arrays, fixed, refs = refs[:13], refs[13:18], refs[18:]
    earlier = refs[: SUMS if row else 0]
    refs = refs[SUMS + 2 if row else 0 :]
    results, refs = refs[:2], refs[2:]
    if row < rows - 1:
        sums, (buffers, scratch) = refs[:SUMS], (refs[SUMS : SUMS + 2], refs[SUMS + 2 : -2])
    else:
        dense_out, buffers, scratch, sums = refs[0], refs[1:3], refs[3 : -SUMS - 2], refs[-SUMS - 2 : -2]
        scratch, flat = scratch[:-1], scratch[-1]
    sems = refs[-2:]
    for i, ref in enumerate(sums):
        ref[...] = earlier[i][...] if row else jnp.zeros(ref.shape, f32)
    copies = [
        pltpu.make_async_copy(buffer, result.at[pl.ds(row * SEQ, SEQ), :], sem)
        for buffer, result, sem in zip(buffers, results, sems)
    ]
    backward_row(
        row, win, place, copies[0], *row_views(arrays[:6], row), *arrays[6:], *fixed, *buffers, *scratch, *sums,
        experts=experts,
    )
    copies[1].start()
    if row == rows - 1:
        backward_flush(place, dense_out, flat, *sums, experts=experts, n_tp=n_tp, shard=shard)
    for copy in copies:
        copy.wait()


def backward_row(
    row, win, place, block_copy,
    part_ref, tokens, cot_ref, marks_ref, cos_ref, sin_ref,
    q_ref, k_ref, v_ref, lse_ref, mixed_ref, middle_ref, probs_ref, small, biases, in_proj, out_proj, router,
    block_out, grad_in_out,
    grad_middle, grad_mixed, inner_ref, keys_aug, values_aug, grad_q, grad_k, grad_v,
    grad_in_proj, grad_out_proj, grad_router, gain_out, bias_out, *, experts,
):
    masks = half_masks()
    bias_low = biases[...].astype(bf16)
    pair_sum = jnp.where(
        (row_ids((2 * LANES, LANES)) % LANES < HD) == (lane_ids((2 * LANES, LANES)) < HD), 1.0, 0.0
    ).astype(bf16)
    gain_one, gain_two = small[0:1, :D], small[0:1, D : 2 * D]
    fold_row, fold_lane = row_ids((LANES, LANES)), lane_ids((LANES, LANES))
    tile = jnp.where(
        (lax.bitwise_xor(fold_row, place[0]) == fold_lane % experts) & (fold_row < experts), 1.0, 0.0
    ).astype(bf16)

    def head(c, carry):
        at = pl.ds(pl.multiple_of(c * RC, RC), RC)
        back = part_ref[at, :].astype(f32)
        middle = middle_ref[at, :]
        block_out[at, :] = (middle + back[:, :D]).astype(bf16)
        scores = back[:, 2 * D :]
        scores = scores + pltpu.roll(scores, LANES - experts, 1)
        probs = probs_ref[at, :]
        inner = jnp.sum(probs * scores, axis=1, keepdims=True)
        grad_logits = (probs * (scores - inner)).astype(bf16)
        grad_normed = mm_nt(grad_logits, router[...]) + back[:, D : 2 * D]
        factor = lax.rsqrt(jnp.mean(middle * middle, axis=-1, keepdims=True) + norm_epsilon)
        normed = (middle * factor * gain_two).astype(bf16)
        grad_router[...] += mm_tn(normed, mm(grad_logits, tile).astype(bf16))
        weighted = grad_normed * gain_two
        gain_out[1:2, :] += jnp.sum(grad_normed * middle * factor, axis=0, keepdims=True)
        cot = cot_ref[at, :].astype(f32)
        grad = (
            cot
            + factor * weighted
            - middle
            * (factor * factor * factor)
            * jnp.mean(weighted * middle, axis=-1, keepdims=True)
        )
        grad_middle[at, :] = grad
        branch = grad.astype(bf16)
        grad_out_proj[...] += mm_tn(mixed_ref[at, :], branch)
        mixed_grad = mm_nt(branch, out_proj[...]).astype(bf16)
        grad_mixed[at, :] = mixed_grad
        features = key_features(marks_ref[at, :].astype(f32)).astype(bf16)
        for p in range(PAIRS):
            cols = slice(p * LANES, (p + 1) * LANES)
            product = mixed_grad[:, cols].astype(f32) * mixed_ref[at, cols].astype(f32)
            high, mid, _ = three_pieces(product)
            inner = mm(jnp.concatenate([high, mid], axis=1).astype(bf16), pair_sum)
            inner_ref[at, cols] = own_summand(-inner)
            keys_aug[p, at, :LANES] = k_ref[at, cols]
            keys_aug[p, at, LANES:] = features
            values_aug[p, at, :LANES] = v_ref[at, cols]
            values_aug[p, at, LANES:] = features
        return carry

    lax.fori_loop(0, SEQ // RC, head, 0, unroll=2)
    block_copy.start()
    grad_k[...] = jnp.zeros(grad_k.shape, f32)
    grad_v[...] = jnp.zeros(grad_v.shape, f32)

    lane = lane_ids((QB, LANES))

    def attend(couple, carry):
        def step(block, key_start, keys):
            at = pl.ds(pl.multiple_of(block * QB, QB), QB)
            marks = marks_ref[at, :]
            key_at = pl.ds(key_start, keys)
            for p in range(PAIRS):
                cols = slice(p * LANES, (p + 1) * LANES)
                queries, logs = q_ref[at, cols], lse_ref[at, cols]
                out_grad, inner = grad_mixed[at, cols], inner_ref[at, cols]
                stacked = jnp.concatenate(
                    [
                        jnp.concatenate(
                            [
                                queries * masks[i],
                                marks * bias_low[2 * p + i : 2 * p + i + 1, :] + logs * masks[i],
                            ],
                            axis=1,
                        )
                        for i in range(2)
                    ],
                    axis=0,
                )
                grads = jnp.concatenate(
                    [
                        jnp.concatenate([out_grad * masks[i], inner * masks[i]], axis=1)
                        for i in range(2)
                    ],
                    axis=0,
                )
                keys_here = keys_aug[p, key_at, :]
                probs = jnp.exp(mm_nt(keys_here, stacked))
                shifted = mm_nt(values_aug[p, key_at, :], grads)
                grad_scores = (probs * shifted).astype(bf16)
                grad_v[key_at, cols] += mm(probs.astype(bf16), grads[:, :LANES])
                grad_k[key_at, cols] += mm(grad_scores, stacked[:, :LANES])
                back = mm_tn(grad_scores, keys_here)
                grad_q[at, cols] = (
                    jnp.where(lane < HD, back[:QB, :LANES], back[QB:, :LANES]) * HD**-0.5
                )
                for i in range(2):
                    bias_out[2 * p + i] += jnp.sum(
                        (marks.astype(f32) * back[i * QB : (i + 1) * QB, LANES:]).reshape(QB // 8, 8, LANES),
                        axis=0,
                    )

        in_windows(win, row, 2 * couple, 2, step)
        return carry

    lax.fori_loop(0, NBLK // 2, attend, 0)

    def tail(c, carry):
        at = pl.ds(pl.multiple_of(c * RC, RC), RC)
        cosine, sine = cos_ref[at, :], sin_ref[at, :]
        pieces = []
        for ref in (grad_q, grad_k):
            for p in range(PAIRS):
                part = ref[at, p * LANES : (p + 1) * LANES]
                pieces.append((part * cosine - swap_halves(part) * sine).astype(bf16))
        pieces.append(grad_v[at, :].astype(bf16))
        grad_projected = jnp.concatenate(pieces, axis=1)
        x = tokens[at, :].astype(f32)
        factor = lax.rsqrt(jnp.mean(x * x, axis=-1, keepdims=True) + norm_epsilon)
        normed = (x * factor * gain_one).astype(bf16)
        grad_in_proj[...] += mm_tn(normed, grad_projected)
        grad_normed = mm_nt(grad_projected, in_proj[...])
        weighted = grad_normed * gain_one
        gain_out[0:1, :] += jnp.sum(grad_normed * x * factor, axis=0, keepdims=True)
        grad_in_out[at, :] = (
            grad_middle[at, :]
            + factor * weighted
            - x * (factor * factor * factor) * jnp.mean(weighted * x, axis=-1, keepdims=True)
        ).astype(bf16)
        return carry

    lax.fori_loop(0, SEQ // RC, tail, 0, unroll=2)


def backward_flush(
    place, dense_out, flat, grad_in_proj, grad_out_proj, grad_router, gain_out, bias_out,
    *, experts, n_tp, shard,
):
    for j in range(9):
        flat[pl.ds(j, D, stride=9), :] = grad_in_proj[:, j * LANES : (j + 1) * LANES]
    for j in range(3):
        flat[pl.ds(9 * D + j, D, stride=3), :] = grad_out_proj[:, j * LANES : (j + 1) * LANES]
    share = LANES // experts
    count = D // share
    lanes = lane_ids((D, LANES))
    grad_router[...] = jnp.where(
        lanes // experts == row_ids((D, LANES)) % share, grad_router[...], 0.0
    )
    merged = grad_router[pl.ds(0, count, stride=share), :]
    for i in range(1, share):
        merged = merged + grad_router[pl.ds(i, count, stride=share), :]
    flat[12 * D : 12 * D + count, :] = merged
    spare = flat.shape[0] - (12 * D + count)
    flat[12 * D + count :, :] = jnp.zeros((spare, LANES), f32)
    n_dev = dense_out.shape[0]
    rows = dense_out.shape[1]
    half = n_dev // 2
    piece_lane = lane_ids((rows, LANES))
    for s in range(n_dev):
        exp_rel = lax.bitwise_xor(s // n_tp, place[0])
        rel = (
            (exp_rel % 2) * half + (exp_rel // 2) * n_tp + lax.bitwise_xor(s % n_tp, place[1])
        )
        start, off = divmod(shard * s, LANES)
        piece = flat[start : start + rows, :]
        if off:
            piece = jnp.where(
                piece_lane < LANES - off,
                pltpu.roll(piece, LANES - off, 1),
                pltpu.roll(flat[start + 1 : start + 1 + rows, :], LANES - off, 1),
            )
        dense_out[rel] = piece.astype(bf16)
    shape = (8, LANES)
    bias_rows, bias_lanes = row_ids(shape), lane_ids(shape)
    sums = jnp.concatenate(
        [jnp.sum(bias_out[h], axis=0, keepdims=True) for h in range(HEADS)]
        + [jnp.zeros((8 - HEADS, LANES), f32)],
        axis=0,
    )
    extra = jnp.zeros((1, LANES), f32)
    for kind in range(2):
        first_lane = SEG_IDS + 3 * kind * VAR_IDS
        own = jnp.sum(
            jnp.where((bias_lanes >= first_lane) & (bias_lanes < first_lane + VAR_IDS), sums, 0.0),
            axis=1,
            keepdims=True,
        )
        extra = extra + jnp.sum(
            jnp.where((bias_lanes == bias_rows + kind * HEADS) & (bias_rows < HEADS), own, 0.0),
            axis=0,
            keepdims=True,
        )
    spare_rows = jnp.concatenate(
        [gain_out[i : i + 1, j * LANES : (j + 1) * LANES] for i in range(2) for j in range(3)]
        + [extra, jnp.zeros((1, LANES), f32)],
        axis=0,
    ).astype(bf16)
    for s in range(n_dev):
        dense_out[s, rows - 8 :, :] = spare_rows


def backward(win, place, row, earlier, arrays, small, biases, weights, sizes):
    experts, n_exp, n_tp, shard, shard_rows = sizes
    tok = arrays[0].shape[0]
    rows = tok // SEQ
    last = row == rows - 1
    sums = [(D, 3 * D), (D, D), (D, LANES), (8, D), (HEADS, 8, LANES)]
    flat_rows = shard * n_exp * n_tp // LANES + shard_rows + 8
    there = [pl.BlockSpec(memory_space=pltpu.HBM)] * 2
    results = [jax.ShapeDtypeStruct((tok, D), bf16)] * 2
    tail_scratch = [pltpu.VMEM((flat_rows, LANES), f32)] + [pltpu.VMEM(shape, f32) for shape in sums]
    return call(
        partial(backward_kernel, row=row, rows=rows, experts=experts, n_tp=n_tp, shard=shard),
        26 if last else 20,
        grid_spec=pltpu.PrefetchScalarGridSpec(
            num_scalar_prefetch=2,
            grid=(1,),
            in_specs=resident(18) + (resident(SUMS) + there if row else []),
            out_specs=there + resident(1 if last else SUMS),
            scratch_shapes=[
                pltpu.VMEM((SEQ, D), bf16),
                pltpu.VMEM((SEQ, D), bf16),
                pltpu.VMEM((SEQ, D), f32),
                pltpu.VMEM((SEQ, D), bf16),
                pltpu.VMEM((SEQ, D), bf16),
                pltpu.VMEM((PAIRS, SEQ, 2 * LANES), bf16),
                pltpu.VMEM((PAIRS, SEQ, 2 * LANES), bf16),
                pltpu.VMEM((SEQ, D), f32),
                pltpu.VMEM((SEQ, D), f32),
                pltpu.VMEM((SEQ, D), f32),
                *(tail_scratch if last else []),
                pltpu.SemaphoreType.DMA(()),
                pltpu.SemaphoreType.DMA(()),
            ],
        ),
        out_shape=results
        + (
            [jax.ShapeDtypeStruct((n_exp * n_tp, shard_rows, LANES), bf16)]
            if last
            else [jax.ShapeDtypeStruct(shape, f32) for shape in sums]
        ),
        input_output_aliases={20 + SUMS: 0, 21 + SUMS: 1} if row else {},
        cost_estimate=cost(2e10, 2e7),
        name="attention_backward",
    )(win, place, *arrays, small, biases, *weights, *earlier)


def swap(values, axis, mask):
    size = lax.axis_size(axis)
    return lax.ppermute(values, axis, [(i, i ^ mask) for i in range(size)])


def add_up(parts):
    parts = [part.astype(f32) for part in parts]
    while len(parts) > 1:
        parts = [sum(parts[i + 1 : i + 2], parts[i]) for i in range(0, len(parts), 2)]
    return parts[0]


def adamw_update(old_state, grad_value, rate, decay, step_value):
    moment_one = moment_rate * old_state[1] + (1.0 - moment_rate) * grad_value
    moment_two = moment_rate * old_state[2] + (1.0 - moment_rate) * grad_value * grad_value
    correction = 1.0 - jnp.power(moment_rate, step_value)
    master = old_state[0] - rate * (
        moment_one / correction / (jnp.sqrt(moment_two / correction) + adam_epsilon)
        + decay * old_state[0]
    )
    average = average_rate * old_state[3] + (1.0 - average_rate) * master
    return jnp.stack([master, moment_one, moment_two, average])


def local(
    tokens, cotangent, routes, segments, variates, positions, step_count,
    dense_state, gate_up_state, down_state, small_state,
):
    tok, seqs = tokens.shape[0], segments.shape[0]
    n_exp, n_tp = lax.axis_size("exp"), lax.axis_size("tp")
    experts = n_exp * gate_up_state.shape[1]
    cap = 2 * tok * TOP // experts
    my_exp, my_tp = lax.axis_index("exp"), lax.axis_index("tp")
    place = jnp.stack([my_exp, my_tp]).astype(jnp.int32)
    shard = dense_state.shape[1]
    shard_rows = -(-(-(-shard // LANES) + 8) // 16) * 16

    def in_line(values):
        return [values] + [swap(values, "tp", j) for j in range(1, n_tp)]

    def in_plane(values):
        return [values] + [swap(values, "exp", m) for m in range(2, n_exp, 2)]

    own = jnp.pad(dense_state[0].astype(bf16), (0, shard_rows * LANES - shard))
    line = jnp.concatenate(in_line(own.reshape(1, shard_rows, LANES)), axis=0)
    routes_later, _ = lax.optimization_barrier((routes.T, line))
    prepared = prepare(place, routes_later, segments, variates, positions, small_state, experts)
    here = jnp.concatenate(in_plane(line), axis=0)

    gate_up = gate_up_state[0, 0].astype(bf16)
    down = down_state[0, 0].astype(bf16)
    slice_ff = gate_up.shape[2]
    ff = slice_ff * n_tp
    cuts = ff // LANES

    def pack(gate_up, down):
        return jnp.stack(
            [
                jnp.concatenate(
                    [gate_up[0, :, at : at + LANES], gate_up[1, :, at : at + LANES]]
                    + [down[at : at + LANES, i : i + LANES] for i in range(0, D, LANES)],
                    axis=0,
                )
                for at in range(0, gate_up.shape[2], LANES)
            ]
        )

    def unpack(packed):
        count = packed.shape[0]
        gate, up = packed[:, :D], packed[:, D : 2 * D]
        return (
            jnp.stack([jnp.concatenate([m[i] for i in range(count)], axis=1) for m in (gate, up)]),
            jnp.concatenate(
                [packed[:, 2 * D + i : 2 * D + i + LANES] for i in range(0, D, LANES)], axis=2
            ).reshape(count * LANES, D),
        )

    if slice_ff % LANES == 0:
        packed = jnp.concatenate(in_line(pack(gate_up, down)), axis=0)
    else:
        packed = pack(
            jnp.concatenate(in_line(gate_up), axis=2), jnp.concatenate(in_line(down), axis=0)
        )
    here, packed, prepared = lax.optimization_barrier((here, packed, prepared))
    place_lanes, place_rows, table, win, marks, cosine, sine, biases = prepared
    there = swap(here, "exp", 1)
    weights = unpack_dense(place, here, there, shard, experts, n_tp)
    if n_exp == 8:
        expert_weights = {0: packed, 2: swap(packed, "exp", 2), 4: swap(packed, "exp", 4)}
    else:
        expert_weights = {2 * i: values for i, values in enumerate(in_plane(packed))}
    expert_weights[1] = swap(packed, "exp", 1)
    saved = forward(
        win, tokens, cotangent, cosine, sine, marks, place_rows, small_state, biases, weights, experts
    )
    saved = [saved[i : i + ROW_OUTS] for i in range(0, len(saved), ROW_OUTS)]
    routed = [outs[6] for outs in saved]
    if n_exp == 8:
        groups = [(0, 1), (6, 7), (2, 3, 4, 5)]
        one, other, _ = lax.optimization_barrier((expert_weights[2], expert_weights[4], saved[-1][7]))
        expert_weights[6] = jnp.concatenate(
            [swap(one[: cuts // 2], "exp", 4), swap(other[cuts // 2 :], "exp", 2)], axis=0
        )
    else:
        groups = [(0, 1)] + [tuple(range(i, min(i + 4, n_exp))) for i in range(2, n_exp, 4)]
    chain, halves, mine = [], {}, {}
    for group in groups:
        part, grads = run_experts(
            table, [expert_weights[r] for r in group], routed, place_lanes, place_rows, chain, group,
            experts, cap,
        )
        if not chain:
            near = (2, 4) if n_exp == 8 else ()
            for m in range(2, n_exp, 2):
                values, _ = lax.optimization_barrier(
                    (expert_weights[m], saved[-1][7] if m in near else part)
                )
                expert_weights[m + 1] = swap(values, "exp", 1)
            part, ready = lax.optimization_barrier((part, [expert_weights[m + 1] for m in near]))
            expert_weights.update((m + 1, values) for m, values in zip(near, ready))
        if group == groups[-1]:
            part, grads, mine[far] = lax.optimization_barrier((part, grads, mine[far]))
        for i in range(0, len(group), 2):
            halves[group[i]] = add_up([grads[i], swap(grads[i + 1], "exp", 1)]).astype(bf16)
        if chain and group != groups[-1] and not mine:
            far = group[0]
            mine = {far: swap(halves[far], "exp", far)}
            part, _ = lax.optimization_barrier((part, halves[far]))
        chain = [part]
    mine[0] = halves[0]
    for m in range(2, n_exp, 2):
        if m not in mine:
            mine[m] = swap(halves[m], "exp", m)

    arrays = (part, tokens, cotangent, marks, cosine, sine)
    sizes = (experts, n_exp, n_tp, shard, shard_rows)
    earlier = []
    for row in range(seqs):
        if row == seqs - 1:
            mine = add_up([mine[m] for m in range(0, n_exp, 2)]).astype(bf16)
            earlier, mine = lax.optimization_barrier((earlier, mine))
        block_out, grad_in, *rest = backward(
            win, place, row, earlier, (*arrays, *saved[row][:6], saved[row][7]), small_state, biases, weights, sizes
        )
        earlier = [*rest, block_out, grad_in]
    dense_grad = rest[0]

    if slice_ff % LANES == 0:
        mine = mine.reshape(n_tp, slice_ff // LANES, 3 * D, LANES)
        arrived = [[mine[0]] + [swap(mine[j], "tp", j) for j in range(1, n_tp)]]
    else:
        mine_in, mine_down = unpack(mine)
        mine_in = mine_in.reshape(2, D, n_tp, slice_ff)
        mine_down = mine_down.reshape(n_tp, slice_ff, D)
        arrived = [
            [mine_in[:, :, 0]] + [swap(mine_in[:, :, j], "tp", j) for j in range(1, n_tp)],
            [mine_down[0]] + [swap(mine_down[j], "tp", j) for j in range(1, n_tp)],
        ]

    dense_grad, arrived = lax.optimization_barrier((dense_grad, arrived))

    dense_grad = dense_grad.reshape(2, n_exp // 2, n_tp, shard_rows, LANES)
    dense_half = add_up([dense_grad[0], swap(dense_grad[1], "exp", 1)]).astype(bf16)
    dense_line = add_up(
        [dense_half[0]] + [swap(dense_half[m // 2], "exp", m) for m in range(2, n_exp, 2)]
    ).astype(bf16)
    dense_parts = [dense_line[0]] + [swap(dense_line[j], "tp", j) for j in range(1, n_tp)]
    dense_mine = add_up(dense_parts)
    small_grad = dense_mine[shard_rows - 8 :].reshape(-1)[: small_state.shape[1]]
    dense_mine = dense_mine[: shard_rows - 8].reshape(-1)[:shard]
    if slice_ff % LANES == 0:
        grad_gate_up, grad_down = unpack(add_up(arrived[0]))
    else:
        grad_gate_up, grad_down = add_up(arrived[0]), add_up(arrived[1])
    grad_gate_up, grad_down = grad_gate_up[None], grad_down[None]

    step_value = step_count[0].astype(f32)
    dense_old, _ = lax.optimization_barrier((dense_state, dense_grad))
    dense_new = adamw_update(dense_old, dense_mine, rate_dense, weight_decay, step_value)
    gate_up_new = adamw_update(gate_up_state, grad_gate_up, rate_expert, weight_decay, step_value)
    down_new = adamw_update(down_state, grad_down, rate_expert, weight_decay, step_value)
    small_new = adamw_update(small_state, small_grad, rate_small, 0.0, step_value)
    return (
        block_out,
        grad_in,
        dense_new,
        dense_new[0].astype(bf16),
        gate_up_new,
        gate_up_new[0].astype(bf16),
        down_new,
        down_new[0].astype(bf16),
        small_new,
    )


def solution(mesh):
    in_specs = (
        P(("exp", "tp"), None),
        P(("exp", "tp"), None),
        P(("exp", "tp"), None),
        P(("exp", "tp"), None),
        P(("exp", "tp"), None),
        P(("exp", "tp"), None),
        P(),
        P(None, ("exp", "tp")),
        P(None, "exp", None, None, "tp"),
        P(None, "exp", "tp", None),
        P(),
    )
    out_specs = (
        P(("exp", "tp"), None),
        P(("exp", "tp"), None),
        P(None, ("exp", "tp")),
        P(("exp", "tp")),
        P(None, "exp", None, None, "tp"),
        P("exp", None, None, "tp"),
        P(None, "exp", "tp", None),
        P("exp", "tp", None),
        P(),
    )
    return jax.shard_map(local, mesh=mesh, in_specs=in_specs, out_specs=out_specs, check_vma=False)
```
